32 devices in a mesh: dap: 32 (over z, y, x, core).
Axes of the slice: x: 2, y: 2, z: 4, core: 2. Of those that a mesh axis runs over, the one named last changes fastest.
Arguments:
- homolog_stack: float32 [64, 64, 256], P('dap'), may hold values from -5 to 5
- couple_tensor: float32 [64, 64, 128], P('dap'), may hold values from -6 to 6
- homolog_presence: int32 [64, 64], P('dap'), may hold values from 0 to 1
- amino_presence: int32 [64], replicated, may hold values 0 or 1
- horizontal_standard_factor: float32 [256], replicated, may hold values from 0.5 to 1.5
- horizontal_asking_matrix: bfloat16 [256, 256], replicated, may hold values from -7 to 7
- horizontal_lookup_triple: bfloat16 [256, 768], replicated, may hold values from -0.375 to 0.375
- horizontal_final_matrix: bfloat16 [256, 256], replicated, may hold values from -0.375 to 0.375
- couple_offset_factor: float32 [128], replicated, may hold values from 0.5 to 1.5
- couple_offset_matrix: bfloat16 [128, 8], replicated, may hold values from -2 to 2
- vertical_standard_factor: float32 [256], replicated, may hold values from 0.5 to 1.5
- vertical_asking_matrix: bfloat16 [256, 256], replicated, may hold values from -7 to 7
- vertical_lookup_triple: bfloat16 [256, 768], replicated, may hold values from -0.375 to 0.375
- vertical_final_matrix: bfloat16 [256, 256], replicated, may hold values from -0.375 to 0.375
- tensor_average_factor: float32 [256], replicated, may hold values from 0.5 to 1.5
- tensor_average_mapping: bfloat16 [256, 64], replicated, may hold values from -0.375 to 0.375
- tensor_average_final: bfloat16 [1024, 128], replicated, may hold values from -0.375 to 0.375
- trio_entry_factors: float32 [2, 128], replicated, may hold values from 0.5 to 1.5
- trio_flank_mappings: bfloat16 [2, 128, 512], replicated, may hold values from -0.5 to 0.5
- trio_final_switches: bfloat16 [2, 128, 128], replicated, may hold values from -0.5 to 0.5
- trio_multiplied_factors: float32 [2, 128], replicated, may hold values from 0.5 to 1.5
- trio_final_matrices: bfloat16 [2, 128, 128], replicated, may hold values from -1 to 1
Outputs:
- msa_out: float32 [64, 64, 256], P(None, 'dap')
- pair_out: float32 [64, 64, 128], P('dap')
The draws below stay inside these ranges and needn't reach their ends.
All inputs are finite; a program needn't handle non-finite values.
Results may differ from the reference program's by a relative error of at most 0.015.
Values may be sent and summed in bfloat16 or wider, within the bound.
No kernel may reach another device: no remote copies, remote signals or barrier semaphores. Data moves between devices by JAX's collectives and lax.ppermute only.
A program may use at most 64 MiB of HBM per device.

```python
import math
import jax
import jax.numpy as jnp
from jax import lax

ALIGNED_FEATURES = 256
CZ = 128
FOCUS_NUMBER = 8
PER_FOCUS_WIDTH = 32
TENSOR_HIDDEN = 32
TRI_HID = 128
CHAIN_WINDOW = 64
ALIGNED_STRANDS = 64


def draw_homolog_presence(key, part):
    leading_lookup, second_key, third_key = jax.random.split(jax.random.fold_in(key, 11), 3)
    column_rate = jax.random.randint(third_key, (1, CHAIN_WINDOW), 15, 101)
    existing_flag = jax.random.randint(leading_lookup, (ALIGNED_STRANDS, CHAIN_WINDOW), 0, 100) < column_rate
    column_alive = jax.random.randint(second_key, (1, CHAIN_WINDOW), 0, 100) < 97
    return jnp.logical_and(existing_flag, column_alive).astype(jnp.int32)


def draw_homolog_stack(key, part):
    profile_key, noise_key = jax.random.split(jax.random.fold_in(key, 53))
    profile = jnp.clip(jax.random.normal(profile_key, (1, CHAIN_WINDOW, ALIGNED_FEATURES), jnp.float32), -3.0, 3.0)
    noise = 0.6 * jnp.clip(jax.random.normal(noise_key, (ALIGNED_STRANDS, CHAIN_WINDOW, ALIGNED_FEATURES), jnp.float32), -3.0, 3.0)
    return profile + noise


def query_weights(key):
    content_vectors = jnp.clip(jax.random.normal(key, (ALIGNED_FEATURES, FOCUS_NUMBER * PER_FOCUS_WIDTH), jnp.float32) * (2.0 / math.sqrt(ALIGNED_FEATURES)), -7.0, 7.0)
    return content_vectors


def draw_horizontal_asking_matrix(key, part):
    return query_weights(jax.random.fold_in(key, 21)).astype(jnp.bfloat16)


def draw_vertical_asking_matrix(key, part):
    return query_weights(jax.random.fold_in(key, 37)).astype(jnp.bfloat16)


def touch_ends(drawn, key, smallest, largest):
    longest = drawn.shape.index(max(drawn.shape))
    spots = []
    for shift in (0, 1):
        where = [jax.random.randint(jax.random.fold_in(key, axis), (), 0, length) for axis, length in enumerate(drawn.shape)]
        where[longest] = (where[longest] + shift) % drawn.shape[longest]
        spots.append(tuple(where))
    return drawn.at[spots[0]].set(smallest).at[spots[1]].set(largest)


def level_of(own_key, shape, cuts, smallest, largest):
    level, own = 1.0, jax.random.fold_in(own_key, 6)
    for axis_at, shards_of in cuts:
        draws = jnp.exp(jax.random.uniform(jax.random.fold_in(own, axis_at), (shards_of,), jnp.float32, smallest / len(cuts), largest / len(cuts)))
        level = level * jnp.repeat(draws, shape[axis_at] // shards_of).reshape([-1 if axis == axis_at else 1 for axis in range(len(shape))])
    return level


def bell_draw(rng, shape, deviation, limit, pieces=(), dtype=jnp.bfloat16):
    factor_of = level_of(rng, shape, pieces, -0.22, 0.18) if pieces else 1.0
    values = jax.random.normal(rng, shape, jnp.float32) * deviation * factor_of
    return jnp.minimum(jnp.maximum(values, -limit), limit).astype(dtype)


def setup_inputs(seed: int = 0) -> dict:
    streams_of = jax.random.split(jax.random.key(seed), 23)
    return {
        "homolog_stack": draw_homolog_stack(jax.random.fold_in(streams_of[22], 71), 0),
        "couple_tensor": bell_draw(streams_of[1], (CHAIN_WINDOW, CHAIN_WINDOW, CZ), 1.0, 6.0, ((0, 32),), jnp.float32),
        "homolog_presence": draw_homolog_presence(jax.random.fold_in(streams_of[22], 71), 0),
        "amino_presence": touch_ends((jax.random.randint(streams_of[3], (CHAIN_WINDOW,), 0, 10) < 9).astype(jnp.int32), jax.random.fold_in(streams_of[3], 1), 0, 1),
        "horizontal_standard_factor": jnp.clip(jax.random.uniform(streams_of[4], (ALIGNED_FEATURES,), jnp.float32, 0.5, 1.5), 0.5, 1.5),
        "horizontal_asking_matrix": draw_horizontal_asking_matrix(jax.random.fold_in(streams_of[22], 71), 0),
        "horizontal_lookup_triple": bell_draw(streams_of[6], (ALIGNED_FEATURES, 3 * FOCUS_NUMBER * PER_FOCUS_WIDTH), ALIGNED_FEATURES ** -0.5, 0.375),
        "horizontal_final_matrix": bell_draw(streams_of[7], (FOCUS_NUMBER * PER_FOCUS_WIDTH, ALIGNED_FEATURES), (FOCUS_NUMBER * PER_FOCUS_WIDTH) ** -0.5, 0.375),
        "couple_offset_factor": jnp.clip(jax.random.uniform(streams_of[8], (CZ,), jnp.float32, 0.5, 1.5), 0.5, 1.5),
        "couple_offset_matrix": bell_draw(streams_of[9], (CZ, FOCUS_NUMBER), (CZ // 16) ** -0.5, 2.0),
        "vertical_standard_factor": jnp.clip(jax.random.uniform(streams_of[10], (ALIGNED_FEATURES,), jnp.float32, 0.5, 1.5), 0.5, 1.5),
        "vertical_asking_matrix": draw_vertical_asking_matrix(jax.random.fold_in(streams_of[22], 71), 0),
        "vertical_lookup_triple": bell_draw(streams_of[12], (ALIGNED_FEATURES, 3 * FOCUS_NUMBER * PER_FOCUS_WIDTH), ALIGNED_FEATURES ** -0.5, 0.375),
        "vertical_final_matrix": bell_draw(streams_of[13], (FOCUS_NUMBER * PER_FOCUS_WIDTH, ALIGNED_FEATURES), (FOCUS_NUMBER * PER_FOCUS_WIDTH) ** -0.5, 0.375),
        "tensor_average_factor": jnp.clip(jax.random.uniform(streams_of[14], (ALIGNED_FEATURES,), jnp.float32, 0.5, 1.5), 0.5, 1.5),
        "tensor_average_mapping": bell_draw(streams_of[15], (ALIGNED_FEATURES, 2 * TENSOR_HIDDEN), ALIGNED_FEATURES ** -0.5, 0.375),
        "tensor_average_final": bell_draw(streams_of[16], (TENSOR_HIDDEN * TENSOR_HIDDEN, CZ), (TENSOR_HIDDEN * TENSOR_HIDDEN // 4) ** -0.5, 0.375),
        "trio_entry_factors": jnp.clip(jax.random.uniform(streams_of[17], (2, CZ), jnp.float32, 0.5, 1.5), 0.5, 1.5),
        "trio_flank_mappings": bell_draw(streams_of[18], (2, CZ, 4 * TRI_HID), CZ ** -0.5, 0.5),
        "trio_final_switches": bell_draw(streams_of[19], (2, CZ, CZ), CZ ** -0.5, 0.5),
        "trio_multiplied_factors": jnp.clip(jax.random.uniform(streams_of[20], (2, TRI_HID), jnp.float32, 0.5, 1.5), 0.5, 1.5),
        "trio_final_matrices": bell_draw(streams_of[21], (2, TRI_HID, CZ), (TRI_HID // 4) ** -0.5, 1.0),
    }


EPSILON = 1e-05
MASK_PENALTY_SCALE = 1000000000.0

def standardize_features(content_vectors, gain, axis):
    centred = content_vectors - lax.optimization_barrier(jnp.mean(content_vectors, axis=axis, keepdims=True))
    spread = lax.optimization_barrier(jnp.mean(centred * centred, axis=axis, keepdims=True))
    return centred * lax.rsqrt(spread + EPSILON) * gain

def triangle(pair_now, gain_in, proj_weight, gate_weight, gain_mid, final_weight, res_float, incoming):
    hidden = TRI_HID
    standardized_source = standardize_features(pair_now, gain_in.astype(jnp.float32), -1).astype(jnp.bfloat16)
    projected = jnp.dot(standardized_source, proj_weight, preferred_element_type=jnp.float32)
    pair_mask = (res_float[:, None] * res_float[None, :])[..., None]
    left_side = (jax.nn.sigmoid(projected[..., hidden:2 * hidden]) * projected[..., :hidden] * pair_mask).astype(jnp.bfloat16)
    right_side = (jax.nn.sigmoid(projected[..., 3 * hidden:]) * projected[..., 2 * hidden:3 * hidden] * pair_mask).astype(jnp.bfloat16)
    gating = jax.nn.sigmoid(jnp.dot(standardized_source, gate_weight, preferred_element_type=jnp.float32))
    if incoming:
        product = jnp.einsum('kic,kjc->ijc', left_side.astype(jnp.float32), right_side.astype(jnp.float32))
    else:
        product = jnp.einsum('ikc,jkc->ijc', left_side.astype(jnp.float32), right_side.astype(jnp.float32))
    product = product.astype(jnp.bfloat16)
    product_normed = standardize_features(product.astype(jnp.float32), gain_mid.astype(jnp.float32), -1).astype(jnp.bfloat16)
    return pair_now + jnp.dot(product_normed, final_weight, preferred_element_type=jnp.float32) * gating

def reference(homolog_stack, couple_tensor, homolog_presence, amino_presence, horizontal_standard_factor, horizontal_asking_matrix, horizontal_lookup_triple, horizontal_final_matrix, couple_offset_factor, couple_offset_matrix, vertical_standard_factor, vertical_asking_matrix, vertical_lookup_triple, vertical_final_matrix, tensor_average_factor, tensor_average_mapping, tensor_average_final, trio_entry_factors, trio_flank_mappings, trio_final_switches, trio_multiplied_factors, trio_final_matrices):
    nested_function = FOCUS_NUMBER * PER_FOCUS_WIDTH
    scaling = 1.0 / math.sqrt(PER_FOCUS_WIDTH)
    mask_as_float = homolog_presence.astype(jnp.float32)
    mask_penalty = MASK_PENALTY_SCALE * (mask_as_float - 1.0)
    standardized_source = standardize_features(homolog_stack, horizontal_standard_factor.astype(jnp.float32), -1).astype(jnp.bfloat16)
    queries = (jnp.dot(standardized_source, horizontal_asking_matrix, preferred_element_type=jnp.float32) * scaling).astype(jnp.bfloat16)
    others = jnp.dot(standardized_source, horizontal_lookup_triple, preferred_element_type=jnp.float32)
    keys_all = others[..., :nested_function].astype(jnp.bfloat16)
    content_entire = others[..., nested_function:2 * nested_function].astype(jnp.bfloat16)
    sigmoid_switches = jax.nn.sigmoid(others[..., 2 * nested_function:])
    pair_normed = standardize_features(couple_tensor, couple_offset_factor.astype(jnp.float32), -1).astype(jnp.bfloat16)
    pair_bias = jnp.dot(pair_normed, couple_offset_matrix, preferred_element_type=jnp.float32).astype(jnp.bfloat16)
    bias_heads = jnp.transpose(pair_bias, (2, 0, 1)).astype(jnp.float32)

    def row_attend(items):
        query_seq, key_seq, value_seq, penalty_seq = items
        shaped = (CHAIN_WINDOW, FOCUS_NUMBER, PER_FOCUS_WIDTH)
        scores = jnp.einsum('ihc,jhc->hij', query_seq.reshape(shaped).astype(jnp.float32), key_seq.reshape(shaped).astype(jnp.float32))
        scores = scores + bias_heads + penalty_seq[None, None, :]
        softmax_probabilities = jax.nn.softmax(scores, axis=-1).astype(jnp.bfloat16)
        mixed = jnp.einsum('hij,jhc->ihc', softmax_probabilities.astype(jnp.float32), value_seq.reshape(shaped).astype(jnp.float32))
        return mixed.reshape(CHAIN_WINDOW, nested_function)
    focused_content = lax.map(row_attend, (queries, keys_all, content_entire, mask_penalty))
    homolog_stack_horizontal = homolog_stack + jnp.dot((focused_content * sigmoid_switches).astype(jnp.bfloat16), horizontal_final_matrix, preferred_element_type=jnp.float32)
    reformed4 = (ALIGNED_STRANDS, CHAIN_WINDOW, FOCUS_NUMBER, PER_FOCUS_WIDTH)
    standardized_source = standardize_features(homolog_stack_horizontal, vertical_standard_factor.astype(jnp.float32), -1).astype(jnp.bfloat16)
    queries = (jnp.dot(standardized_source, vertical_asking_matrix, preferred_element_type=jnp.float32) * scaling).astype(jnp.bfloat16).reshape(reformed4)
    others = jnp.dot(standardized_source, vertical_lookup_triple, preferred_element_type=jnp.float32)
    keys_all = others[..., :nested_function].astype(jnp.bfloat16).reshape(reformed4)
    content_entire = others[..., nested_function:2 * nested_function].astype(jnp.bfloat16).reshape(reformed4)
    sigmoid_switches = jax.nn.sigmoid(others[..., 2 * nested_function:])
    scores = jnp.einsum('sihc,tihc->ihst', queries.astype(jnp.float32), keys_all.astype(jnp.float32))
    scores = scores + jnp.transpose(mask_penalty)[:, None, None, :]
    softmax_probabilities = jax.nn.softmax(scores, axis=-1).astype(jnp.bfloat16)
    focused_content = jnp.einsum('uovg,guox->vuox', softmax_probabilities.astype(jnp.float32), content_entire.astype(jnp.float32)).reshape(ALIGNED_STRANDS, CHAIN_WINDOW, nested_function)
    alignment_after_columns = homolog_stack_horizontal + jnp.dot((focused_content * sigmoid_switches).astype(jnp.bfloat16), vertical_final_matrix, preferred_element_type=jnp.float32)
    standardized_source = standardize_features(alignment_after_columns, tensor_average_factor.astype(jnp.float32), -1).astype(jnp.bfloat16)
    halves = jnp.dot(standardized_source, tensor_average_mapping, preferred_element_type=jnp.float32)
    left_proj = (halves[..., :TENSOR_HIDDEN] * mask_as_float[..., None]).astype(jnp.bfloat16)
    right_proj = (halves[..., TENSOR_HIDDEN:] * mask_as_float[..., None]).astype(jnp.bfloat16)
    right_float = right_proj.astype(jnp.float32)

    def opm_row(items):
        left_row, mask_row = items
        outer = jnp.einsum('sa,sjb->jab', left_row.astype(jnp.float32), right_float)
        outer = outer.astype(jnp.bfloat16).reshape(CHAIN_WINDOW, TENSOR_HIDDEN * TENSOR_HIDDEN)
        counts = jnp.dot(mask_row, mask_as_float, precision=lax.Precision.HIGHEST)
        return jnp.dot(outer, tensor_average_final, preferred_element_type=jnp.float32) / jnp.maximum(counts, 1.0)[:, None]
    product = lax.map(opm_row, (jnp.moveaxis(left_proj, 1, 0), jnp.transpose(mask_as_float)))
    pair_one = couple_tensor + product
    res_float = amino_presence.astype(jnp.float32)
    pair_two = triangle(pair_one, trio_entry_factors[0], trio_flank_mappings[0], trio_final_switches[0], trio_multiplied_factors[0], trio_final_matrices[0], res_float, False)
    pair_after_incoming = triangle(pair_two, trio_entry_factors[1], trio_flank_mappings[1], trio_final_switches[1], trio_multiplied_factors[1], trio_final_matrices[1], res_float, True)
    return (alignment_after_columns, pair_after_incoming)
```

```python
import math

import jax
import jax.numpy as jnp
from jax import lax
from jax.sharding import PartitionSpec as P

FOCUS_NUMBER = 8
PER_FOCUS_WIDTH = 32
TENSOR_HIDDEN = 32
TRI_HID = 128


EPSILON = 1e-05
MASK_PENALTY_SCALE = 1000000000.0


def standardize_features(content_vectors, gain, axis):
    centred = content_vectors - jnp.mean(content_vectors, axis=axis, keepdims=True)
    spread = jnp.mean(centred * centred, axis=axis, keepdims=True)
    return centred * lax.rsqrt(spread + EPSILON) * gain


def gather_blocks(block):
    device_count = lax.axis_size("dap")
    copies = jnp.broadcast_to(block[None], (device_count,) + block.shape)
    return lax.all_to_all(copies, "dap", split_axis=0, concat_axis=0, tiled=True)


def triangle(
    pair_now, gain_in, proj_weight, gate_weight, gain_mid, final_weight, amino_presence, incoming
):
    hidden = TRI_HID
    row_count = pair_now.shape[0]
    my_index = lax.axis_index("dap")
    standardized_source = standardize_features(pair_now, gain_in, -1).astype(jnp.bfloat16)
    projected = jnp.einsum(
        "rkd,de->erk", standardized_source, proj_weight, preferred_element_type=jnp.float32
    )
    res_float = amino_presence.astype(jnp.float32)
    own_rows = lax.dynamic_slice_in_dim(res_float, my_index * row_count, row_count)
    pair_mask = own_rows[:, None] * res_float[None, :]
    left_side = (
        jax.nn.sigmoid(projected[hidden : 2 * hidden]) * projected[:hidden] * pair_mask[None]
    ).astype(jnp.bfloat16)
    right_side = (
        jax.nn.sigmoid(projected[3 * hidden :])
        * projected[2 * hidden : 3 * hidden]
        * pair_mask[None]
    ).astype(jnp.bfloat16)
    gating = jax.nn.sigmoid(
        jnp.dot(standardized_source, gate_weight, preferred_element_type=jnp.float32)
    )
    device_count = lax.axis_size("dap")
    per_device = hidden // device_count
    both = jnp.stack(
        [
            left_side.reshape(device_count, per_device, row_count, -1),
            right_side.reshape(device_count, per_device, row_count, -1),
        ],
        axis=1,
    )
    both = lax.all_to_all(both, "dap", split_axis=0, concat_axis=0, tiled=True)
    both = jnp.moveaxis(both, 0, 2).reshape(2, per_device, device_count * row_count, -1)
    left_chan, right_chan = both[0], both[1]
    if incoming:
        product = jnp.einsum(
            "cki,ckj->cij", left_chan, right_chan, preferred_element_type=jnp.float32
        )
    else:
        product = jnp.einsum(
            "cik,cjk->cij", left_chan, right_chan, preferred_element_type=jnp.float32
        )
    product = product.astype(jnp.bfloat16)
    returned = lax.all_to_all(product, "dap", split_axis=1, concat_axis=0, tiled=True)
    product_normed = standardize_features(
        returned.astype(jnp.float32), gain_mid[:, None, None], 0
    ).astype(jnp.bfloat16)
    update = jnp.einsum(
        "crj,cd->rjd", product_normed, final_weight, preferred_element_type=jnp.float32
    )
    return pair_now + update * gating


def shards(
    homolog_stack,
    couple_tensor,
    homolog_presence,
    amino_presence,
    horizontal_standard_factor,
    horizontal_asking_matrix,
    horizontal_lookup_triple,
    horizontal_final_matrix,
    couple_offset_factor,
    couple_offset_matrix,
    vertical_standard_factor,
    vertical_asking_matrix,
    vertical_lookup_triple,
    vertical_final_matrix,
    tensor_average_factor,
    tensor_average_mapping,
    tensor_average_final,
    trio_entry_factors,
    trio_flank_mappings,
    trio_final_switches,
    trio_multiplied_factors,
    trio_final_matrices,
):
    nested_function = FOCUS_NUMBER * PER_FOCUS_WIDTH
    scaling = 1.0 / math.sqrt(PER_FOCUS_WIDTH)
    strand_portion = homolog_stack.shape[0]
    amino_total = homolog_stack.shape[1]
    row_count = couple_tensor.shape[0]
    pair_normed = standardize_features(couple_tensor, couple_offset_factor, -1).astype(jnp.bfloat16)
    bias_local = jnp.einsum(
        "rjc,ch->hrj", pair_normed, couple_offset_matrix, preferred_element_type=jnp.float32
    ).astype(jnp.bfloat16)
    standardized_source = standardize_features(
        homolog_stack, horizontal_standard_factor, -1
    ).astype(jnp.bfloat16)
    shaped = (strand_portion, amino_total, FOCUS_NUMBER, PER_FOCUS_WIDTH)
    queries = (
        (
            jnp.dot(
                standardized_source, horizontal_asking_matrix, preferred_element_type=jnp.float32
            )
            * scaling
        )
        .astype(jnp.bfloat16)
        .reshape(shaped)
    )
    others = jnp.dot(
        standardized_source, horizontal_lookup_triple, preferred_element_type=jnp.float32
    )
    keys_all = others[..., :nested_function].astype(jnp.bfloat16).reshape(shaped)
    content_entire = (
        others[..., nested_function : 2 * nested_function].astype(jnp.bfloat16).reshape(shaped)
    )
    sigmoid_switches = jax.nn.sigmoid(others[..., 2 * nested_function :])
    mask_penalty = MASK_PENALTY_SCALE * (homolog_presence.astype(jnp.float32) - 1.0)

    def attend(bias_piece):
        query_rows = bias_piece.shape[1]
        scores = jnp.einsum(
            "sihc,sjhc->shij", queries, keys_all, preferred_element_type=jnp.float32
        )
        scores = scores + bias_piece.astype(jnp.float32)[None] + mask_penalty[:, None, None, :]
        softmax_probabilities = jax.nn.softmax(scores, axis=-1).astype(jnp.bfloat16)
        mixed = jnp.einsum(
            "shij,sjhc->sihc",
            softmax_probabilities,
            content_entire,
            preferred_element_type=jnp.float32,
        )
        return mixed.reshape(strand_portion, query_rows, nested_function)

    bias_whole = jnp.moveaxis(gather_blocks(bias_local), 0, 1).reshape(
        FOCUS_NUMBER, amino_total, amino_total
    )
    block_rows = math.gcd(amino_total, 256)

    def one_block(block_index):
        return attend(bias_whole)

    blocks = lax.map(one_block, jnp.arange(amino_total // block_rows, dtype=jnp.int32))
    focused_content = jnp.moveaxis(blocks, 0, 1).reshape(
        strand_portion, amino_total, nested_function
    )
    homolog_stack_horizontal = homolog_stack + jnp.dot(
        (focused_content * sigmoid_switches).astype(jnp.bfloat16),
        horizontal_final_matrix,
        preferred_element_type=jnp.float32,
    )
    travelling = jnp.concatenate(
        [
            homolog_stack_horizontal.astype(jnp.bfloat16),
            jnp.broadcast_to(
                homolog_presence.astype(jnp.bfloat16)[..., None],
                (strand_portion, amino_total, 128),
            ),
        ],
        axis=-1,
    )
    arrived = lax.all_to_all(travelling, "dap", split_axis=1, concat_axis=0, tiled=True)
    column_view = arrived[..., :nested_function].astype(jnp.float32)
    col_mask = arrived[..., nested_function].astype(jnp.float32)
    seq_total = column_view.shape[0]
    col_shape = (seq_total, row_count, FOCUS_NUMBER, PER_FOCUS_WIDTH)
    standardized_source = standardize_features(column_view, vertical_standard_factor, -1).astype(
        jnp.bfloat16
    )
    col_queries = (
        (
            jnp.dot(standardized_source, vertical_asking_matrix, preferred_element_type=jnp.float32)
            * scaling
        )
        .astype(jnp.bfloat16)
        .reshape(col_shape)
    )
    col_others = jnp.dot(
        standardized_source, vertical_lookup_triple, preferred_element_type=jnp.float32
    )
    col_keys = col_others[..., :nested_function].astype(jnp.bfloat16).reshape(col_shape)
    col_values = (
        col_others[..., nested_function : 2 * nested_function]
        .astype(jnp.bfloat16)
        .reshape(col_shape)
    )
    col_gates = jax.nn.sigmoid(col_others[..., 2 * nested_function :])
    col_penalty = MASK_PENALTY_SCALE * (col_mask - 1.0)
    scores = jnp.einsum(
        "sihc,tihc->ihst", col_queries, col_keys, preferred_element_type=jnp.float32
    )
    scores = scores + jnp.transpose(col_penalty)[:, None, None, :]
    softmax_probabilities = jax.nn.softmax(scores, axis=-1).astype(jnp.bfloat16)
    col_mixed = jnp.einsum(
        "uovg,guox->vuox", softmax_probabilities, col_values, preferred_element_type=jnp.float32
    ).reshape(seq_total, row_count, nested_function)
    alignment_after_columns = column_view + jnp.dot(
        (col_mixed * col_gates).astype(jnp.bfloat16),
        vertical_final_matrix,
        preferred_element_type=jnp.float32,
    )
    standardized_source = standardize_features(
        alignment_after_columns, tensor_average_factor, -1
    ).astype(jnp.bfloat16)
    halves = jnp.dot(
        standardized_source, tensor_average_mapping, preferred_element_type=jnp.float32
    )
    left_proj = (halves[..., :TENSOR_HIDDEN] * col_mask[..., None]).astype(jnp.bfloat16)
    right_proj = (halves[..., TENSOR_HIDDEN:] * col_mask[..., None]).astype(jnp.bfloat16)
    block = jnp.concatenate(
        [right_proj, col_mask.astype(jnp.bfloat16)[..., None]], axis=-1
    )
    block = jnp.transpose(block, (1, 2, 0))
    whole = gather_blocks(block).reshape(amino_total, TENSOR_HIDDEN + 1, seq_total)
    right_whole = jnp.transpose(whole[:, :TENSOR_HIDDEN], (2, 0, 1))
    mask_whole = jnp.transpose(whole[:, TENSOR_HIDDEN])
    outer = jnp.einsum("sra,sjb->rjab", left_proj, right_whole, preferred_element_type=jnp.float32)
    outer = outer.astype(jnp.bfloat16).reshape(
        row_count, amino_total, TENSOR_HIDDEN * TENSOR_HIDDEN
    )
    counts = jnp.dot(
        jnp.transpose(col_mask), mask_whole.astype(jnp.float32), precision=lax.Precision.HIGHEST
    )
    product = (
        jnp.dot(outer, tensor_average_final, preferred_element_type=jnp.float32)
        / jnp.maximum(counts, 1.0)[..., None]
    )
    pair_one = couple_tensor + product
    pair_two = triangle(
        pair_one,
        trio_entry_factors[0],
        trio_flank_mappings[0],
        trio_final_switches[0],
        trio_multiplied_factors[0],
        trio_final_matrices[0],
        amino_presence,
        False,
    )
    pair_after_incoming = triangle(
        pair_two,
        trio_entry_factors[1],
        trio_flank_mappings[1],
        trio_final_switches[1],
        trio_multiplied_factors[1],
        trio_final_matrices[1],
        amino_presence,
        True,
    )
    return (alignment_after_columns, pair_after_incoming)


def solution(mesh):
    placed = (
        P("dap", None, None),
        P("dap", None, None),
        P("dap", None),
        P(),
        P(),
        P(),
        P(),
        P(),
        P(),
        P(),
        P(),
        P(),
        P(),
        P(),
        P(),
        P(),
        P(),
        P(),
        P(),
        P(),
        P(),
        P(),
    )
    return jax.shard_map(
        shards,
        mesh=mesh,
        in_specs=placed,
        out_specs=(P(None, "dap", None), P("dap", None, None)),
        check_vma=False,
    )
```

```python
import math

import jax
import jax.numpy as jnp
from jax import lax
from jax.experimental import pallas as pl
from jax.experimental.pallas import tpu as pltpu
from jax.sharding import PartitionSpec as P

FOCUS_NUMBER = 8
PER_FOCUS_WIDTH = 32
TENSOR_HIDDEN = 32
TRI_HID = 128


EPSILON = 1e-05
MASK_PENALTY_SCALE = 1000000000.0


def standardize_features(content_vectors, gain, axis):
    centred = content_vectors - jnp.mean(content_vectors, axis=axis, keepdims=True)
    spread = jnp.mean(centred * centred, axis=axis, keepdims=True)
    return centred * lax.rsqrt(spread + EPSILON) * gain


def gather_blocks(block):
    device_count = lax.axis_size("dap")
    copies = jnp.broadcast_to(block[None], (device_count,) + block.shape)
    return lax.all_to_all(copies, "dap", split_axis=0, concat_axis=0, tiled=True)


def triangle(
    pair_now, gain_in, proj_weight, gate_weight, gain_mid, final_weight, amino_presence, incoming
):
    hidden = TRI_HID
    row_count = pair_now.shape[0]
    my_index = lax.axis_index("dap")
    standardized_source = standardize_features(pair_now, gain_in, -1).astype(jnp.bfloat16)
    projected = jnp.einsum(
        "rkd,de->erk", standardized_source, proj_weight, preferred_element_type=jnp.float32
    )
    res_float = amino_presence.astype(jnp.float32)
    own_rows = lax.dynamic_slice_in_dim(res_float, my_index * row_count, row_count)
    pair_mask = own_rows[:, None] * res_float[None, :]
    left_side = (
        jax.nn.sigmoid(projected[hidden : 2 * hidden]) * projected[:hidden] * pair_mask[None]
    ).astype(jnp.bfloat16)
    right_side = (
        jax.nn.sigmoid(projected[3 * hidden :])
        * projected[2 * hidden : 3 * hidden]
        * pair_mask[None]
    ).astype(jnp.bfloat16)
    gating = jax.nn.sigmoid(
        jnp.dot(standardized_source, gate_weight, preferred_element_type=jnp.float32)
    )
    device_count = lax.axis_size("dap")
    per_device = hidden // device_count
    both = jnp.stack(
        [
            left_side.reshape(device_count, per_device, row_count, -1),
            right_side.reshape(device_count, per_device, row_count, -1),
        ],
        axis=1,
    )
    both = lax.all_to_all(both, "dap", split_axis=0, concat_axis=0, tiled=True)
    both = jnp.moveaxis(both, 0, 2).reshape(2, per_device, device_count * row_count, -1)
    left_chan, right_chan = both[0], both[1]
    if incoming:
        product = jnp.einsum(
            "cki,ckj->cij", left_chan, right_chan, preferred_element_type=jnp.float32
        )
    else:
        product = jnp.einsum(
            "cik,cjk->cij", left_chan, right_chan, preferred_element_type=jnp.float32
        )
    product = product.astype(jnp.bfloat16)
    returned = lax.all_to_all(product, "dap", split_axis=1, concat_axis=0, tiled=True)
    product_normed = standardize_features(
        returned.astype(jnp.float32), gain_mid[:, None, None], 0
    ).astype(jnp.bfloat16)
    update = jnp.einsum(
        "crj,cd->rjd", product_normed, final_weight, preferred_element_type=jnp.float32
    )
    return pair_now + update * gating


def shards(
    homolog_stack,
    couple_tensor,
    homolog_presence,
    amino_presence,
    horizontal_standard_factor,
    horizontal_asking_matrix,
    horizontal_lookup_triple,
    horizontal_final_matrix,
    couple_offset_factor,
    couple_offset_matrix,
    vertical_standard_factor,
    vertical_asking_matrix,
    vertical_lookup_triple,
    vertical_final_matrix,
    tensor_average_factor,
    tensor_average_mapping,
    tensor_average_final,
    trio_entry_factors,
    trio_flank_mappings,
    trio_final_switches,
    trio_multiplied_factors,
    trio_final_matrices,
):
    nested_function = FOCUS_NUMBER * PER_FOCUS_WIDTH
    scaling = 1.0 / math.sqrt(PER_FOCUS_WIDTH)
    strand_portion = homolog_stack.shape[0]
    amino_total = homolog_stack.shape[1]
    row_count = couple_tensor.shape[0]
    pair_normed = standardize_features(couple_tensor, couple_offset_factor, -1).astype(jnp.bfloat16)
    bias_local = jnp.einsum(
        "rjc,ch->hrj", pair_normed, couple_offset_matrix, preferred_element_type=jnp.float32
    ).astype(jnp.bfloat16)
    standardized_source = standardize_features(
        homolog_stack, horizontal_standard_factor, -1
    ).astype(jnp.bfloat16)
    shaped = (strand_portion, amino_total, FOCUS_NUMBER, PER_FOCUS_WIDTH)
    queries = (
        (
            jnp.dot(
                standardized_source, horizontal_asking_matrix, preferred_element_type=jnp.float32
            )
            * scaling
        )
        .astype(jnp.bfloat16)
        .reshape(shaped)
    )
    others = jnp.dot(
        standardized_source, horizontal_lookup_triple, preferred_element_type=jnp.float32
    )
    keys_all = others[..., :nested_function].astype(jnp.bfloat16).reshape(shaped)
    content_entire = (
        others[..., nested_function : 2 * nested_function].astype(jnp.bfloat16).reshape(shaped)
    )
    sigmoid_switches = jax.nn.sigmoid(others[..., 2 * nested_function :])
    mask_penalty = MASK_PENALTY_SCALE * (homolog_presence.astype(jnp.float32) - 1.0)

    def attend(bias_piece):
        query_rows = bias_piece.shape[1]
        scores = jnp.einsum(
            "sihc,sjhc->shij", queries, keys_all, preferred_element_type=jnp.float32
        )
        scores = scores + bias_piece.astype(jnp.float32)[None] + mask_penalty[:, None, None, :]
        softmax_probabilities = jax.nn.softmax(scores, axis=-1).astype(jnp.bfloat16)
        mixed = jnp.einsum(
            "shij,sjhc->sihc",
            softmax_probabilities,
            content_entire,
            preferred_element_type=jnp.float32,
        )
        return mixed.reshape(strand_portion, query_rows, nested_function)

    bias_whole = jnp.moveaxis(gather_blocks(bias_local), 0, 1).reshape(
        FOCUS_NUMBER, amino_total, amino_total
    )
    block_rows = math.gcd(amino_total, 256)

    def one_block(block_index):
        return attend(bias_whole)

    blocks = lax.map(one_block, jnp.arange(amino_total // block_rows, dtype=jnp.int32))
    focused_content = jnp.moveaxis(blocks, 0, 1).reshape(
        strand_portion, amino_total, nested_function
    )
    homolog_stack_horizontal = homolog_stack + jnp.dot(
        (focused_content * sigmoid_switches).astype(jnp.bfloat16),
        horizontal_final_matrix,
        preferred_element_type=jnp.float32,
    )
    travelling = jnp.concatenate(
        [
            homolog_stack_horizontal.astype(jnp.bfloat16),
            jnp.broadcast_to(
                homolog_presence.astype(jnp.bfloat16)[..., None],
                (strand_portion, amino_total, 128),
            ),
        ],
        axis=-1,
    )
    arrived = lax.all_to_all(travelling, "dap", split_axis=1, concat_axis=0, tiled=True)
    column_view = arrived[..., :nested_function].astype(jnp.float32)
    col_mask = arrived[..., nested_function].astype(jnp.float32)
    seq_total = column_view.shape[0]
    col_shape = (seq_total, row_count, FOCUS_NUMBER, PER_FOCUS_WIDTH)
    standardized_source = standardize_features(column_view, vertical_standard_factor, -1).astype(
        jnp.bfloat16
    )
    col_queries = (
        (
            jnp.dot(standardized_source, vertical_asking_matrix, preferred_element_type=jnp.float32)
            * scaling
        )
        .astype(jnp.bfloat16)
        .reshape(col_shape)
    )
    col_others = jnp.dot(
        standardized_source, vertical_lookup_triple, preferred_element_type=jnp.float32
    )
    col_keys = col_others[..., :nested_function].astype(jnp.bfloat16).reshape(col_shape)
    col_values = (
        col_others[..., nested_function : 2 * nested_function]
        .astype(jnp.bfloat16)
        .reshape(col_shape)
    )
    col_gates = jax.nn.sigmoid(col_others[..., 2 * nested_function :])
    col_penalty = MASK_PENALTY_SCALE * (col_mask - 1.0)
    scores = jnp.einsum(
        "sihc,tihc->ihst", col_queries, col_keys, preferred_element_type=jnp.float32
    )
    scores = scores + jnp.transpose(col_penalty)[:, None, None, :]
    softmax_probabilities = jax.nn.softmax(scores, axis=-1).astype(jnp.bfloat16)
    col_mixed = jnp.einsum(
        "uovg,guox->vuox", softmax_probabilities, col_values, preferred_element_type=jnp.float32
    ).reshape(seq_total, row_count, nested_function)
    alignment_after_columns = column_view + jnp.dot(
        (col_mixed * col_gates).astype(jnp.bfloat16),
        vertical_final_matrix,
        preferred_element_type=jnp.float32,
    )
    standardized_source = standardize_features(
        alignment_after_columns, tensor_average_factor, -1
    ).astype(jnp.bfloat16)
    halves = jnp.dot(
        standardized_source, tensor_average_mapping, preferred_element_type=jnp.float32
    )
    left_proj = (halves[..., :TENSOR_HIDDEN] * col_mask[..., None]).astype(jnp.bfloat16)
    right_proj = (halves[..., TENSOR_HIDDEN:] * col_mask[..., None]).astype(jnp.bfloat16)
    block = jnp.concatenate(
        [right_proj, col_mask.astype(jnp.bfloat16)[..., None]], axis=-1
    )
    block = jnp.transpose(block, (1, 2, 0))
    whole = gather_blocks(block).reshape(amino_total, TENSOR_HIDDEN + 1, seq_total)
    right_whole = jnp.transpose(whole[:, :TENSOR_HIDDEN], (2, 0, 1))
    mask_whole = jnp.transpose(whole[:, TENSOR_HIDDEN])
    outer = jnp.einsum("sra,sjb->rjab", left_proj, right_whole, preferred_element_type=jnp.float32)
    outer = outer.astype(jnp.bfloat16).reshape(
        row_count, amino_total, TENSOR_HIDDEN * TENSOR_HIDDEN
    )
    counts = jnp.dot(
        jnp.transpose(col_mask), mask_whole.astype(jnp.float32), precision=lax.Precision.HIGHEST
    )
    product = (
        jnp.dot(outer, tensor_average_final, preferred_element_type=jnp.float32)
        / jnp.maximum(counts, 1.0)[..., None]
    )
    pair_one = couple_tensor + product
    pair_two = triangle(
        pair_one,
        trio_entry_factors[0],
        trio_flank_mappings[0],
        trio_final_switches[0],
        trio_multiplied_factors[0],
        trio_final_matrices[0],
        amino_presence,
        False,
    )
    pair_after_incoming = triangle(
        pair_two,
        trio_entry_factors[1],
        trio_flank_mappings[1],
        trio_final_switches[1],
        trio_multiplied_factors[1],
        trio_final_matrices[1],
        amino_presence,
        True,
    )
    return (alignment_after_columns, pair_after_incoming)


def normed_rows(x, gain):
    centred = x - jnp.mean(x, axis=-1, keepdims=True)
    spread = jnp.mean(centred * centred, axis=-1, keepdims=True)
    return centred * lax.rsqrt(spread + EPSILON) * gain


def dot_nn(a, b):
    return lax.dot_general(a, b, (((1,), (0,)), ((), ())), preferred_element_type=jnp.float32)


def dot_nt(a, b):
    return lax.dot_general(a, b, (((1,), (1,)), ((), ())), preferred_element_type=jnp.float32)


def dot_tn(a, b):
    return lax.dot_general(a, b, (((0,), (0,)), ((), ())), preferred_element_type=jnp.float32)


def lane_iota(shape):
    return lax.broadcasted_iota(jnp.int32, shape, len(shape) - 1)


def vmem_call(body, outs, scratch=(), smem=(), count=0, cost=None, grant=20 << 20):
    whole = pl.BlockSpec(memory_space=pltpu.VMEM)
    scalar = pl.BlockSpec(memory_space=pltpu.SMEM)
    return pl.pallas_call(
        body,
        out_shape=outs,
        in_specs=[scalar if k in smem else whole for k in range(count)],
        out_specs=jax.tree.map(lambda _: whole, outs),
        scratch_shapes=list(scratch),
        cost_estimate=cost,
        compiler_params=pltpu.CompilerParams(vmem_limit_bytes=grant),
    )


def bias_body(pair_ref, gain_ref, weight_ref, present_ref, out_ref):
    normed = normed_rows(pair_ref[...], gain_ref[...]).astype(jnp.bfloat16)
    bias = dot_nt(weight_ref[...], normed)
    present = present_ref[...].astype(jnp.float32)
    mask_row = jnp.concatenate([present[0:1], present[1:2]], axis=1)
    fill = jnp.zeros((out_ref.shape[1] - bias.shape[0] - 1, bias.shape[1]), jnp.float32)
    block = jnp.concatenate([bias, mask_row, fill], axis=0).astype(jnp.bfloat16)
    out_ref[...] = jnp.broadcast_to(block[None], out_ref.shape)


def put_parts(ref, value):
    lanes = ref.shape[2]
    for part in range(ref.shape[0]):
        ref[part] = value[:, part * lanes : (part + 1) * lanes]


def rows_of(ref, rows):
    return jnp.concatenate([ref[part, rows, :] for part in range(ref.shape[0])], axis=1)


def project_body(x_ref, gain_ref, ask_ref, look_ref, q_ref, k_ref, v_ref, g_ref):
    width = ask_ref.shape[1]
    normed = normed_rows(x_ref[...], gain_ref[...]).astype(jnp.bfloat16)
    scaling = 1.0 / math.sqrt(PER_FOCUS_WIDTH)
    q = (dot_nn(normed, ask_ref[...]) * scaling).astype(jnp.bfloat16).astype(jnp.float32)
    put_parts(q_ref, q)
    others = dot_nn(normed, look_ref[...])
    k_ref[...] = others[:, :width].astype(jnp.bfloat16)
    v_ref[...] = others[:, width : 2 * width].astype(jnp.bfloat16)
    put_parts(g_ref, jax.nn.sigmoid(others[:, 2 * width :]))


def head_spread(q):
    head_of = lane_iota(q.shape) // PER_FOCUS_WIDTH
    return jnp.concatenate(
        [jnp.where(head_of == h, q, 0.0) for h in range(FOCUS_NUMBER)], axis=0
    ).astype(jnp.bfloat16)


def attend_heads(q, k, v, offset):
    scores = dot_nt(head_spread(q), k) + offset
    scores = scores - jnp.max(scores, axis=-1, keepdims=True)
    raised = jnp.exp(scores)
    shares = (raised / jnp.sum(raised, axis=-1, keepdims=True)).astype(jnp.bfloat16)
    mixed = dot_nn(shares, v)
    rows = q.shape[0]
    head_of = lane_iota(q.shape) // PER_FOCUS_WIDTH
    total = jnp.where(head_of == 0, mixed[:rows], 0.0)
    for h in range(1, FOCUS_NUMBER):
        total = jnp.where(head_of == h, mixed[h * rows : (h + 1) * rows], total)
    return total


def row_body(blk_ref, x_ref, q_ref, k_ref, v_ref, g_ref, final_ref, present_ref, out_ref, wide, send, x_parts):
    devices = blk_ref.shape[0]
    put_parts(x_parts, x_ref[...])
    per_block = blk_ref.shape[1]
    half = wide.shape[1] // 2
    per_seq = 2 * devices
    wide[...] = blk_ref[...].astype(jnp.float32).reshape(wide.shape)
    penalty = MASK_PENALTY_SCALE * (present_ref[...].astype(jnp.float32) - 1.0)
    heads = [wide[pl.ds(h, devices, stride=per_block), :] for h in range(FOCUS_NUMBER)]
    for s in range(2):
        keys = k_ref[s * per_seq : (s + 1) * per_seq, :]
        values = v_ref[s * per_seq : (s + 1) * per_seq, :]
        for r in range(2):
            rows = pl.ds(s * per_seq + r, devices, stride=2)
            bias = jnp.concatenate([b[:, r * half : (r + 1) * half] for b in heads], axis=0)
            mixed = attend_heads(rows_of(q_ref, rows), keys, values, bias + penalty[s : s + 1])
            y = (mixed * rows_of(g_ref, rows)).astype(jnp.bfloat16)
            updated = rows_of(x_parts, rows) + dot_nn(y, final_ref[...])
            for part in range(updated.shape[1] // (2 * half)):
                to = pl.ds((s * 2 + r) * 2 + part, devices, stride=out_ref.shape[1])
                send[to, :] = updated[:, part * 2 * half : (part + 1) * 2 * half]
    out_ref[...] = send[...].reshape(out_ref.shape).astype(jnp.bfloat16)


def mask_block(blk_ref, wide):
    wide[...] = blk_ref[...].astype(jnp.float32).reshape(wide.shape)
    rows = pl.ds(FOCUS_NUMBER, blk_ref.shape[0], stride=blk_ref.shape[1])
    return wide[rows, :].astype(jnp.bfloat16)


def column_body(
    arrived_ref, blk_ref, gain_ref, ask_ref, look_ref, final_ref, gain_out_ref, map_ref,
    msa_ref, opm_ref, wide, wide_blk, x_all, msa,
):
    devices = arrived_ref.shape[0]
    width = ask_ref.shape[1]
    lanes = wide.shape[1]
    half = lanes // 2
    seqs = 2 * devices
    me = lax.axis_index("dap")
    wide[...] = arrived_ref[...].astype(jnp.float32).reshape(wide.shape)
    for r in range(2):
        for s in range(2):
            base = (s * 2 + r) * 2
            at = (r * 2 + s) * devices
            for part in range(2):
                x_all[at : at + devices, part * lanes : (part + 1) * lanes] = wide[
                    pl.ds(base + part, devices, stride=8), :
                ]
    mask_lanes = mask_block(blk_ref, wide_blk)
    row = lax.broadcasted_iota(jnp.int32, (8, lanes), 0)
    wanted = (row % 2) * half + 2 * me + row // 2
    pick = jnp.where((lane_iota((8, lanes)) == wanted) & (row < 4), 1.0, 0.0).astype(jnp.bfloat16)
    picked = dot_nt(pick, mask_lanes)
    present = [
        jnp.concatenate([picked[2 * r : 2 * r + 1], picked[2 * r + 1 : 2 * r + 2]], axis=1)
        for r in range(2)
    ]
    x = x_all[...]
    normed = normed_rows(x, gain_ref[...]).astype(jnp.bfloat16)
    scaling = 1.0 / math.sqrt(PER_FOCUS_WIDTH)
    q = (dot_nn(normed, ask_ref[...]) * scaling).astype(jnp.bfloat16).astype(jnp.float32)
    others = dot_nn(normed, look_ref[...])
    keys = others[:, :width].astype(jnp.bfloat16)
    values = others[:, width : 2 * width].astype(jnp.bfloat16)
    gates = jax.nn.sigmoid(others[:, 2 * width :])
    mixed = jnp.concatenate(
        [
            attend_heads(
                q[r * seqs : (r + 1) * seqs],
                keys[r * seqs : (r + 1) * seqs],
                values[r * seqs : (r + 1) * seqs],
                MASK_PENALTY_SCALE * (present[r] - 1.0),
            )
            for r in range(2)
        ],
        axis=0,
    )
    updated = x + dot_nn((mixed * gates).astype(jnp.bfloat16), final_ref[...])
    for r in range(2):
        for s in range(2):
            at = (r * 2 + s) * devices
            for part in range(2):
                msa[r * 2 + part, pl.ds(s, devices, stride=2), :] = updated[
                    at : at + devices, part * lanes : (part + 1) * lanes
                ]
    for part in range(4):
        msa_ref[:, part * lanes : (part + 1) * lanes] = msa[part]
    normed = normed_rows(updated, gain_out_ref[...]).astype(jnp.bfloat16)
    sides = [
        dot_nt(map_ref[...], normed[r * seqs : (r + 1) * seqs]) * present[r] for r in range(2)
    ]
    block = jnp.concatenate(sides, axis=1).astype(jnp.bfloat16)
    opm_ref[...] = jnp.broadcast_to(block[None], opm_ref.shape)


def gated(projected, q_at, g_at, width):
    return jax.nn.sigmoid(projected[:, g_at : g_at + width]) * projected[:, q_at : q_at + width]


def presence_down(amino_row, half, lanes):
    square = lax.broadcasted_iota(jnp.int32, (half, half), 0) == lane_iota((half, half))
    diagonal = jnp.where(square, amino_row.astype(jnp.float32), 0.0).astype(jnp.bfloat16)
    return dot_nn(diagonal, jnp.ones((half, lanes), jnp.bfloat16))


def gathered_at(chip, my_chip, chips):
    apart = chip ^ my_chip
    stages = chips.bit_length() - 1
    place = jnp.int32(0)
    for k in range(stages):
        place = place | (((apart >> (stages - 1 - k)) & 1) << k)
    return place


def opm_body(
    own_ref, oth_ref, blk_ref, near_ref, far_ref, fin_ref, amino_ref, amino_row_ref, gain_ref,
    flank_ref, switch_ref,
    pair_one_ref, left_ref, gate_ref, right_ref,
    order, order16, outer, counts, mkeys, wide_blk,
):
    chips, both, lanes = own_ref.shape
    hidden = both // 2
    half = lanes // 2
    channels = switch_ref.shape[0]
    me = lax.axis_index("dap")
    parity = lax.rem(me, 2)
    my_chip = me // 2
    own = own_ref[:, hidden:, :].astype(jnp.float32)
    oth = oth_ref[:, hidden:, :].astype(jnp.float32)
    flag = jnp.broadcast_to(parity, (1, 1, 1)) == 0
    order16[0] = jnp.where(flag, own, oth).reshape(order16.shape[1:])
    order16[1] = jnp.where(flag, oth, own).reshape(order16.shape[1:])
    for b in range(hidden):
        for p in range(2):
            rows = order16[p, pl.ds(b, chips, stride=hidden), :]
            for r in range(2):
                order[pl.ds(b * half + 2 * p + r, chips, stride=4), :] = (
                    pltpu.roll(rows, half, 1) if r else rows
                )
    rights = order[...].astype(jnp.bfloat16)[:, :half]
    for r in range(2):
        lhs = own_ref[:, :hidden, :].reshape(chips * hidden, lanes)[:, r * half : (r + 1) * half]
        outer[r] = dot_nt(lhs, rights).astype(jnp.bfloat16).reshape(outer.shape[1:])
    mask_rows = mask_block(blk_ref, wide_blk)
    total = jnp.zeros((half, lanes), jnp.float32)
    for s in range(2):
        part = mask_rows[:, s * half : (s + 1) * half]
        total = total + dot_tn(part, jnp.concatenate([part, part], axis=1))
    counts[...] = 1.0 / jnp.maximum(total, 1.0)
    mkeys[...] = presence_down(amino_row_ref[...], half, lanes)
    gain = gain_ref[...]
    low = lane_iota((channels, lanes)) < half
    low_row = lane_iota((1, lanes)) < half
    group = 4
    near = near_ref.shape[0]

    @pl.loop(0, chips // group)
    def _(block):
        pairs, keeps = [], []
        for c in range(group):
            chip = block * group + c
            sides = []
            for r in range(2):
                strip = outer[r, chip]
                sides.append(
                    jnp.concatenate(
                        [strip[:, g * lanes : (g + 1) * lanes] for g in range(hidden // 2)], axis=0
                    )
                )
            res = dot_nn(fin_ref[...], jnp.concatenate(sides, axis=1))
            a0, a1 = res[:channels, :lanes], res[:channels, lanes:]
            b0, b1 = res[channels:, :lanes], res[channels:, lanes:]
            turned = jnp.where(low, a0, b1) + pltpu.roll(jnp.where(low, a1, b0), half, 1)
            i0 = 4 * chip + 2 * parity
            share = jnp.where(low_row, counts[pl.ds(i0, 1), :], counts[pl.ds(i0 + 1, 1), :])
            place = gathered_at(chip, my_chip, chips)
            at = lax.rem(place, near)
            couple = jnp.where(
                jnp.broadcast_to(place, (1, 1)) < near,
                near_ref[at].astype(jnp.float32),
                far_ref[at].astype(jnp.float32),
            )
            pairs.append(jnp.transpose(turned * share) + couple)
            for r in range(2):
                keeps.append(mkeys[...] * amino_ref[i0 + r].astype(jnp.float32))
        pair = jnp.concatenate(pairs, axis=0)
        keep = jnp.concatenate(keeps, axis=0)
        normed = normed_rows(pair, gain).astype(jnp.bfloat16)
        projected = dot_nn(normed, flank_ref[...])
        left = gated(projected, 0, channels, channels) * keep
        right = gated(projected, 2 * channels, 3 * channels, channels) * keep
        gate = jax.nn.sigmoid(dot_nn(normed, switch_ref[...]))
        for c in range(group):
            chip = block * group + c
            rows = slice(c * lanes, (c + 1) * lanes)
            pair_one_ref[chip] = pair[rows]
            gate_ref[chip] = gate[rows]
            left_ref[chip] = jnp.transpose(left[rows])
            right_ref[chip] = jnp.transpose(right[rows]).astype(jnp.bfloat16)


def outgoing_body(
    pair_one_ref, left_ref, gate_ref, own_ref, oth_ref, amino_ref, amino_row_ref, gain_mid_ref,
    final_ref, gain_ref, flank_ref,
    two_ref, send_ref,
    sides, prods, mkeys, pair_two, rows_out, cols,
):
    chips, channels, lanes = own_ref.shape
    half = lanes // 2
    me = lax.axis_index("dap")
    parity = lax.rem(me, 2)
    my_chip = me // 2
    flag = jnp.broadcast_to(parity, (1, 1)) == 0

    @pl.loop(0, chips)
    def _(chip):
        own = own_ref[chip].astype(jnp.float32)
        oth = oth_ref[chip].astype(jnp.float32)
        rows = pl.ds(pl.multiple_of(chip * channels, channels), channels)
        sides[0, rows, :] = jnp.where(flag, own, oth)
        sides[1, rows, :] = jnp.where(flag, oth, own)

    low = lane_iota((chips, lanes)) < half

    per_step = 32

    @pl.loop(0, channels // per_step)
    def _(octet):
        results = []
        for c in range(per_step):
            at = pl.ds(octet * per_step + c, chips, stride=channels)
            lhs = left_ref[at, :].astype(jnp.bfloat16)
            pieces = [[], []]
            for p in range(2):
                rows = sides[p, at, :]
                turned = pltpu.roll(rows, half, 1)
                pieces[0] += [jnp.where(low, rows, 0.0), jnp.where(low, turned, 0.0)]
                pieces[1] += [jnp.where(low, 0.0, turned), jnp.where(low, 0.0, rows)]
            rhs = jnp.concatenate(pieces[0] + pieces[1], axis=0).astype(jnp.bfloat16)
            results.append(dot_nt(lhs, rhs))
        for c in range(per_step):
            to = pl.ds(pl.multiple_of((octet * per_step + c) * chips, chips), chips)
            prods[to, :] = results[c].astype(jnp.bfloat16).astype(jnp.float32)

    mkeys[...] = presence_down(amino_row_ref[...], half, channels)
    gain_mid = jnp.transpose(jnp.broadcast_to(gain_mid_ref[...], (channels, channels)))
    final_t = jnp.transpose(final_ref[...].astype(jnp.float32)).astype(jnp.bfloat16)
    gain = gain_ref[...]
    flank_right = flank_ref[:, 2 * channels :]
    flank_left = flank_ref[:, : 2 * channels]
    octet = pl.multiple_of(8 * (my_chip // 2), 8)
    group = 4
    for block in range(chips // group):
        changed = []
        for c in range(group):
            x = prods[pl.ds(block * group + c, channels, stride=chips), :]
            centred = x - jnp.mean(x, axis=0, keepdims=True)
            spread = jnp.mean(centred * centred, axis=0, keepdims=True)
            changed.append((centred * lax.rsqrt(spread + EPSILON) * gain_mid).astype(jnp.bfloat16))
        changed = dot_nn(final_t, jnp.concatenate(changed, axis=1))
        for c in range(group):
            part = jnp.transpose(changed[:, c * lanes : (c + 1) * lanes])
            for k in range(8):
                r, p, rj = k // 4, (k // 2) % 2, k % 2
                rows_out[c, pl.ds(r * half + 2 * p + rj, chips, stride=4), :] = part[
                    k * chips : (k + 1) * chips
                ]
        twos, keeps = [], []
        for c in range(group):
            chip = block * group + c
            two = pair_one_ref[chip] + rows_out[c] * gate_ref[chip]
            twos.append(two)
            for r in range(2):
                keeps.append(amino_ref[4 * chip + 2 * parity + r].astype(jnp.float32))
        two = jnp.concatenate(twos, axis=0)
        full = normed_rows(two, gain)
        normed = full.astype(jnp.bfloat16)
        keep = jnp.concatenate([mkeys[...] * m for m in keeps], axis=0)
        going = (gated(dot_nn(normed, flank_right), 0, channels, channels) * keep).astype(jnp.bfloat16)
        cols[...] = full
        few = jnp.concatenate(
            [cols[pl.ds(k * half + octet, 8), :] for k in range(2 * group)], axis=0
        ).astype(jnp.bfloat16)
        mine = mkeys[pl.ds(octet, 8), :]
        keep = jnp.concatenate([mine * m for m in keeps], axis=0)
        few = (gated(dot_nn(few, flank_left), 0, channels, channels) * keep).astype(jnp.bfloat16)
        for c in range(group):
            chip = block * group + c
            pair_two[chip] = twos[c]
            send_ref[chip, :lanes, :] = going[c * lanes : (c + 1) * lanes]
            send_ref[chip, lanes:, :] = few[c * 16 : (c + 1) * 16]
    two_ref[...] = pair_two[my_chip]


def incoming_body(
    own_ref, oth_ref, two_ref, couple_ref, gain_ref, switch_ref, gain_mid_ref, final_ref,
    out_ref, right, left,
):
    chips, _, channels = own_ref.shape
    lanes2 = out_ref.shape[0]
    half = lanes2 // 2
    me = lax.axis_index("dap")
    first = 4 * lax.rem(me // 2, 2) + 2 * lax.rem(me, 2)
    row = lax.broadcasted_iota(jnp.int32, (8, channels), 0)
    totals = tuple(jnp.zeros((half, channels), jnp.float32) for _ in range(2))
    for side_ref in (own_ref, oth_ref):

        def step(chip, totals, side_ref=side_ref):
            totals = list(totals)
            tail = side_ref[chip, lanes2:, :].astype(jnp.float32)
            for k in range(2):
                there = side_ref[chip, k * half : (k + 1) * half, :].astype(jnp.float32)
                for i in range(2):
                    picked = jnp.where(row == first + i, tail[8 * k : 8 * k + 8], 0.0)
                    one = jnp.sum(picked, axis=0, keepdims=True)
                    totals[i] = totals[i] + one * there
            return tuple(totals)

        totals = lax.fori_loop(0, chips, step, totals)
    prod = jnp.concatenate(totals, axis=0).astype(jnp.bfloat16).astype(jnp.float32)
    changed = dot_nn(normed_rows(prod, gain_mid_ref[...]).astype(jnp.bfloat16), final_ref[...])
    two = two_ref[...]
    normed = normed_rows(two, gain_ref[...]).astype(jnp.bfloat16)
    gate = jax.nn.sigmoid(dot_nn(normed, switch_ref[...]))
    couple = couple_ref[...]
    lost = couple - couple.astype(jnp.bfloat16).astype(jnp.float32)
    out_ref[...] = two + lost + changed * gate


def paired_shards(
    homolog_stack,
    couple_tensor,
    homolog_presence,
    amino_presence,
    horizontal_standard_factor,
    horizontal_asking_matrix,
    horizontal_lookup_triple,
    horizontal_final_matrix,
    couple_offset_factor,
    couple_offset_matrix,
    vertical_standard_factor,
    vertical_asking_matrix,
    vertical_lookup_triple,
    vertical_final_matrix,
    tensor_average_factor,
    tensor_average_mapping,
    tensor_average_final,
    trio_entry_factors,
    trio_flank_mappings,
    trio_final_switches,
    trio_multiplied_factors,
    trio_final_matrices,
):
    devices = lax.axis_size("dap")
    chips = devices // 2
    strands, aminos, features = homolog_stack.shape
    rows, _, channels = couple_tensor.shape
    lanes = rows * aminos
    hidden = TENSOR_HIDDEN
    f32, bf16 = jnp.float32, jnp.bfloat16
    shape = jax.ShapeDtypeStruct
    same_parity = [[2 * chip + p for chip in range(chips)] for p in range(2)]
    swap = [(d, d ^ 1) for d in range(devices)]

    def line(v):
        return v.reshape(1, -1)

    couple = couple_tensor.reshape(lanes, channels)
    x = homolog_stack.reshape(strands * aminos, features)
    block = vmem_call(
        bias_body, shape((devices, 16, lanes), bf16), count=4
    )(couple, line(couple_offset_factor), couple_offset_matrix.T, homolog_presence)
    blocks = lax.all_to_all(block, "dap", split_axis=0, concat_axis=0, tiled=True)
    q, k, v, g = vmem_call(
        project_body,
        (
            shape((features // lanes, lanes, lanes), f32),
            shape((lanes, features), bf16),
            shape((lanes, features), bf16),
            shape((features // lanes, lanes, lanes), f32),
        ),
        count=4,
    )(x, line(horizontal_standard_factor), horizontal_asking_matrix, horizontal_lookup_triple)
    near = couple.astype(bf16)[None]
    stages = chips.bit_length() - 1
    for stage in range(stages):
        reach = devices >> (stage + 1)
        far = lax.ppermute(near, "dap", [(d, d ^ reach) for d in range(devices)])
        if stage < stages - 1:
            near = jnp.concatenate([near, far], axis=0)
    sent = vmem_call(
        row_body,
        shape((devices, 8, lanes), bf16),
        scratch=[
            pltpu.VMEM((devices * 16, lanes), f32),
            pltpu.VMEM((devices * 8, lanes), f32),
            pltpu.VMEM((features // lanes, lanes, lanes), f32),
        ],
        count=8,
    )(blocks, x, q, k, v, g, horizontal_final_matrix, homolog_presence)
    arrived = lax.all_to_all(sent, "dap", split_axis=0, concat_axis=0, tiled=True)
    msa, opm = vmem_call(
        column_body,
        (shape((devices * strands, rows * features), f32), shape((chips, 2 * hidden, lanes), bf16)),
        scratch=[
            pltpu.VMEM((devices * 8, lanes), f32),
            pltpu.VMEM((devices * 16, lanes), f32),
            pltpu.VMEM((lanes, features), f32),
            pltpu.VMEM((4, devices * strands, lanes), f32),
        ],
        count=8,
    )(
        arrived,
        blocks,
        line(vertical_standard_factor),
        vertical_asking_matrix,
        vertical_lookup_triple,
        vertical_final_matrix,
        line(tensor_average_factor),
        tensor_average_mapping.T,
    )
    opm_own = lax.all_to_all(
        opm, "dap", split_axis=0, concat_axis=0, tiled=True, axis_index_groups=same_parity
    )
    opm_oth = lax.ppermute(opm_own, "dap", swap)
    final = jnp.transpose(
        tensor_average_final.reshape(hidden, hidden // 2, 2, channels), (2, 3, 1, 0)
    ).reshape(2 * channels, hidden * hidden // 2)
    stack = (chips, lanes, channels)
    amino_row = line(amino_presence)
    pair_one, left, gate, right_own = vmem_call(
        opm_body,
        (shape(stack, f32), shape(stack, f32), shape(stack, f32), shape(stack, bf16)),
        scratch=[
            pltpu.VMEM((hidden * aminos, lanes), f32),
            pltpu.VMEM((2, chips * hidden, lanes), f32),
            pltpu.VMEM((2, chips, hidden, hidden * aminos), bf16),
            pltpu.VMEM((aminos, lanes), f32),
            pltpu.VMEM((aminos, channels), f32),
            pltpu.VMEM((devices * 16, lanes), f32),
        ],
        smem=(6,),
        count=11,
    )(
        opm_own,
        opm_oth,
        blocks,
        near,
        far,
        final,
        amino_presence,
        amino_row,
        line(trio_entry_factors[0]),
        trio_flank_mappings[0],
        trio_final_switches[0],
    )
    right_oth = lax.ppermute(right_own, "dap", swap)
    two, going = vmem_call(
        outgoing_body,
        (shape((lanes, channels), f32), shape((chips, lanes + 16, channels), bf16)),
        scratch=[
            pltpu.VMEM((2, chips * channels, lanes), f32),
            pltpu.VMEM((channels * chips, lanes), f32),
            pltpu.VMEM((aminos, channels), f32),
            pltpu.VMEM(stack, f32),
            pltpu.VMEM((4, lanes, channels), f32),
            pltpu.VMEM((4 * lanes, channels), f32),
        ],
        smem=(5,),
        count=11,
    )(
        pair_one,
        left.reshape(chips * channels, lanes),
        gate,
        right_own,
        right_oth,
        amino_presence,
        amino_row,
        line(trio_multiplied_factors[0]),
        trio_final_matrices[0],
        line(trio_entry_factors[1]),
        trio_flank_mappings[1],
    )
    coming = lax.ppermute(going, "dap", swap)
    pair_out = vmem_call(
        incoming_body,
        shape((lanes, channels), f32),
        scratch=[pltpu.VMEM((8, channels), f32), pltpu.VMEM((8, channels), f32)],
        count=8,
    )(
        going,
        coming,
        two,
        couple,
        line(trio_entry_factors[1]),
        trio_final_switches[1],
        line(trio_multiplied_factors[1]),
        trio_final_matrices[1],
    )
    return (
        msa.reshape(devices * strands, rows, features),
        pair_out.reshape(rows, aminos, channels),
    )


def fits_pairs(homolog_stack, couple_tensor, devices):
    strands, aminos, features = homolog_stack.shape
    rows, _, channels = couple_tensor.shape
    lanes = 128
    return (
        strands == rows == 2
        and devices % 8 == 0
        and devices & (devices - 1) == 0
        and rows * aminos == lanes == channels
        and aminos == 2 * devices
        and features == 2 * lanes
    )


def either(*arrays):
    if fits_pairs(arrays[0], arrays[1], lax.axis_size("dap")):
        return paired_shards(*arrays)
    return shards(*arrays)


def solution(mesh):
    placed = (
        P("dap", None, None),
        P("dap", None, None),
        P("dap", None),
        P(),
        P(),
        P(),
        P(),
        P(),
        P(),
        P(),
        P(),
        P(),
        P(),
        P(),
        P(),
        P(),
        P(),
        P(),
        P(),
        P(),
        P(),
        P(),
    )
    return jax.shard_map(
        either,
        mesh=mesh,
        in_specs=placed,
        out_specs=(P(None, "dap", None), P("dap", None, None)),
        check_vma=False,
    )
```

```python
import functools
import math

import jax
import jax.numpy as jnp
from jax import lax
from jax.experimental import pallas as pl
from jax.experimental.pallas import tpu as pltpu
from jax.sharding import PartitionSpec as P

FOCUS_NUMBER = 8
PER_FOCUS_WIDTH = 32
TENSOR_HIDDEN = 32
TRI_HID = 128


EPSILON = 1e-05
MASK_PENALTY_SCALE = 1000000000.0


def standardize_features(content_vectors, gain, axis):
    centred = content_vectors - jnp.mean(content_vectors, axis=axis, keepdims=True)
    spread = jnp.mean(centred * centred, axis=axis, keepdims=True)
    return centred * lax.rsqrt(spread + EPSILON) * gain


def gather_blocks(block):
    device_count = lax.axis_size("dap")
    copies = jnp.broadcast_to(block[None], (device_count,) + block.shape)
    return lax.all_to_all(copies, "dap", split_axis=0, concat_axis=0, tiled=True)


def triangle(
    pair_now, gain_in, proj_weight, gate_weight, gain_mid, final_weight, amino_presence, incoming
):
    hidden = TRI_HID
    row_count = pair_now.shape[0]
    my_index = lax.axis_index("dap")
    standardized_source = standardize_features(pair_now, gain_in, -1).astype(jnp.bfloat16)
    projected = jnp.einsum(
        "rkd,de->erk", standardized_source, proj_weight, preferred_element_type=jnp.float32
    )
    res_float = amino_presence.astype(jnp.float32)
    own_rows = lax.dynamic_slice_in_dim(res_float, my_index * row_count, row_count)
    pair_mask = own_rows[:, None] * res_float[None, :]
    left_side = (
        jax.nn.sigmoid(projected[hidden : 2 * hidden]) * projected[:hidden] * pair_mask[None]
    ).astype(jnp.bfloat16)
    right_side = (
        jax.nn.sigmoid(projected[3 * hidden :])
        * projected[2 * hidden : 3 * hidden]
        * pair_mask[None]
    ).astype(jnp.bfloat16)
    gating = jax.nn.sigmoid(
        jnp.dot(standardized_source, gate_weight, preferred_element_type=jnp.float32)
    )
    device_count = lax.axis_size("dap")
    per_device = hidden // device_count
    both = jnp.stack(
        [
            left_side.reshape(device_count, per_device, row_count, -1),
            right_side.reshape(device_count, per_device, row_count, -1),
        ],
        axis=1,
    )
    both = lax.all_to_all(both, "dap", split_axis=0, concat_axis=0, tiled=True)
    both = jnp.moveaxis(both, 0, 2).reshape(2, per_device, device_count * row_count, -1)
    left_chan, right_chan = both[0], both[1]
    if incoming:
        product = jnp.einsum(
            "cki,ckj->cij", left_chan, right_chan, preferred_element_type=jnp.float32
        )
    else:
        product = jnp.einsum(
            "cik,cjk->cij", left_chan, right_chan, preferred_element_type=jnp.float32
        )
    product = product.astype(jnp.bfloat16)
    returned = lax.all_to_all(product, "dap", split_axis=1, concat_axis=0, tiled=True)
    product_normed = standardize_features(
        returned.astype(jnp.float32), gain_mid[:, None, None], 0
    ).astype(jnp.bfloat16)
    update = jnp.einsum(
        "crj,cd->rjd", product_normed, final_weight, preferred_element_type=jnp.float32
    )
    return pair_now + update * gating


def shards(
    homolog_stack,
    couple_tensor,
    homolog_presence,
    amino_presence,
    horizontal_standard_factor,
    horizontal_asking_matrix,
    horizontal_lookup_triple,
    horizontal_final_matrix,
    couple_offset_factor,
    couple_offset_matrix,
    vertical_standard_factor,
    vertical_asking_matrix,
    vertical_lookup_triple,
    vertical_final_matrix,
    tensor_average_factor,
    tensor_average_mapping,
    tensor_average_final,
    trio_entry_factors,
    trio_flank_mappings,
    trio_final_switches,
    trio_multiplied_factors,
    trio_final_matrices,
):
    nested_function = FOCUS_NUMBER * PER_FOCUS_WIDTH
    scaling = 1.0 / math.sqrt(PER_FOCUS_WIDTH)
    strand_portion = homolog_stack.shape[0]
    amino_total = homolog_stack.shape[1]
    row_count = couple_tensor.shape[0]
    pair_normed = standardize_features(couple_tensor, couple_offset_factor, -1).astype(jnp.bfloat16)
    bias_local = jnp.einsum(
        "rjc,ch->hrj", pair_normed, couple_offset_matrix, preferred_element_type=jnp.float32
    ).astype(jnp.bfloat16)
    standardized_source = standardize_features(
        homolog_stack, horizontal_standard_factor, -1
    ).astype(jnp.bfloat16)
    shaped = (strand_portion, amino_total, FOCUS_NUMBER, PER_FOCUS_WIDTH)
    queries = (
        (
            jnp.dot(
                standardized_source, horizontal_asking_matrix, preferred_element_type=jnp.float32
            )
            * scaling
        )
        .astype(jnp.bfloat16)
        .reshape(shaped)
    )
    others = jnp.dot(
        standardized_source, horizontal_lookup_triple, preferred_element_type=jnp.float32
    )
    keys_all = others[..., :nested_function].astype(jnp.bfloat16).reshape(shaped)
    content_entire = (
        others[..., nested_function : 2 * nested_function].astype(jnp.bfloat16).reshape(shaped)
    )
    sigmoid_switches = jax.nn.sigmoid(others[..., 2 * nested_function :])
    mask_penalty = MASK_PENALTY_SCALE * (homolog_presence.astype(jnp.float32) - 1.0)

    def attend(bias_piece):
        query_rows = bias_piece.shape[1]
        scores = jnp.einsum(
            "sihc,sjhc->shij", queries, keys_all, preferred_element_type=jnp.float32
        )
        scores = scores + bias_piece.astype(jnp.float32)[None] + mask_penalty[:, None, None, :]
        softmax_probabilities = jax.nn.softmax(scores, axis=-1).astype(jnp.bfloat16)
        mixed = jnp.einsum(
            "shij,sjhc->sihc",
            softmax_probabilities,
            content_entire,
            preferred_element_type=jnp.float32,
        )
        return mixed.reshape(strand_portion, query_rows, nested_function)

    bias_whole = jnp.moveaxis(gather_blocks(bias_local), 0, 1).reshape(
        FOCUS_NUMBER, amino_total, amino_total
    )
    block_rows = math.gcd(amino_total, 256)

    def one_block(block_index):
        return attend(bias_whole)

    blocks = lax.map(one_block, jnp.arange(amino_total // block_rows, dtype=jnp.int32))
    focused_content = jnp.moveaxis(blocks, 0, 1).reshape(
        strand_portion, amino_total, nested_function
    )
    homolog_stack_horizontal = homolog_stack + jnp.dot(
        (focused_content * sigmoid_switches).astype(jnp.bfloat16),
        horizontal_final_matrix,
        preferred_element_type=jnp.float32,
    )
    travelling = jnp.concatenate(
        [
            homolog_stack_horizontal.astype(jnp.bfloat16),
            jnp.broadcast_to(
                homolog_presence.astype(jnp.bfloat16)[..., None],
                (strand_portion, amino_total, 128),
            ),
        ],
        axis=-1,
    )
    arrived = lax.all_to_all(travelling, "dap", split_axis=1, concat_axis=0, tiled=True)
    column_view = arrived[..., :nested_function].astype(jnp.float32)
    col_mask = arrived[..., nested_function].astype(jnp.float32)
    seq_total = column_view.shape[0]
    col_shape = (seq_total, row_count, FOCUS_NUMBER, PER_FOCUS_WIDTH)
    standardized_source = standardize_features(column_view, vertical_standard_factor, -1).astype(
        jnp.bfloat16
    )
    col_queries = (
        (
            jnp.dot(standardized_source, vertical_asking_matrix, preferred_element_type=jnp.float32)
            * scaling
        )
        .astype(jnp.bfloat16)
        .reshape(col_shape)
    )
    col_others = jnp.dot(
        standardized_source, vertical_lookup_triple, preferred_element_type=jnp.float32
    )
    col_keys = col_others[..., :nested_function].astype(jnp.bfloat16).reshape(col_shape)
    col_values = (
        col_others[..., nested_function : 2 * nested_function]
        .astype(jnp.bfloat16)
        .reshape(col_shape)
    )
    col_gates = jax.nn.sigmoid(col_others[..., 2 * nested_function :])
    col_penalty = MASK_PENALTY_SCALE * (col_mask - 1.0)
    scores = jnp.einsum(
        "sihc,tihc->ihst", col_queries, col_keys, preferred_element_type=jnp.float32
    )
    scores = scores + jnp.transpose(col_penalty)[:, None, None, :]
    softmax_probabilities = jax.nn.softmax(scores, axis=-1).astype(jnp.bfloat16)
    col_mixed = jnp.einsum(
        "uovg,guox->vuox", softmax_probabilities, col_values, preferred_element_type=jnp.float32
    ).reshape(seq_total, row_count, nested_function)
    alignment_after_columns = column_view + jnp.dot(
        (col_mixed * col_gates).astype(jnp.bfloat16),
        vertical_final_matrix,
        preferred_element_type=jnp.float32,
    )
    standardized_source = standardize_features(
        alignment_after_columns, tensor_average_factor, -1
    ).astype(jnp.bfloat16)
    halves = jnp.dot(
        standardized_source, tensor_average_mapping, preferred_element_type=jnp.float32
    )
    left_proj = (halves[..., :TENSOR_HIDDEN] * col_mask[..., None]).astype(jnp.bfloat16)
    right_proj = (halves[..., TENSOR_HIDDEN:] * col_mask[..., None]).astype(jnp.bfloat16)
    block = jnp.concatenate(
        [right_proj, col_mask.astype(jnp.bfloat16)[..., None]], axis=-1
    )
    block = jnp.transpose(block, (1, 2, 0))
    whole = gather_blocks(block).reshape(amino_total, TENSOR_HIDDEN + 1, seq_total)
    right_whole = jnp.transpose(whole[:, :TENSOR_HIDDEN], (2, 0, 1))
    mask_whole = jnp.transpose(whole[:, TENSOR_HIDDEN])
    outer = jnp.einsum("sra,sjb->rjab", left_proj, right_whole, preferred_element_type=jnp.float32)
    outer = outer.astype(jnp.bfloat16).reshape(
        row_count, amino_total, TENSOR_HIDDEN * TENSOR_HIDDEN
    )
    counts = jnp.dot(
        jnp.transpose(col_mask), mask_whole.astype(jnp.float32), precision=lax.Precision.HIGHEST
    )
    product = (
        jnp.dot(outer, tensor_average_final, preferred_element_type=jnp.float32)
        / jnp.maximum(counts, 1.0)[..., None]
    )
    pair_one = couple_tensor + product
    pair_two = triangle(
        pair_one,
        trio_entry_factors[0],
        trio_flank_mappings[0],
        trio_final_switches[0],
        trio_multiplied_factors[0],
        trio_final_matrices[0],
        amino_presence,
        False,
    )
    pair_after_incoming = triangle(
        pair_two,
        trio_entry_factors[1],
        trio_flank_mappings[1],
        trio_final_switches[1],
        trio_multiplied_factors[1],
        trio_final_matrices[1],
        amino_presence,
        True,
    )
    return (alignment_after_columns, pair_after_incoming)


def normed_rows(x, gain):
    centred = x - jnp.mean(x, axis=-1, keepdims=True)
    spread = jnp.mean(centred * centred, axis=-1, keepdims=True)
    return centred * lax.rsqrt(spread + EPSILON) * gain


def dot_nn(a, b):
    return lax.dot_general(a, b, (((1,), (0,)), ((), ())), preferred_element_type=jnp.float32)


def dot_nt(a, b):
    return lax.dot_general(a, b, (((1,), (1,)), ((), ())), preferred_element_type=jnp.float32)


def dot_tn(a, b):
    return lax.dot_general(a, b, (((0,), (0,)), ((), ())), preferred_element_type=jnp.float32)


def lane_iota(shape):
    return lax.broadcasted_iota(jnp.int32, shape, len(shape) - 1)


def vmem_call(body, outs, scratch=(), count=0, later=0, away=(), grant=20 << 20):
    whole = pl.BlockSpec(memory_space=pltpu.VMEM)
    there = pl.BlockSpec(memory_space=pl.ANY)
    hbm = pl.BlockSpec(memory_space=pltpu.HBM)

    def reader(*refs):
        body(*refs[:count], *refs[count + later :])

    return pl.pallas_call(
        reader,
        out_shape=outs,
        in_specs=[hbm if k in away else whole for k in range(count)] + [there] * later,
        out_specs=jax.tree.map(lambda _: whole, outs),
        scratch_shapes=list(scratch),
        compiler_params=pltpu.CompilerParams(vmem_limit_bytes=grant),
    )


ROW_GAIN, COLUMN_GAIN, MEAN_GAIN, ENTRY_GAINS, MID_GAINS, PRESENCE = range(6)


def bias_body(pair_at, gain_at, weight_at, present_at, out_ref, near_ref, pair, gain, weight, present, sems):
    moves = [
        pltpu.make_async_copy(there, here, sems.at[k])
        for k, (there, here) in enumerate(
            ((pair_at, pair), (gain_at, gain), (weight_at, weight), (present_at, present))
        )
    ]
    for move in moves:
        move.start()
    for move in moves:
        move.wait()
    near_ref[0] = pair[...].astype(jnp.bfloat16)
    normed = normed_rows(pair[...], gain[...]).astype(jnp.bfloat16)
    bias = dot_nt(weight[...], normed)
    here = present[...].astype(jnp.float32)
    mask_row = jnp.concatenate([here[0:1], here[1:2]], axis=1)
    fill = jnp.zeros((out_ref.shape[1] - bias.shape[0] - 1, bias.shape[1]), jnp.float32)
    block = jnp.concatenate([bias, mask_row, fill], axis=0).astype(jnp.bfloat16)
    out_ref[...] = jnp.broadcast_to(block[None], out_ref.shape)


def put_parts(ref, value):
    lanes = ref.shape[2]
    for part in range(ref.shape[0]):
        ref[part] = value[:, part * lanes : (part + 1) * lanes]


def rows_of(ref, rows):
    return jnp.concatenate([ref[part, rows, :] for part in range(ref.shape[0])], axis=1)


def project_body(x_ref, small_ref, ask_ref, look_ref, q_ref, k_ref, v_ref, g_ref):
    width = ask_ref.shape[1]
    normed = normed_rows(x_ref[...], small_ref[ROW_GAIN : ROW_GAIN + 1]).astype(jnp.bfloat16)
    scaling = 1.0 / math.sqrt(PER_FOCUS_WIDTH)
    q = (dot_nn(normed, ask_ref[...]) * scaling).astype(jnp.bfloat16).astype(jnp.float32)
    put_parts(q_ref, q)
    others = dot_nn(normed, look_ref[...])
    k_ref[...] = others[:, :width].astype(jnp.bfloat16)
    v_ref[...] = others[:, width : 2 * width].astype(jnp.bfloat16)
    put_parts(g_ref, jax.nn.sigmoid(others[:, 2 * width :]))


def head_spread(q):
    head_of = lane_iota(q.shape) // PER_FOCUS_WIDTH
    return jnp.concatenate(
        [jnp.where(head_of == h, q, 0.0) for h in range(FOCUS_NUMBER)], axis=0
    ).astype(jnp.bfloat16)


def attend_heads(q, k, v, offset):
    scores = dot_nt(head_spread(q), k) + offset
    scores = scores - jnp.max(scores, axis=-1, keepdims=True)
    raised = jnp.exp(scores)
    shares = (raised / jnp.sum(raised, axis=-1, keepdims=True)).astype(jnp.bfloat16)
    mixed = dot_nn(shares, v)
    rows = q.shape[0]
    head_of = lane_iota(q.shape) // PER_FOCUS_WIDTH
    total = jnp.where(head_of == 0, mixed[:rows], 0.0)
    for h in range(1, FOCUS_NUMBER):
        total = jnp.where(head_of == h, mixed[h * rows : (h + 1) * rows], total)
    return total


def row_body(blk_ref, x_ref, q_ref, k_ref, v_ref, g_ref, final_ref, out_ref, wide, send, x_parts):
    devices = blk_ref.shape[0]
    put_parts(x_parts, x_ref[...])
    per_block = blk_ref.shape[1]
    half = wide.shape[1] // 2
    per_seq = 2 * devices
    wide[...] = blk_ref[...].astype(jnp.float32).reshape(wide.shape)
    mine = wide[pl.ds(lax.axis_index("dap") * per_block + FOCUS_NUMBER, 1), :]
    penalty = MASK_PENALTY_SCALE * (mine - 1.0)
    heads = [wide[pl.ds(h, devices, stride=per_block), :] for h in range(FOCUS_NUMBER)]
    for s in range(2):
        keys = k_ref[s * per_seq : (s + 1) * per_seq, :]
        values = v_ref[s * per_seq : (s + 1) * per_seq, :]
        for r in range(2):
            rows = pl.ds(s * per_seq + r, devices, stride=2)
            bias = jnp.concatenate([b[:, r * half : (r + 1) * half] for b in heads], axis=0)
            mixed = attend_heads(rows_of(q_ref, rows), keys, values, bias + penalty[:, s * half : (s + 1) * half])
            y = (mixed * rows_of(g_ref, rows)).astype(jnp.bfloat16)
            updated = rows_of(x_parts, rows) + dot_nn(y, final_ref[...])
            for part in range(updated.shape[1] // (2 * half)):
                to = pl.ds((s * 2 + r) * 2 + part, devices, stride=out_ref.shape[1])
                send[to, :] = updated[:, part * 2 * half : (part + 1) * 2 * half]
    out_ref[...] = send[...].reshape(out_ref.shape).astype(jnp.bfloat16)


def mask_block(blk_ref, wide):
    wide[...] = blk_ref[...].astype(jnp.float32).reshape(wide.shape)
    rows = pl.ds(FOCUS_NUMBER, blk_ref.shape[0], stride=blk_ref.shape[1])
    return wide[rows, :].astype(jnp.bfloat16)


def column_body(
    arrived_ref, blk_ref, small_ref, ask_ref, look_ref, final_ref, map_ref,
    msa_ref, opm_ref, wide, wide_blk, x_all, msa,
):
    devices = arrived_ref.shape[0]
    width = ask_ref.shape[1]
    lanes = wide.shape[1]
    half = lanes // 2
    seqs = 2 * devices
    me = lax.axis_index("dap")
    wide[...] = arrived_ref[...].astype(jnp.float32).reshape(wide.shape)
    for r in range(2):
        for s in range(2):
            base = (s * 2 + r) * 2
            at = (r * 2 + s) * devices
            for part in range(2):
                x_all[at : at + devices, part * lanes : (part + 1) * lanes] = wide[
                    pl.ds(base + part, devices, stride=8), :
                ]
    mask_lanes = mask_block(blk_ref, wide_blk)
    row = lax.broadcasted_iota(jnp.int32, (8, lanes), 0)
    wanted = (row % 2) * half + 2 * me + row // 2
    pick = jnp.where((lane_iota((8, lanes)) == wanted) & (row < 4), 1.0, 0.0).astype(jnp.bfloat16)
    picked = dot_nt(pick, mask_lanes)
    present = [
        jnp.concatenate([picked[2 * r : 2 * r + 1], picked[2 * r + 1 : 2 * r + 2]], axis=1)
        for r in range(2)
    ]
    x = x_all[...]
    normed = normed_rows(x, small_ref[COLUMN_GAIN : COLUMN_GAIN + 1]).astype(jnp.bfloat16)
    scaling = 1.0 / math.sqrt(PER_FOCUS_WIDTH)
    q = (dot_nn(normed, ask_ref[...]) * scaling).astype(jnp.bfloat16).astype(jnp.float32)
    others = dot_nn(normed, look_ref[...])
    keys = others[:, :width].astype(jnp.bfloat16)
    values = others[:, width : 2 * width].astype(jnp.bfloat16)
    gates = jax.nn.sigmoid(others[:, 2 * width :])
    mixed = jnp.concatenate(
        [
            attend_heads(
                q[r * seqs : (r + 1) * seqs],
                keys[r * seqs : (r + 1) * seqs],
                values[r * seqs : (r + 1) * seqs],
                MASK_PENALTY_SCALE * (present[r] - 1.0),
            )
            for r in range(2)
        ],
        axis=0,
    )
    updated = x + dot_nn((mixed * gates).astype(jnp.bfloat16), final_ref[...])
    for r in range(2):
        for s in range(2):
            at = (r * 2 + s) * devices
            for part in range(2):
                msa[r * 2 + part, pl.ds(s, devices, stride=2), :] = updated[
                    at : at + devices, part * lanes : (part + 1) * lanes
                ]
    for part in range(4):
        msa_ref[:, part * lanes : (part + 1) * lanes] = msa[part]
    normed = normed_rows(updated, small_ref[MEAN_GAIN : MEAN_GAIN + 1]).astype(jnp.bfloat16)
    sides = [
        dot_nt(map_ref[...], normed[r * seqs : (r + 1) * seqs]) * present[r] for r in range(2)
    ]
    block = jnp.concatenate(sides, axis=1).astype(jnp.bfloat16)
    opm_ref[...] = jnp.broadcast_to(block[None], opm_ref.shape)


def gated(projected, q_at, g_at, width):
    return jax.nn.sigmoid(projected[:, g_at : g_at + width]) * projected[:, q_at : q_at + width]


def presence_down(amino_row, half, lanes):
    square = lax.broadcasted_iota(jnp.int32, (half, half), 0) == lane_iota((half, half))
    diagonal = jnp.where(square, amino_row.astype(jnp.float32), 0.0).astype(jnp.bfloat16)
    return dot_nn(diagonal, jnp.ones((half, lanes), jnp.bfloat16))


def opm_body(steps, own_ref, oth_ref, *refs):
    couples, refs = refs[:steps], refs[steps:]
    (
        blk_ref, fin_ref, small_ref, flank_ref, switch_ref,
        pair_one_ref, left_ref, gate_ref, right_ref,
        order, order16, outer, counts, mkeys, wide_blk,
    ) = refs
    chips, lanes, channels = pair_one_ref.shape
    hidden = outer.shape[2]
    half = lanes // 2
    me = lax.axis_index("dap")
    parity = lax.rem(me, 2)
    my_chip = me // 2
    for k in range(steps):
        for h in range(chips // steps):
            pair_one_ref[my_chip ^ (h * steps + k)] = couples[k][h].astype(jnp.float32)
    rows = (chips * hidden, lanes)
    order16[parity] = own_ref[:, hidden:, :].astype(jnp.float32).reshape(rows)
    order16[1 - parity] = oth_ref[:, hidden:, :].astype(jnp.float32).reshape(rows)
    for b in range(hidden):
        for p in range(2):
            rows = order16[p, pl.ds(b, chips, stride=hidden), :]
            for r in range(2):
                order[pl.ds(b * half + 2 * p + r, chips, stride=4), :] = (
                    pltpu.roll(rows, half, 1) if r else rows
                )
    rights = order[...].astype(jnp.bfloat16)[:, :half]
    for r in range(2):
        lhs = own_ref[:, :hidden, :].reshape(chips * hidden, lanes)[:, r * half : (r + 1) * half]
        outer[r] = dot_nt(lhs, rights).astype(jnp.bfloat16).reshape(outer.shape[1:])
    mask_rows = mask_block(blk_ref, wide_blk)
    total = jnp.zeros((half, lanes), jnp.float32)
    for s in range(2):
        part = mask_rows[:, s * half : (s + 1) * half]
        total = total + dot_tn(part, jnp.concatenate([part, part], axis=1))
    counts[...] = 1.0 / jnp.maximum(total, 1.0)
    mkeys[...] = presence_down(small_ref[PRESENCE : PRESENCE + 1, :half], half, lanes)
    gain = small_ref[ENTRY_GAINS : ENTRY_GAINS + 1, :channels]
    low = lane_iota((channels, lanes)) < half
    low_row = lane_iota((1, lanes)) < half
    group = 4

    @pl.loop(0, chips // group)
    def _(block):
        pairs, keeps = [], []
        for c in range(group):
            chip = block * group + c
            sides = []
            for r in range(2):
                strip = outer[r, chip]
                sides.append(
                    jnp.concatenate(
                        [strip[:, g * lanes : (g + 1) * lanes] for g in range(hidden // 2)], axis=0
                    )
                )
            res = dot_nn(fin_ref[...], jnp.concatenate(sides, axis=1))
            a0, a1 = res[:channels, :lanes], res[:channels, lanes:]
            b0, b1 = res[channels:, :lanes], res[channels:, lanes:]
            turned = jnp.where(low, a0, b1) + pltpu.roll(jnp.where(low, a1, b0), half, 1)
            i0 = 4 * chip + 2 * parity
            share = jnp.where(low_row, counts[pl.ds(i0, 1), :], counts[pl.ds(i0 + 1, 1), :])
            pairs.append(jnp.transpose(turned * share) + pair_one_ref[chip])
            for r in range(2):
                keeps.append(mkeys[...] * mkeys[pl.ds(i0 + r, 1), :])
        pair = jnp.concatenate(pairs, axis=0)
        keep = jnp.concatenate(keeps, axis=0)
        normed = normed_rows(pair, gain).astype(jnp.bfloat16)
        projected = dot_nn(normed, flank_ref[0])
        left = gated(projected, 0, channels, channels) * keep
        right = gated(projected, 2 * channels, 3 * channels, channels) * keep
        gate = jax.nn.sigmoid(dot_nn(normed, switch_ref[0]))
        for c in range(group):
            chip = block * group + c
            rows = slice(c * lanes, (c + 1) * lanes)
            pair_one_ref[chip] = pair[rows]
            gate_ref[chip] = gate[rows]
            left_ref[chip] = jnp.transpose(left[rows])
            right_ref[chip] = jnp.transpose(right[rows]).astype(jnp.bfloat16)


def outgoing_body(
    pair_one_ref, left_ref, gate_ref, own_ref, oth_ref, small_ref, final_ref, flank_ref,
    two_ref, send_ref,
    sides, prods, mkeys, pair_two, rows_out, cols,
):
    chips, channels, lanes = own_ref.shape
    half = lanes // 2
    me = lax.axis_index("dap")
    parity = lax.rem(me, 2)
    my_chip = me // 2
    flag = jnp.broadcast_to(parity, (1, 1)) == 0

    @pl.loop(0, chips)
    def _(chip):
        own = own_ref[chip].astype(jnp.float32)
        oth = oth_ref[chip].astype(jnp.float32)
        rows = pl.ds(pl.multiple_of(chip * channels, channels), channels)
        sides[0, rows, :] = jnp.where(flag, own, oth)
        sides[1, rows, :] = jnp.where(flag, oth, own)

    low = lane_iota((chips, lanes)) < half

    per_step = 32

    @pl.loop(0, channels // per_step)
    def _(octet):
        results = []
        for c in range(per_step):
            at = pl.ds(octet * per_step + c, chips, stride=channels)
            lhs = left_ref[at, :].astype(jnp.bfloat16)
            pieces = [[], []]
            for p in range(2):
                rows = sides[p, at, :]
                turned = pltpu.roll(rows, half, 1)
                pieces[0] += [jnp.where(low, rows, 0.0), jnp.where(low, turned, 0.0)]
                pieces[1] += [jnp.where(low, 0.0, turned), jnp.where(low, 0.0, rows)]
            rhs = jnp.concatenate(pieces[0] + pieces[1], axis=0).astype(jnp.bfloat16)
            results.append(dot_nt(lhs, rhs))
        for c in range(per_step):
            to = pl.ds(pl.multiple_of((octet * per_step + c) * chips, chips), chips)
            prods[to, :] = results[c].astype(jnp.bfloat16).astype(jnp.float32)

    mkeys[...] = presence_down(small_ref[PRESENCE : PRESENCE + 1, :half], half, channels)
    gain_mid = small_ref[MID_GAINS : MID_GAINS + 1, :channels]
    gain_mid = jnp.transpose(jnp.broadcast_to(gain_mid, (channels, channels)))
    final_t = jnp.transpose(final_ref[0].astype(jnp.float32)).astype(jnp.bfloat16)
    gain = small_ref[ENTRY_GAINS : ENTRY_GAINS + 1, channels : 2 * channels]
    flank_right = flank_ref[1, :, 2 * channels :]
    flank_left = flank_ref[1, :, : 2 * channels]
    octet = pl.multiple_of(8 * (my_chip // 2), 8)
    group = 4
    for block in range(chips // group):
        changed = []
        for c in range(group):
            x = prods[pl.ds(block * group + c, channels, stride=chips), :]
            centred = x - jnp.mean(x, axis=0, keepdims=True)
            spread = jnp.mean(centred * centred, axis=0, keepdims=True)
            changed.append((centred * lax.rsqrt(spread + EPSILON) * gain_mid).astype(jnp.bfloat16))
        changed = dot_nn(final_t, jnp.concatenate(changed, axis=1))
        for c in range(group):
            part = jnp.transpose(changed[:, c * lanes : (c + 1) * lanes])
            for k in range(8):
                r, p, rj = k // 4, (k // 2) % 2, k % 2
                rows_out[c, pl.ds(r * half + 2 * p + rj, chips, stride=4), :] = part[
                    k * chips : (k + 1) * chips
                ]
        twos, keeps = [], []
        for c in range(group):
            chip = block * group + c
            two = pair_one_ref[chip] + rows_out[c] * gate_ref[chip]
            twos.append(two)
            for r in range(2):
                keeps.append(mkeys[pl.ds(4 * chip + 2 * parity + r, 1), :])
        two = jnp.concatenate(twos, axis=0)
        full = normed_rows(two, gain)
        normed = full.astype(jnp.bfloat16)
        keep = jnp.concatenate([mkeys[...] * m for m in keeps], axis=0)
        going = (gated(dot_nn(normed, flank_right), 0, channels, channels) * keep).astype(jnp.bfloat16)
        cols[...] = full
        few = jnp.concatenate(
            [cols[pl.ds(k * half + octet, 8), :] for k in range(2 * group)], axis=0
        ).astype(jnp.bfloat16)
        mine = mkeys[pl.ds(octet, 8), :]
        keep = jnp.concatenate([mine * m for m in keeps], axis=0)
        few = (gated(dot_nn(few, flank_left), 0, channels, channels) * keep).astype(jnp.bfloat16)
        for c in range(group):
            chip = block * group + c
            pair_two[chip] = twos[c]
            send_ref[chip, :lanes, :] = going[c * lanes : (c + 1) * lanes]
            send_ref[chip, lanes:, :] = few[c * 16 : (c + 1) * 16]
    two_ref[...] = pair_two[my_chip]


def incoming_body(
    own_ref, oth_ref, two_ref, couple_ref, small_ref, switch_ref, final_ref,
    out_ref,
):
    chips, _, channels = own_ref.shape
    lanes2 = out_ref.shape[0]
    half = lanes2 // 2
    me = lax.axis_index("dap")
    gain_mid = small_ref[MID_GAINS : MID_GAINS + 1, channels : 2 * channels]
    gain = small_ref[ENTRY_GAINS : ENTRY_GAINS + 1, channels : 2 * channels]
    first = 4 * lax.rem(me // 2, 2) + 2 * lax.rem(me, 2)
    row = lax.broadcasted_iota(jnp.int32, (8, channels), 0)
    totals = tuple(jnp.zeros((half, channels), jnp.float32) for _ in range(2))
    for side_ref in (own_ref, oth_ref):

        def step(chip, totals, side_ref=side_ref):
            totals = list(totals)
            tail = side_ref[chip, lanes2:, :].astype(jnp.float32)
            for k in range(2):
                there = side_ref[chip, k * half : (k + 1) * half, :].astype(jnp.float32)
                for i in range(2):
                    picked = jnp.where(row == first + i, tail[8 * k : 8 * k + 8], 0.0)
                    one = jnp.sum(picked, axis=0, keepdims=True)
                    totals[i] = totals[i] + one * there
            return tuple(totals)

        totals = lax.fori_loop(0, chips, step, totals)
    prod = jnp.concatenate(totals, axis=0).astype(jnp.bfloat16).astype(jnp.float32)
    changed = dot_nn(normed_rows(prod, gain_mid).astype(jnp.bfloat16), final_ref[1])
    two = two_ref[...]
    normed = normed_rows(two, gain).astype(jnp.bfloat16)
    gate = jax.nn.sigmoid(dot_nn(normed, switch_ref[1]))
    couple = couple_ref[...]
    lost = couple - couple.astype(jnp.bfloat16).astype(jnp.float32)
    out_ref[...] = two + lost + changed * gate


def gather_by_steps(block, chips):
    bits = chips.bit_length() - 1
    steps = 1 << (bits // 2)
    devices = 2 * chips

    def fetch(value, apart):
        return lax.ppermute(value, "dap", [(d, d ^ (2 * apart)) for d in range(devices)])

    parts = [fetch(block, h * steps) for h in range(1, chips // steps)]
    near = jnp.concatenate([block] + parts, axis=0)
    return near, [fetch(near, k) for k in range(1, steps)]


def paired_shards(
    homolog_stack,
    couple_tensor,
    homolog_presence,
    amino_presence,
    horizontal_standard_factor,
    horizontal_asking_matrix,
    horizontal_lookup_triple,
    horizontal_final_matrix,
    couple_offset_factor,
    couple_offset_matrix,
    vertical_standard_factor,
    vertical_asking_matrix,
    vertical_lookup_triple,
    vertical_final_matrix,
    tensor_average_factor,
    tensor_average_mapping,
    tensor_average_final,
    trio_entry_factors,
    trio_flank_mappings,
    trio_final_switches,
    trio_multiplied_factors,
    trio_final_matrices,
):
    devices = lax.axis_size("dap")
    chips = devices // 2
    strands, aminos, features = homolog_stack.shape
    rows, _, channels = couple_tensor.shape
    lanes = rows * aminos
    heads = FOCUS_NUMBER
    hidden = TENSOR_HIDDEN
    f32, bf16 = jnp.float32, jnp.bfloat16
    shape = jax.ShapeDtypeStruct
    same_parity = [[2 * chip + p for chip in range(chips)] for p in range(2)]
    swap = [(d, d ^ 1) for d in range(devices)]

    def line(v):
        return v.reshape(1, -1)

    couple = couple_tensor.reshape(lanes, channels)
    x = homolog_stack.reshape(strands * aminos, features)
    block, near = vmem_call(
        bias_body,
        (shape((devices, 16, lanes), bf16), shape((1, lanes, channels), bf16)),
        scratch=[
            pltpu.VMEM((lanes, channels), f32),
            pltpu.VMEM((1, channels), f32),
            pltpu.VMEM((heads, channels), bf16),
            pltpu.VMEM((strands, aminos), jnp.int32),
            pltpu.SemaphoreType.DMA((4,)),
        ],
        count=4,
        away=range(4),
        grant=60 << 20,
    )(couple, line(couple_offset_factor), couple_offset_matrix.T, homolog_presence)
    blocks = lax.all_to_all(block, "dap", split_axis=0, concat_axis=0, tiled=True)
    small = jnp.concatenate(
        [
            line(horizontal_standard_factor),
            line(vertical_standard_factor),
            line(tensor_average_factor),
            line(trio_entry_factors),
            line(trio_multiplied_factors),
            jnp.pad(line(amino_presence.astype(f32)), ((0, 0), (0, features - aminos))),
            jnp.zeros((2, features), f32),
        ],
        axis=0,
    )
    final = jnp.transpose(
        tensor_average_final.reshape(hidden, hidden // 2, 2, channels), (2, 3, 1, 0)
    ).reshape(2 * channels, hidden * hidden // 2)
    q, k, v, g = vmem_call(
        project_body,
        (
            shape((features // lanes, lanes, lanes), f32),
            shape((lanes, features), bf16),
            shape((lanes, features), bf16),
            shape((features // lanes, lanes, lanes), f32),
        ),
        count=4,
    )(x, small, horizontal_asking_matrix, horizontal_lookup_triple)
    near, fars = gather_by_steps(near, chips)
    couples = [near, *fars]
    sent = vmem_call(
        row_body,
        shape((devices, 8, lanes), bf16),
        scratch=[
            pltpu.VMEM((devices * 16, lanes), f32),
            pltpu.VMEM((devices * 8, lanes), f32),
            pltpu.VMEM((features // lanes, lanes, lanes), f32),
        ],
        count=7,
    )(blocks, x, q, k, v, g, horizontal_final_matrix)
    arrived = lax.all_to_all(sent, "dap", split_axis=0, concat_axis=0, tiled=True)
    msa, opm = vmem_call(
        column_body,
        (shape((devices * strands, rows * features), f32), shape((chips, 2 * hidden, lanes), bf16)),
        scratch=[
            pltpu.VMEM((devices * 8, lanes), f32),
            pltpu.VMEM((devices * 16, lanes), f32),
            pltpu.VMEM((lanes, features), f32),
            pltpu.VMEM((4, devices * strands, lanes), f32),
        ],
        count=7,
        later=1,
    )(
        arrived,
        blocks,
        small,
        vertical_asking_matrix,
        vertical_lookup_triple,
        vertical_final_matrix,
        tensor_average_mapping.T,
        final,
    )
    opm_own = lax.all_to_all(
        opm, "dap", split_axis=0, concat_axis=0, tiled=True, axis_index_groups=same_parity
    )
    opm_oth = lax.ppermute(opm_own, "dap", swap)
    stack = (chips, lanes, channels)
    pair_one, left, gate, right_own = vmem_call(
        functools.partial(opm_body, len(couples)),
        (shape(stack, f32), shape(stack, f32), shape(stack, f32), shape(stack, bf16)),
        scratch=[
            pltpu.VMEM((hidden * aminos, lanes), f32),
            pltpu.VMEM((2, chips * hidden, lanes), f32),
            pltpu.VMEM((2, chips, hidden, hidden * aminos), bf16),
            pltpu.VMEM((aminos, lanes), f32),
            pltpu.VMEM((aminos, channels), f32),
            pltpu.VMEM((devices * 16, lanes), f32),
        ],
        count=len(couples) + 7,
    )(
        opm_own,
        opm_oth,
        *couples,
        blocks,
        final,
        small,
        trio_flank_mappings,
        trio_final_switches,
    )
    right_oth = lax.ppermute(right_own, "dap", swap)
    two, going = vmem_call(
        outgoing_body,
        (shape((lanes, channels), f32), shape((chips, lanes + 16, channels), bf16)),
        scratch=[
            pltpu.VMEM((2, chips * channels, lanes), f32),
            pltpu.VMEM((channels * chips, lanes), f32),
            pltpu.VMEM((aminos, channels), f32),
            pltpu.VMEM(stack, f32),
            pltpu.VMEM((4, lanes, channels), f32),
            pltpu.VMEM((4 * lanes, channels), f32),
        ],
        count=8,
    )(
        pair_one,
        left.reshape(chips * channels, lanes),
        gate,
        right_own,
        right_oth,
        small,
        trio_final_matrices,
        trio_flank_mappings,
    )
    coming = lax.ppermute(going, "dap", swap)
    pair_out = vmem_call(
        incoming_body, shape((lanes, channels), f32), count=7
    )(going, coming, two, couple, small, trio_final_switches, trio_final_matrices)
    return (
        msa.reshape(devices * strands, rows, features),
        pair_out.reshape(rows, aminos, channels),
    )


def fits_pairs(homolog_stack, couple_tensor, devices):
    strands, aminos, features = homolog_stack.shape
    rows, _, channels = couple_tensor.shape
    lanes = 128
    return (
        strands == rows == 2
        and devices % 8 == 0
        and devices & (devices - 1) == 0
        and rows * aminos == lanes == channels
        and aminos == 2 * devices
        and features == 2 * lanes
    )


def either(*arrays):
    if fits_pairs(arrays[0], arrays[1], lax.axis_size("dap")):
        return paired_shards(*arrays)
    return shards(*arrays)


def solution(mesh):
    placed = (
        P("dap", None, None),
        P("dap", None, None),
        P("dap", None),
        P(),
        P(),
        P(),
        P(),
        P(),
        P(),
        P(),
        P(),
        P(),
        P(),
        P(),
        P(),
        P(),
        P(),
        P(),
        P(),
        P(),
        P(),
        P(),
    )
    return jax.shard_map(
        either,
        mesh=mesh,
        in_specs=placed,
        out_specs=(P(None, "dap", None), P("dap", None, None)),
        check_vma=False,
    )
```

```python
import functools
import math

import jax
import jax.numpy as jnp
from jax import lax
from jax.experimental import pallas as pl
from jax.experimental.pallas import tpu as pltpu
from jax.sharding import PartitionSpec as P

FOCUS_NUMBER = 8
PER_FOCUS_WIDTH = 32
TENSOR_HIDDEN = 32
TRI_HID = 128


EPSILON = 1e-05
MASK_PENALTY_SCALE = 1000000000.0


def standardize_features(content_vectors, gain, axis):
    centred = content_vectors - jnp.mean(content_vectors, axis=axis, keepdims=True)
    spread = jnp.mean(centred * centred, axis=axis, keepdims=True)
    return centred * lax.rsqrt(spread + EPSILON) * gain


def gather_blocks(block):
    device_count = lax.axis_size("dap")
    copies = jnp.broadcast_to(block[None], (device_count,) + block.shape)
    return lax.all_to_all(copies, "dap", split_axis=0, concat_axis=0, tiled=True)


def triangle(
    pair_now, gain_in, proj_weight, gate_weight, gain_mid, final_weight, amino_presence, incoming
):
    hidden = TRI_HID
    row_count = pair_now.shape[0]
    my_index = lax.axis_index("dap")
    standardized_source = standardize_features(pair_now, gain_in, -1).astype(jnp.bfloat16)
    projected = jnp.einsum(
        "rkd,de->erk", standardized_source, proj_weight, preferred_element_type=jnp.float32
    )
    res_float = amino_presence.astype(jnp.float32)
    own_rows = lax.dynamic_slice_in_dim(res_float, my_index * row_count, row_count)
    pair_mask = own_rows[:, None] * res_float[None, :]
    left_side = (
        jax.nn.sigmoid(projected[hidden : 2 * hidden]) * projected[:hidden] * pair_mask[None]
    ).astype(jnp.bfloat16)
    right_side = (
        jax.nn.sigmoid(projected[3 * hidden :])
        * projected[2 * hidden : 3 * hidden]
        * pair_mask[None]
    ).astype(jnp.bfloat16)
    gating = jax.nn.sigmoid(
        jnp.dot(standardized_source, gate_weight, preferred_element_type=jnp.float32)
    )
    device_count = lax.axis_size("dap")
    per_device = hidden // device_count
    both = jnp.stack(
        [
            left_side.reshape(device_count, per_device, row_count, -1),
            right_side.reshape(device_count, per_device, row_count, -1),
        ],
        axis=1,
    )
    both = lax.all_to_all(both, "dap", split_axis=0, concat_axis=0, tiled=True)
    both = jnp.moveaxis(both, 0, 2).reshape(2, per_device, device_count * row_count, -1)
    left_chan, right_chan = both[0], both[1]
    if incoming:
        product = jnp.einsum(
            "cki,ckj->cij", left_chan, right_chan, preferred_element_type=jnp.float32
        )
    else:
        product = jnp.einsum(
            "cik,cjk->cij", left_chan, right_chan, preferred_element_type=jnp.float32
        )
    product = product.astype(jnp.bfloat16)
    returned = lax.all_to_all(product, "dap", split_axis=1, concat_axis=0, tiled=True)
    product_normed = standardize_features(
        returned.astype(jnp.float32), gain_mid[:, None, None], 0
    ).astype(jnp.bfloat16)
    update = jnp.einsum(
        "crj,cd->rjd", product_normed, final_weight, preferred_element_type=jnp.float32
    )
    return pair_now + update * gating


def shards(
    homolog_stack,
    couple_tensor,
    homolog_presence,
    amino_presence,
    horizontal_standard_factor,
    horizontal_asking_matrix,
    horizontal_lookup_triple,
    horizontal_final_matrix,
    couple_offset_factor,
    couple_offset_matrix,
    vertical_standard_factor,
    vertical_asking_matrix,
    vertical_lookup_triple,
    vertical_final_matrix,
    tensor_average_factor,
    tensor_average_mapping,
    tensor_average_final,
    trio_entry_factors,
    trio_flank_mappings,
    trio_final_switches,
    trio_multiplied_factors,
    trio_final_matrices,
):
    nested_function = FOCUS_NUMBER * PER_FOCUS_WIDTH
    scaling = 1.0 / math.sqrt(PER_FOCUS_WIDTH)
    strand_portion = homolog_stack.shape[0]
    amino_total = homolog_stack.shape[1]
    row_count = couple_tensor.shape[0]
    pair_normed = standardize_features(couple_tensor, couple_offset_factor, -1).astype(jnp.bfloat16)
    bias_local = jnp.einsum(
        "rjc,ch->hrj", pair_normed, couple_offset_matrix, preferred_element_type=jnp.float32
    ).astype(jnp.bfloat16)
    standardized_source = standardize_features(
        homolog_stack, horizontal_standard_factor, -1
    ).astype(jnp.bfloat16)
    shaped = (strand_portion, amino_total, FOCUS_NUMBER, PER_FOCUS_WIDTH)
    queries = (
        (
            jnp.dot(
                standardized_source, horizontal_asking_matrix, preferred_element_type=jnp.float32
            )
            * scaling
        )
        .astype(jnp.bfloat16)
        .reshape(shaped)
    )
    others = jnp.dot(
        standardized_source, horizontal_lookup_triple, preferred_element_type=jnp.float32
    )
    keys_all = others[..., :nested_function].astype(jnp.bfloat16).reshape(shaped)
    content_entire = (
        others[..., nested_function : 2 * nested_function].astype(jnp.bfloat16).reshape(shaped)
    )
    sigmoid_switches = jax.nn.sigmoid(others[..., 2 * nested_function :])
    mask_penalty = MASK_PENALTY_SCALE * (homolog_presence.astype(jnp.float32) - 1.0)

    def attend(bias_piece):
        query_rows = bias_piece.shape[1]
        scores = jnp.einsum(
            "sihc,sjhc->shij", queries, keys_all, preferred_element_type=jnp.float32
        )
        scores = scores + bias_piece.astype(jnp.float32)[None] + mask_penalty[:, None, None, :]
        softmax_probabilities = jax.nn.softmax(scores, axis=-1).astype(jnp.bfloat16)
        mixed = jnp.einsum(
            "shij,sjhc->sihc",
            softmax_probabilities,
            content_entire,
            preferred_element_type=jnp.float32,
        )
        return mixed.reshape(strand_portion, query_rows, nested_function)

    bias_whole = jnp.moveaxis(gather_blocks(bias_local), 0, 1).reshape(
        FOCUS_NUMBER, amino_total, amino_total
    )
    block_rows = math.gcd(amino_total, 256)

    def one_block(block_index):
        return attend(bias_whole)

    blocks = lax.map(one_block, jnp.arange(amino_total // block_rows, dtype=jnp.int32))
    focused_content = jnp.moveaxis(blocks, 0, 1).reshape(
        strand_portion, amino_total, nested_function
    )
    homolog_stack_horizontal = homolog_stack + jnp.dot(
        (focused_content * sigmoid_switches).astype(jnp.bfloat16),
        horizontal_final_matrix,
        preferred_element_type=jnp.float32,
    )
    travelling = jnp.concatenate(
        [
            homolog_stack_horizontal.astype(jnp.bfloat16),
            jnp.broadcast_to(
                homolog_presence.astype(jnp.bfloat16)[..., None],
                (strand_portion, amino_total, 128),
            ),
        ],
        axis=-1,
    )
    arrived = lax.all_to_all(travelling, "dap", split_axis=1, concat_axis=0, tiled=True)
    column_view = arrived[..., :nested_function].astype(jnp.float32)
    col_mask = arrived[..., nested_function].astype(jnp.float32)
    seq_total = column_view.shape[0]
    col_shape = (seq_total, row_count, FOCUS_NUMBER, PER_FOCUS_WIDTH)
    standardized_source = standardize_features(column_view, vertical_standard_factor, -1).astype(
        jnp.bfloat16
    )
    col_queries = (
        (
            jnp.dot(standardized_source, vertical_asking_matrix, preferred_element_type=jnp.float32)
            * scaling
        )
        .astype(jnp.bfloat16)
        .reshape(col_shape)
    )
    col_others = jnp.dot(
        standardized_source, vertical_lookup_triple, preferred_element_type=jnp.float32
    )
    col_keys = col_others[..., :nested_function].astype(jnp.bfloat16).reshape(col_shape)
    col_values = (
        col_others[..., nested_function : 2 * nested_function]
        .astype(jnp.bfloat16)
        .reshape(col_shape)
    )
    col_gates = jax.nn.sigmoid(col_others[..., 2 * nested_function :])
    col_penalty = MASK_PENALTY_SCALE * (col_mask - 1.0)
    scores = jnp.einsum(
        "sihc,tihc->ihst", col_queries, col_keys, preferred_element_type=jnp.float32
    )
    scores = scores + jnp.transpose(col_penalty)[:, None, None, :]
    softmax_probabilities = jax.nn.softmax(scores, axis=-1).astype(jnp.bfloat16)
    col_mixed = jnp.einsum(
        "uovg,guox->vuox", softmax_probabilities, col_values, preferred_element_type=jnp.float32
    ).reshape(seq_total, row_count, nested_function)
    alignment_after_columns = column_view + jnp.dot(
        (col_mixed * col_gates).astype(jnp.bfloat16),
        vertical_final_matrix,
        preferred_element_type=jnp.float32,
    )
    standardized_source = standardize_features(
        alignment_after_columns, tensor_average_factor, -1
    ).astype(jnp.bfloat16)
    halves = jnp.dot(
        standardized_source, tensor_average_mapping, preferred_element_type=jnp.float32
    )
    left_proj = (halves[..., :TENSOR_HIDDEN] * col_mask[..., None]).astype(jnp.bfloat16)
    right_proj = (halves[..., TENSOR_HIDDEN:] * col_mask[..., None]).astype(jnp.bfloat16)
    block = jnp.concatenate(
        [right_proj, col_mask.astype(jnp.bfloat16)[..., None]], axis=-1
    )
    block = jnp.transpose(block, (1, 2, 0))
    whole = gather_blocks(block).reshape(amino_total, TENSOR_HIDDEN + 1, seq_total)
    right_whole = jnp.transpose(whole[:, :TENSOR_HIDDEN], (2, 0, 1))
    mask_whole = jnp.transpose(whole[:, TENSOR_HIDDEN])
    outer = jnp.einsum("sra,sjb->rjab", left_proj, right_whole, preferred_element_type=jnp.float32)
    outer = outer.astype(jnp.bfloat16).reshape(
        row_count, amino_total, TENSOR_HIDDEN * TENSOR_HIDDEN
    )
    counts = jnp.dot(
        jnp.transpose(col_mask), mask_whole.astype(jnp.float32), precision=lax.Precision.HIGHEST
    )
    product = (
        jnp.dot(outer, tensor_average_final, preferred_element_type=jnp.float32)
        / jnp.maximum(counts, 1.0)[..., None]
    )
    pair_one = couple_tensor + product
    pair_two = triangle(
        pair_one,
        trio_entry_factors[0],
        trio_flank_mappings[0],
        trio_final_switches[0],
        trio_multiplied_factors[0],
        trio_final_matrices[0],
        amino_presence,
        False,
    )
    pair_after_incoming = triangle(
        pair_two,
        trio_entry_factors[1],
        trio_flank_mappings[1],
        trio_final_switches[1],
        trio_multiplied_factors[1],
        trio_final_matrices[1],
        amino_presence,
        True,
    )
    return (alignment_after_columns, pair_after_incoming)


def normed_rows(x, gain):
    centred = x - jnp.mean(x, axis=-1, keepdims=True)
    spread = jnp.mean(centred * centred, axis=-1, keepdims=True)
    return centred * lax.rsqrt(spread + EPSILON) * gain


def dot_nn(a, b):
    return lax.dot_general(a, b, (((1,), (0,)), ((), ())), preferred_element_type=jnp.float32)


def dot_nt(a, b):
    return lax.dot_general(a, b, (((1,), (1,)), ((), ())), preferred_element_type=jnp.float32)


def dot_tn(a, b):
    return lax.dot_general(a, b, (((0,), (0,)), ((), ())), preferred_element_type=jnp.float32)


def lane_iota(shape):
    return lax.broadcasted_iota(jnp.int32, shape, len(shape) - 1)


def vmem_call(body, outs, scratch=(), count=0, later=0, away=(), grant=20 << 20):
    whole = pl.BlockSpec(memory_space=pltpu.VMEM)
    there = pl.BlockSpec(memory_space=pl.ANY)
    hbm = pl.BlockSpec(memory_space=pltpu.HBM)

    def reader(*refs):
        body(*refs[:count], *refs[count + later :])

    return pl.pallas_call(
        reader,
        out_shape=outs,
        in_specs=[hbm if k in away else whole for k in range(count)] + [there] * later,
        out_specs=jax.tree.map(lambda _: whole, outs),
        scratch_shapes=list(scratch),
        compiler_params=pltpu.CompilerParams(vmem_limit_bytes=grant),
    )


ROW_GAIN, COLUMN_GAIN, MEAN_GAIN, ENTRY_GAINS, MID_GAINS, PRESENCE = range(6)


def bias_body(pair_at, gain_at, weight_at, present_at, out_ref, near_ref, pair, gain, weight, present, sems):
    moves = [
        pltpu.make_async_copy(there, here, sems.at[k])
        for k, (there, here) in enumerate(
            ((pair_at, pair), (gain_at, gain), (weight_at, weight), (present_at, present))
        )
    ]
    for move in moves:
        move.start()
    for move in moves:
        move.wait()
    near_ref[0] = pair[...].astype(jnp.bfloat16)
    normed = normed_rows(pair[...], gain[...]).astype(jnp.bfloat16)
    bias = dot_nt(weight[...], normed)
    here = present[...].astype(jnp.float32)
    mask_row = jnp.concatenate([here[0:1], here[1:2]], axis=1)
    fill = jnp.zeros((out_ref.shape[1] - bias.shape[0] - 1, bias.shape[1]), jnp.float32)
    block = jnp.concatenate([bias, mask_row, fill], axis=0).astype(jnp.bfloat16)
    out_ref[...] = jnp.broadcast_to(block[None], out_ref.shape)


def put_parts(ref, value):
    lanes = ref.shape[2]
    for part in range(ref.shape[0]):
        ref[part] = value[:, part * lanes : (part + 1) * lanes]


def rows_of(ref, rows):
    return jnp.concatenate([ref[part, rows, :] for part in range(ref.shape[0])], axis=1)


def project_body(x_ref, small_ref, ask_ref, look_ref, q_ref, k_ref, v_ref, g_ref):
    width = ask_ref.shape[1]
    normed = normed_rows(x_ref[...], small_ref[ROW_GAIN : ROW_GAIN + 1]).astype(jnp.bfloat16)
    scaling = 1.0 / math.sqrt(PER_FOCUS_WIDTH)
    q = (dot_nn(normed, ask_ref[...]) * scaling).astype(jnp.bfloat16).astype(jnp.float32)
    put_parts(q_ref, q)
    others = dot_nn(normed, look_ref[...])
    k_ref[...] = others[:, :width].astype(jnp.bfloat16)
    v_ref[...] = others[:, width : 2 * width].astype(jnp.bfloat16)
    put_parts(g_ref, jax.nn.sigmoid(others[:, 2 * width :]))


def head_spread(q):
    head_of = lane_iota(q.shape) // PER_FOCUS_WIDTH
    return jnp.concatenate(
        [jnp.where(head_of == h, q, 0.0) for h in range(FOCUS_NUMBER)], axis=0
    ).astype(jnp.bfloat16)


def attend_heads(q, k, v, offset):
    scores = dot_nt(head_spread(q), k) + offset
    scores = scores - jnp.max(scores, axis=-1, keepdims=True)
    raised = jnp.exp(scores)
    shares = (raised / jnp.sum(raised, axis=-1, keepdims=True)).astype(jnp.bfloat16)
    mixed = dot_nn(shares, v)
    rows = q.shape[0]
    head_of = lane_iota(q.shape) // PER_FOCUS_WIDTH
    total = jnp.where(head_of == 0, mixed[:rows], 0.0)
    for h in range(1, FOCUS_NUMBER):
        total = jnp.where(head_of == h, mixed[h * rows : (h + 1) * rows], total)
    return total


def row_body(blk_ref, x_ref, q_ref, k_ref, v_ref, g_ref, final_ref, out_ref, wide, send, x_parts):
    devices = blk_ref.shape[0]
    put_parts(x_parts, x_ref[...])
    per_block = blk_ref.shape[1]
    half = wide.shape[1] // 2
    per_seq = 2 * devices
    wide[...] = blk_ref[...].astype(jnp.float32).reshape(wide.shape)
    mine = wide[pl.ds(lax.axis_index("dap") * per_block + FOCUS_NUMBER, 1), :]
    penalty = MASK_PENALTY_SCALE * (mine - 1.0)
    heads = [wide[pl.ds(h, devices, stride=per_block), :] for h in range(FOCUS_NUMBER)]
    for s in range(2):
        keys = k_ref[s * per_seq : (s + 1) * per_seq, :]
        values = v_ref[s * per_seq : (s + 1) * per_seq, :]
        for r in range(2):
            rows = pl.ds(s * per_seq + r, devices, stride=2)
            bias = jnp.concatenate([b[:, r * half : (r + 1) * half] for b in heads], axis=0)
            mixed = attend_heads(rows_of(q_ref, rows), keys, values, bias + penalty[:, s * half : (s + 1) * half])
            y = (mixed * rows_of(g_ref, rows)).astype(jnp.bfloat16)
            updated = rows_of(x_parts, rows) + dot_nn(y, final_ref[...])
            for part in range(updated.shape[1] // (2 * half)):
                to = pl.ds((s * 2 + r) * 2 + part, devices, stride=out_ref.shape[1])
                send[to, :] = updated[:, part * 2 * half : (part + 1) * 2 * half]
    out_ref[...] = send[...].reshape(out_ref.shape).astype(jnp.bfloat16)


def mask_block(blk_ref, wide):
    wide[...] = blk_ref[...].astype(jnp.float32).reshape(wide.shape)
    rows = pl.ds(FOCUS_NUMBER, blk_ref.shape[0], stride=blk_ref.shape[1])
    return wide[rows, :].astype(jnp.bfloat16)


def column_body(
    arrived_ref, blk_ref, small_ref, ask_ref, look_ref, final_ref, map_ref,
    msa_ref, opm_ref, wide, wide_blk, x_all, msa,
):
    devices = arrived_ref.shape[0]
    width = ask_ref.shape[1]
    lanes = wide.shape[1]
    half = lanes // 2
    seqs = 2 * devices
    me = lax.axis_index("dap")
    wide[...] = arrived_ref[...].astype(jnp.float32).reshape(wide.shape)
    for r in range(2):
        for s in range(2):
            base = (s * 2 + r) * 2
            at = (r * 2 + s) * devices
            for part in range(2):
                x_all[at : at + devices, part * lanes : (part + 1) * lanes] = wide[
                    pl.ds(base + part, devices, stride=8), :
                ]
    mask_lanes = mask_block(blk_ref, wide_blk)
    row = lax.broadcasted_iota(jnp.int32, (8, lanes), 0)
    wanted = (row % 2) * half + 2 * me + row // 2
    pick = jnp.where((lane_iota((8, lanes)) == wanted) & (row < 4), 1.0, 0.0).astype(jnp.bfloat16)
    picked = dot_nt(pick, mask_lanes)
    present = [
        jnp.concatenate([picked[2 * r : 2 * r + 1], picked[2 * r + 1 : 2 * r + 2]], axis=1)
        for r in range(2)
    ]
    x = x_all[...]
    normed = normed_rows(x, small_ref[COLUMN_GAIN : COLUMN_GAIN + 1]).astype(jnp.bfloat16)
    scaling = 1.0 / math.sqrt(PER_FOCUS_WIDTH)
    q = (dot_nn(normed, ask_ref[...]) * scaling).astype(jnp.bfloat16).astype(jnp.float32)
    others = dot_nn(normed, look_ref[...])
    keys = others[:, :width].astype(jnp.bfloat16)
    values = others[:, width : 2 * width].astype(jnp.bfloat16)
    gates = jax.nn.sigmoid(others[:, 2 * width :])
    mixed = jnp.concatenate(
        [
            attend_heads(
                q[r * seqs : (r + 1) * seqs],
                keys[r * seqs : (r + 1) * seqs],
                values[r * seqs : (r + 1) * seqs],
                MASK_PENALTY_SCALE * (present[r] - 1.0),
            )
            for r in range(2)
        ],
        axis=0,
    )
    updated = x + dot_nn((mixed * gates).astype(jnp.bfloat16), final_ref[...])
    for r in range(2):
        for s in range(2):
            at = (r * 2 + s) * devices
            for part in range(2):
                msa[r * 2 + part, pl.ds(s, devices, stride=2), :] = updated[
                    at : at + devices, part * lanes : (part + 1) * lanes
                ]
    for part in range(4):
        msa_ref[:, part * lanes : (part + 1) * lanes] = msa[part]
    normed = normed_rows(updated, small_ref[MEAN_GAIN : MEAN_GAIN + 1]).astype(jnp.bfloat16)
    sides = [
        dot_nt(map_ref[...], normed[r * seqs : (r + 1) * seqs]) * present[r] for r in range(2)
    ]
    block = jnp.concatenate(sides, axis=1).astype(jnp.bfloat16)
    opm_ref[...] = jnp.broadcast_to(block[None], opm_ref.shape)


def gated(projected, q_at, g_at, width):
    return jax.nn.sigmoid(projected[:, g_at : g_at + width]) * projected[:, q_at : q_at + width]


def presence_down(amino_row, half, lanes):
    square = lax.broadcasted_iota(jnp.int32, (half, half), 0) == lane_iota((half, half))
    diagonal = jnp.where(square, amino_row.astype(jnp.float32), 0.0).astype(jnp.bfloat16)
    return dot_nn(diagonal, jnp.ones((half, lanes), jnp.bfloat16))


def opm_body(steps, own_ref, oth_ref, *refs):
    couples, refs = refs[:steps], refs[steps:]
    (
        blk_ref, fin_ref, small_ref, flank_ref,
        pair_one_ref, normed_ref, right_ref,
        order, order16, outer, counts, mkeys, wide_blk,
    ) = refs
    chips, lanes, channels = pair_one_ref.shape
    hidden = outer.shape[2]
    half = lanes // 2
    me = lax.axis_index("dap")
    parity = lax.rem(me, 2)
    my_chip = me // 2
    for k in range(steps):
        for h in range(chips // steps):
            pair_one_ref[my_chip ^ (h * steps + k)] = couples[k][h].astype(jnp.float32)
    rows = (chips * hidden, lanes)
    order16[parity] = own_ref[:, hidden:, :].astype(jnp.float32).reshape(rows)
    order16[1 - parity] = oth_ref[:, hidden:, :].astype(jnp.float32).reshape(rows)
    for b in range(hidden):
        for p in range(2):
            rows = order16[p, pl.ds(b, chips, stride=hidden), :]
            for r in range(2):
                order[pl.ds(b * half + 2 * p + r, chips, stride=4), :] = (
                    pltpu.roll(rows, half, 1) if r else rows
                )
    rights = order[...].astype(jnp.bfloat16)[:, :half]
    for r in range(2):
        lhs = own_ref[:, :hidden, :].reshape(chips * hidden, lanes)[:, r * half : (r + 1) * half]
        outer[r] = dot_nt(lhs, rights).astype(jnp.bfloat16).reshape(outer.shape[1:])
    mask_rows = mask_block(blk_ref, wide_blk)
    total = jnp.zeros((half, lanes), jnp.float32)
    for s in range(2):
        part = mask_rows[:, s * half : (s + 1) * half]
        total = total + dot_tn(part, jnp.concatenate([part, part], axis=1))
    counts[...] = 1.0 / jnp.maximum(total, 1.0)
    mkeys[...] = presence_down(small_ref[PRESENCE : PRESENCE + 1, :half], half, lanes)
    gain = small_ref[ENTRY_GAINS : ENTRY_GAINS + 1, :channels]
    low = lane_iota((channels, lanes)) < half
    low_row = lane_iota((1, lanes)) < half
    group = 16

    @pl.loop(0, chips // group)
    def _(block):
        pairs, keeps = [], []
        for c in range(group):
            chip = block * group + c
            sides = []
            for r in range(2):
                strip = outer[r, chip]
                sides.append(
                    jnp.concatenate(
                        [strip[:, g * lanes : (g + 1) * lanes] for g in range(hidden // 2)], axis=0
                    )
                )
            res = dot_nn(fin_ref[...], jnp.concatenate(sides, axis=1))
            a0, a1 = res[:channels, :lanes], res[:channels, lanes:]
            b0, b1 = res[channels:, :lanes], res[channels:, lanes:]
            turned = jnp.where(low, a0, b1) + pltpu.roll(jnp.where(low, a1, b0), half, 1)
            i0 = 4 * chip + 2 * parity
            share = jnp.where(low_row, counts[pl.ds(i0, 1), :], counts[pl.ds(i0 + 1, 1), :])
            pairs.append(jnp.transpose(turned * share) + pair_one_ref[chip])
            for r in range(2):
                keeps.append(mkeys[...] * mkeys[pl.ds(i0 + r, 1), :])
        pair = jnp.concatenate(pairs, axis=0)
        keep = jnp.concatenate(keeps, axis=0)
        normed = normed_rows(pair, gain).astype(jnp.bfloat16)
        projected = dot_nn(normed, flank_ref[0, :, 2 * channels :])
        right = gated(projected, 0, channels, channels) * keep
        for c in range(group):
            chip = block * group + c
            rows = slice(c * lanes, (c + 1) * lanes)
            pair_one_ref[chip] = pair[rows]
            normed_ref[chip] = normed[rows]
            right_ref[chip] = jnp.transpose(right[rows]).astype(jnp.bfloat16)


def left_body(normed_ref, small_ref, flank_ref, switch_ref, left_ref, gate_ref, mkeys):
    chips, lanes, channels = gate_ref.shape
    half = lanes // 2
    parity = lax.rem(lax.axis_index("dap"), 2)
    mkeys[...] = presence_down(small_ref[PRESENCE : PRESENCE + 1, :half], half, lanes)
    group = 8
    for block in range(chips // group):
        keeps = []
        for c in range(group):
            for r in range(2):
                keeps.append(mkeys[...] * mkeys[pl.ds(4 * (block * group + c) + 2 * parity + r, 1), :])
        normed = normed_ref[block * group : (block + 1) * group].reshape(group * lanes, channels)
        projected = dot_nn(normed, flank_ref[0, :, : 2 * channels])
        left = gated(projected, 0, channels, channels) * jnp.concatenate(keeps, axis=0)
        gate = jax.nn.sigmoid(dot_nn(normed, switch_ref[0]))
        for c in range(group):
            chip = block * group + c
            rows = slice(c * lanes, (c + 1) * lanes)
            gate_ref[chip] = gate[rows]
            left_ref[chip * channels : (chip + 1) * channels, :] = jnp.transpose(left[rows])


def outgoing_body(
    pair_one_ref, left_ref, gate_ref, own_ref, oth_ref, small_ref, final_ref, flank_ref,
    two_ref, send_ref,
    sides, prods, mkeys, pair_two, rows_out, cols,
):
    chips, channels, lanes = own_ref.shape
    half = lanes // 2
    me = lax.axis_index("dap")
    parity = lax.rem(me, 2)
    my_chip = me // 2
    flag = jnp.broadcast_to(parity, (1, 1)) == 0

    @pl.loop(0, chips)
    def _(chip):
        own = own_ref[chip].astype(jnp.float32)
        oth = oth_ref[chip].astype(jnp.float32)
        rows = pl.ds(pl.multiple_of(chip * channels, channels), channels)
        sides[0, rows, :] = jnp.where(flag, own, oth)
        sides[1, rows, :] = jnp.where(flag, oth, own)

    low = lane_iota((chips, lanes)) < half

    per_step = 64

    @pl.loop(0, channels // per_step)
    def _(octet):
        results = []
        stacked = []
        for ref in (left_ref, sides.at[0], sides.at[1]):
            stacked.append([])
            for o in range(per_step // 8):
                eight = jnp.stack(
                    [
                        ref[pl.ds(pl.multiple_of(chip * channels + octet * per_step + o * 8, 8), 8), :]
                        for chip in range(chips)
                    ]
                )
                stacked[-1].append(jnp.swapaxes(eight, 0, 1))
        for c in range(per_step):
            lhs = stacked[0][c // 8][c % 8].astype(jnp.bfloat16)
            pieces = [[], []]
            for p in range(2):
                rows = stacked[1 + p][c // 8][c % 8]
                turned = pltpu.roll(rows, half, 1)
                pieces[0] += [jnp.where(low, rows, 0.0), jnp.where(low, turned, 0.0)]
                pieces[1] += [jnp.where(low, 0.0, turned), jnp.where(low, 0.0, rows)]
            rhs = jnp.concatenate(pieces[0] + pieces[1], axis=0).astype(jnp.bfloat16)
            results.append(dot_nt(lhs, rhs))
        for c in range(per_step):
            to = pl.ds(pl.multiple_of((octet * per_step + c) * chips, chips), chips)
            prods[to, :] = results[c].astype(jnp.bfloat16).astype(jnp.float32)

    mkeys[...] = presence_down(small_ref[PRESENCE : PRESENCE + 1, :half], half, channels)
    gain_mid = small_ref[MID_GAINS : MID_GAINS + 1, :channels]
    gain_mid = jnp.transpose(jnp.broadcast_to(gain_mid, (channels, channels)))
    final_t = jnp.transpose(final_ref[0].astype(jnp.float32)).astype(jnp.bfloat16)
    gain = small_ref[ENTRY_GAINS : ENTRY_GAINS + 1, channels : 2 * channels]
    flank_right = flank_ref[1, :, 2 * channels :]
    flank_left = flank_ref[1, :, : 2 * channels]
    octet = pl.multiple_of(8 * (my_chip // 2), 8)
    group = 8
    for block in range(chips // group):
        changed = []
        for c in range(group):
            x = prods[pl.ds(block * group + c, channels, stride=chips), :]
            centred = x - jnp.mean(x, axis=0, keepdims=True)
            spread = jnp.mean(centred * centred, axis=0, keepdims=True)
            changed.append((centred * lax.rsqrt(spread + EPSILON) * gain_mid).astype(jnp.bfloat16))
        changed = dot_nn(final_t, jnp.concatenate(changed, axis=1))
        for c in range(group):
            part = jnp.transpose(changed[:, c * lanes : (c + 1) * lanes])
            for k in range(8):
                r, p, rj = k // 4, (k // 2) % 2, k % 2
                rows_out[block * group + c, pl.ds(r * half + 2 * p + rj, chips, stride=4), :] = part[
                    k * chips : (k + 1) * chips
                ]
        twos, keeps = [], []
        for c in range(group):
            chip = block * group + c
            two = pair_one_ref[chip] + rows_out[chip] * gate_ref[chip]
            twos.append(two)
            for r in range(2):
                keeps.append(mkeys[pl.ds(4 * chip + 2 * parity + r, 1), :])
        two = jnp.concatenate(twos, axis=0)
        full = normed_rows(two, gain)
        normed = full.astype(jnp.bfloat16)
        keep = jnp.concatenate([mkeys[...] * m for m in keeps], axis=0)
        going = (gated(dot_nn(normed, flank_right), 0, channels, channels) * keep).astype(jnp.bfloat16)
        cols[block] = full
        few = jnp.concatenate(
            [cols[block, pl.ds(k * half + octet, 8), :] for k in range(2 * group)], axis=0
        ).astype(jnp.bfloat16)
        mine = mkeys[pl.ds(octet, 8), :]
        keep = jnp.concatenate([mine * m for m in keeps], axis=0)
        few = (gated(dot_nn(few, flank_left), 0, channels, channels) * keep).astype(jnp.bfloat16)
        for c in range(group):
            chip = block * group + c
            pair_two[chip] = twos[c]
            send_ref[chip, :lanes, :] = going[c * lanes : (c + 1) * lanes]
            send_ref[chip, lanes:, :] = few[c * 16 : (c + 1) * 16]
    two_ref[...] = pair_two[my_chip]


def add_products(side_ref, tails, totals):
    chips = side_ref.shape[0]
    half, _ = totals[0].shape
    lanes = 2 * half
    me = lax.axis_index("dap")
    first = 4 * lax.rem(me // 2, 2) + 2 * lax.rem(me, 2)
    tails[...] = side_ref[:, lanes:, :].astype(jnp.float32).reshape(tails.shape)
    ahead = 4

    def step(block, totals):
        totals = list(totals)
        for c in range(ahead):
            chip = block * ahead + c
            for k in range(2):
                there = side_ref[chip, k * half : (k + 1) * half, :].astype(jnp.float32)
                for i in range(2):
                    one = tails[pl.ds(chip * 16 + 8 * k + first + i, 1), :]
                    totals[i] = totals[i] + one * there
        return tuple(totals)

    return lax.fori_loop(0, chips // ahead, step, tuple(totals))


def incoming_own_body(own_ref, two_ref, couple_ref, small_ref, switch_ref, sums_ref, kept_ref, gate_ref, tails):
    lanes, channels = two_ref.shape
    half = lanes // 2
    zero = jnp.zeros((half, channels), jnp.float32)
    sums_ref[...] = jnp.concatenate(add_products(own_ref, tails, (zero, zero)), axis=0)
    two = two_ref[...]
    gain = small_ref[ENTRY_GAINS : ENTRY_GAINS + 1, channels : 2 * channels]
    normed = normed_rows(two, gain).astype(jnp.bfloat16)
    gate_ref[...] = jax.nn.sigmoid(dot_nn(normed, switch_ref[1]))
    couple = couple_ref[...]
    kept_ref[...] = two + (couple - couple.astype(jnp.bfloat16).astype(jnp.float32))


def incoming_body(oth_ref, sums_ref, kept_ref, gate_ref, small_ref, final_ref, out_ref, tails):
    lanes, channels = out_ref.shape
    half = lanes // 2
    prod = jnp.concatenate(
        add_products(oth_ref, tails, (sums_ref[:half, :], sums_ref[half:, :])), axis=0
    )
    prod = prod.astype(jnp.bfloat16).astype(jnp.float32)
    gain_mid = small_ref[MID_GAINS : MID_GAINS + 1, channels : 2 * channels]
    changed = dot_nn(normed_rows(prod, gain_mid).astype(jnp.bfloat16), final_ref[1])
    out_ref[...] = kept_ref[...] + changed * gate_ref[...]


def gather_by_steps(block, chips):
    bits = chips.bit_length() - 1
    steps = 1 << (bits // 2)
    devices = 2 * chips

    def fetch(value, apart):
        return lax.ppermute(value, "dap", [(d, d ^ (2 * apart)) for d in range(devices)])

    parts = [fetch(block, h * steps) for h in range(1, chips // steps)]
    near = jnp.concatenate([block] + parts, axis=0)
    return near, [fetch(near, k) for k in range(1, steps)]


def paired_shards(
    homolog_stack,
    couple_tensor,
    homolog_presence,
    amino_presence,
    horizontal_standard_factor,
    horizontal_asking_matrix,
    horizontal_lookup_triple,
    horizontal_final_matrix,
    couple_offset_factor,
    couple_offset_matrix,
    vertical_standard_factor,
    vertical_asking_matrix,
    vertical_lookup_triple,
    vertical_final_matrix,
    tensor_average_factor,
    tensor_average_mapping,
    tensor_average_final,
    trio_entry_factors,
    trio_flank_mappings,
    trio_final_switches,
    trio_multiplied_factors,
    trio_final_matrices,
):
    devices = lax.axis_size("dap")
    chips = devices // 2
    strands, aminos, features = homolog_stack.shape
    rows, _, channels = couple_tensor.shape
    lanes = rows * aminos
    heads = FOCUS_NUMBER
    hidden = TENSOR_HIDDEN
    f32, bf16 = jnp.float32, jnp.bfloat16
    shape = jax.ShapeDtypeStruct
    same_parity = [[2 * chip + p for chip in range(chips)] for p in range(2)]
    swap = [(d, d ^ 1) for d in range(devices)]

    def line(v):
        return v.reshape(1, -1)

    couple = couple_tensor.reshape(lanes, channels)
    x = homolog_stack.reshape(strands * aminos, features)
    block, near = vmem_call(
        bias_body,
        (shape((devices, 16, lanes), bf16), shape((1, lanes, channels), bf16)),
        scratch=[
            pltpu.VMEM((lanes, channels), f32),
            pltpu.VMEM((1, channels), f32),
            pltpu.VMEM((heads, channels), bf16),
            pltpu.VMEM((strands, aminos), jnp.int32),
            pltpu.SemaphoreType.DMA((4,)),
        ],
        count=4,
        away=range(4),
        grant=60 << 20,
    )(couple, line(couple_offset_factor), couple_offset_matrix.T, homolog_presence)
    blocks = lax.all_to_all(block, "dap", split_axis=0, concat_axis=0, tiled=True)
    small = jnp.concatenate(
        [
            line(horizontal_standard_factor),
            line(vertical_standard_factor),
            line(tensor_average_factor),
            line(trio_entry_factors),
            line(trio_multiplied_factors),
            jnp.pad(line(amino_presence.astype(f32)), ((0, 0), (0, features - aminos))),
            jnp.zeros((2, features), f32),
        ],
        axis=0,
    )
    final = jnp.transpose(
        tensor_average_final.reshape(hidden, hidden // 2, 2, channels), (2, 3, 1, 0)
    ).reshape(2 * channels, hidden * hidden // 2)
    q, k, v, g = vmem_call(
        project_body,
        (
            shape((features // lanes, lanes, lanes), f32),
            shape((lanes, features), bf16),
            shape((lanes, features), bf16),
            shape((features // lanes, lanes, lanes), f32),
        ),
        count=4,
    )(x, small, horizontal_asking_matrix, horizontal_lookup_triple)
    near, fars = gather_by_steps(near, chips)
    couples = [near, *fars]
    sent = vmem_call(
        row_body,
        shape((devices, 8, lanes), bf16),
        scratch=[
            pltpu.VMEM((devices * 16, lanes), f32),
            pltpu.VMEM((devices * 8, lanes), f32),
            pltpu.VMEM((features // lanes, lanes, lanes), f32),
        ],
        count=7,
    )(blocks, x, q, k, v, g, horizontal_final_matrix)
    arrived = lax.all_to_all(sent, "dap", split_axis=0, concat_axis=0, tiled=True)
    msa, opm = vmem_call(
        column_body,
        (shape((devices * strands, rows * features), f32), shape((chips, 2 * hidden, lanes), bf16)),
        scratch=[
            pltpu.VMEM((devices * 8, lanes), f32),
            pltpu.VMEM((devices * 16, lanes), f32),
            pltpu.VMEM((lanes, features), f32),
            pltpu.VMEM((4, devices * strands, lanes), f32),
        ],
        count=7,
        later=1,
    )(
        arrived,
        blocks,
        small,
        vertical_asking_matrix,
        vertical_lookup_triple,
        vertical_final_matrix,
        tensor_average_mapping.T,
        final,
    )
    opm_own = lax.all_to_all(
        opm, "dap", split_axis=0, concat_axis=0, tiled=True, axis_index_groups=same_parity
    )
    opm_oth = lax.ppermute(opm_own, "dap", swap)
    msa = msa.reshape(devices * strands, rows, features)
    stack = (chips, lanes, channels)
    pair_one, normed, right_own = vmem_call(
        functools.partial(opm_body, len(couples)),
        (shape(stack, f32), shape(stack, bf16), shape(stack, bf16)),
        scratch=[
            pltpu.VMEM((hidden * aminos, lanes), f32),
            pltpu.VMEM((2, chips * hidden, lanes), f32),
            pltpu.VMEM((2, chips, hidden, hidden * aminos), bf16),
            pltpu.VMEM((aminos, lanes), f32),
            pltpu.VMEM((aminos, channels), f32),
            pltpu.VMEM((devices * 16, lanes), f32),
        ],
        count=len(couples) + 6,
        later=1,
    )(
        opm_own,
        opm_oth,
        *couples,
        blocks,
        final,
        small,
        trio_flank_mappings,
        msa,
    )
    right_oth = lax.ppermute(right_own, "dap", swap)
    left, gate = vmem_call(
        left_body,
        (shape((chips * channels, lanes), f32), shape(stack, f32)),
        scratch=[pltpu.VMEM((aminos, channels), f32)],
        count=4,
    )(normed, small, trio_flank_mappings, trio_final_switches)
    two, going = vmem_call(
        outgoing_body,
        (shape((lanes, channels), f32), shape((chips, lanes + 16, channels), bf16)),
        scratch=[
            pltpu.VMEM((2, chips * channels, lanes), f32),
            pltpu.VMEM((channels * chips, lanes), f32),
            pltpu.VMEM((aminos, channels), f32),
            pltpu.VMEM(stack, f32),
            pltpu.VMEM(stack, f32),
            pltpu.VMEM((chips // 8, 8 * lanes, channels), f32),
        ],
        count=8,
    )(
        pair_one,
        left,
        gate,
        right_own,
        right_oth,
        small,
        trio_final_matrices,
        trio_flank_mappings,
    )
    coming = lax.ppermute(going, "dap", swap)
    own_rows = shape((lanes, channels), f32)
    tails = [pltpu.VMEM((chips * 16, channels), f32)]
    sums, kept, gate = vmem_call(
        incoming_own_body, (own_rows,) * 3, scratch=tails, count=5
    )(going, two, couple, small, trio_final_switches)
    pair_out = vmem_call(incoming_body, own_rows, scratch=tails, count=6)(
        coming, sums, kept, gate, small, trio_final_matrices
    )
    return msa, pair_out.reshape(rows, aminos, channels)


def fits_pairs(homolog_stack, couple_tensor, devices):
    strands, aminos, features = homolog_stack.shape
    rows, _, channels = couple_tensor.shape
    lanes = 128
    return (
        strands == rows == 2
        and devices % 8 == 0
        and devices & (devices - 1) == 0
        and rows * aminos == lanes == channels
        and aminos == 2 * devices
        and features == 2 * lanes
    )


def either(*arrays):
    if fits_pairs(arrays[0], arrays[1], lax.axis_size("dap")):
        return paired_shards(*arrays)
    return shards(*arrays)


def solution(mesh):
    placed = (
        P("dap", None, None),
        P("dap", None, None),
        P("dap", None),
        P(),
        P(),
        P(),
        P(),
        P(),
        P(),
        P(),
        P(),
        P(),
        P(),
        P(),
        P(),
        P(),
        P(),
        P(),
        P(),
        P(),
        P(),
        P(),
    )
    return jax.shard_map(
        either,
        mesh=mesh,
        in_specs=placed,
        out_specs=(P(None, "dap", None), P("dap", None, None)),
        check_vma=False,
    )
```

```python
import functools
import math

import jax
import jax.numpy as jnp
from jax import lax
from jax.experimental import pallas as pl
from jax.experimental.pallas import tpu as pltpu
from jax.sharding import PartitionSpec as P

FOCUS_NUMBER = 8
PER_FOCUS_WIDTH = 32
TENSOR_HIDDEN = 32
TRI_HID = 128


EPSILON = 1e-05
MASK_PENALTY_SCALE = 1000000000.0


def standardize_features(content_vectors, gain, axis):
    centred = content_vectors - jnp.mean(content_vectors, axis=axis, keepdims=True)
    spread = jnp.mean(centred * centred, axis=axis, keepdims=True)
    return centred * lax.rsqrt(spread + EPSILON) * gain


def gather_blocks(block):
    device_count = lax.axis_size("dap")
    copies = jnp.broadcast_to(block[None], (device_count,) + block.shape)
    return lax.all_to_all(copies, "dap", split_axis=0, concat_axis=0, tiled=True)


def triangle(
    pair_now, gain_in, proj_weight, gate_weight, gain_mid, final_weight, amino_presence, incoming
):
    hidden = TRI_HID
    row_count = pair_now.shape[0]
    my_index = lax.axis_index("dap")
    standardized_source = standardize_features(pair_now, gain_in, -1).astype(jnp.bfloat16)
    projected = jnp.einsum(
        "rkd,de->erk", standardized_source, proj_weight, preferred_element_type=jnp.float32
    )
    res_float = amino_presence.astype(jnp.float32)
    own_rows = lax.dynamic_slice_in_dim(res_float, my_index * row_count, row_count)
    pair_mask = own_rows[:, None] * res_float[None, :]
    left_side = (
        jax.nn.sigmoid(projected[hidden : 2 * hidden]) * projected[:hidden] * pair_mask[None]
    ).astype(jnp.bfloat16)
    right_side = (
        jax.nn.sigmoid(projected[3 * hidden :])
        * projected[2 * hidden : 3 * hidden]
        * pair_mask[None]
    ).astype(jnp.bfloat16)
    gating = jax.nn.sigmoid(
        jnp.dot(standardized_source, gate_weight, preferred_element_type=jnp.float32)
    )
    device_count = lax.axis_size("dap")
    per_device = hidden // device_count
    both = jnp.stack(
        [
            left_side.reshape(device_count, per_device, row_count, -1),
            right_side.reshape(device_count, per_device, row_count, -1),
        ],
        axis=1,
    )
    both = lax.all_to_all(both, "dap", split_axis=0, concat_axis=0, tiled=True)
    both = jnp.moveaxis(both, 0, 2).reshape(2, per_device, device_count * row_count, -1)
    left_chan, right_chan = both[0], both[1]
    if incoming:
        product = jnp.einsum(
            "cki,ckj->cij", left_chan, right_chan, preferred_element_type=jnp.float32
        )
    else:
        product = jnp.einsum(
            "cik,cjk->cij", left_chan, right_chan, preferred_element_type=jnp.float32
        )
    product = product.astype(jnp.bfloat16)
    returned = lax.all_to_all(product, "dap", split_axis=1, concat_axis=0, tiled=True)
    product_normed = standardize_features(
        returned.astype(jnp.float32), gain_mid[:, None, None], 0
    ).astype(jnp.bfloat16)
    update = jnp.einsum(
        "crj,cd->rjd", product_normed, final_weight, preferred_element_type=jnp.float32
    )
    return pair_now + update * gating


def shards(
    homolog_stack,
    couple_tensor,
    homolog_presence,
    amino_presence,
    horizontal_standard_factor,
    horizontal_asking_matrix,
    horizontal_lookup_triple,
    horizontal_final_matrix,
    couple_offset_factor,
    couple_offset_matrix,
    vertical_standard_factor,
    vertical_asking_matrix,
    vertical_lookup_triple,
    vertical_final_matrix,
    tensor_average_factor,
    tensor_average_mapping,
    tensor_average_final,
    trio_entry_factors,
    trio_flank_mappings,
    trio_final_switches,
    trio_multiplied_factors,
    trio_final_matrices,
):
    nested_function = FOCUS_NUMBER * PER_FOCUS_WIDTH
    scaling = 1.0 / math.sqrt(PER_FOCUS_WIDTH)
    strand_portion = homolog_stack.shape[0]
    amino_total = homolog_stack.shape[1]
    row_count = couple_tensor.shape[0]
    pair_normed = standardize_features(couple_tensor, couple_offset_factor, -1).astype(jnp.bfloat16)
    bias_local = jnp.einsum(
        "rjc,ch->hrj", pair_normed, couple_offset_matrix, preferred_element_type=jnp.float32
    ).astype(jnp.bfloat16)
    standardized_source = standardize_features(
        homolog_stack, horizontal_standard_factor, -1
    ).astype(jnp.bfloat16)
    shaped = (strand_portion, amino_total, FOCUS_NUMBER, PER_FOCUS_WIDTH)
    queries = (
        (
            jnp.dot(
                standardized_source, horizontal_asking_matrix, preferred_element_type=jnp.float32
            )
            * scaling
        )
        .astype(jnp.bfloat16)
        .reshape(shaped)
    )
    others = jnp.dot(
        standardized_source, horizontal_lookup_triple, preferred_element_type=jnp.float32
    )
    keys_all = others[..., :nested_function].astype(jnp.bfloat16).reshape(shaped)
    content_entire = (
        others[..., nested_function : 2 * nested_function].astype(jnp.bfloat16).reshape(shaped)
    )
    sigmoid_switches = jax.nn.sigmoid(others[..., 2 * nested_function :])
    mask_penalty = MASK_PENALTY_SCALE * (homolog_presence.astype(jnp.float32) - 1.0)

    def attend(bias_piece):
        query_rows = bias_piece.shape[1]
        scores = jnp.einsum(
            "sihc,sjhc->shij", queries, keys_all, preferred_element_type=jnp.float32
        )
        scores = scores + bias_piece.astype(jnp.float32)[None] + mask_penalty[:, None, None, :]
        softmax_probabilities = jax.nn.softmax(scores, axis=-1).astype(jnp.bfloat16)
        mixed = jnp.einsum(
            "shij,sjhc->sihc",
            softmax_probabilities,
            content_entire,
            preferred_element_type=jnp.float32,
        )
        return mixed.reshape(strand_portion, query_rows, nested_function)

    bias_whole = jnp.moveaxis(gather_blocks(bias_local), 0, 1).reshape(
        FOCUS_NUMBER, amino_total, amino_total
    )
    block_rows = math.gcd(amino_total, 256)

    def one_block(block_index):
        return attend(bias_whole)

    blocks = lax.map(one_block, jnp.arange(amino_total // block_rows, dtype=jnp.int32))
    focused_content = jnp.moveaxis(blocks, 0, 1).reshape(
        strand_portion, amino_total, nested_function
    )
    homolog_stack_horizontal = homolog_stack + jnp.dot(
        (focused_content * sigmoid_switches).astype(jnp.bfloat16),
        horizontal_final_matrix,
        preferred_element_type=jnp.float32,
    )
    travelling = jnp.concatenate(
        [
            homolog_stack_horizontal.astype(jnp.bfloat16),
            jnp.broadcast_to(
                homolog_presence.astype(jnp.bfloat16)[..., None],
                (strand_portion, amino_total, 128),
            ),
        ],
        axis=-1,
    )
    arrived = lax.all_to_all(travelling, "dap", split_axis=1, concat_axis=0, tiled=True)
    column_view = arrived[..., :nested_function].astype(jnp.float32)
    col_mask = arrived[..., nested_function].astype(jnp.float32)
    seq_total = column_view.shape[0]
    col_shape = (seq_total, row_count, FOCUS_NUMBER, PER_FOCUS_WIDTH)
    standardized_source = standardize_features(column_view, vertical_standard_factor, -1).astype(
        jnp.bfloat16
    )
    col_queries = (
        (
            jnp.dot(standardized_source, vertical_asking_matrix, preferred_element_type=jnp.float32)
            * scaling
        )
        .astype(jnp.bfloat16)
        .reshape(col_shape)
    )
    col_others = jnp.dot(
        standardized_source, vertical_lookup_triple, preferred_element_type=jnp.float32
    )
    col_keys = col_others[..., :nested_function].astype(jnp.bfloat16).reshape(col_shape)
    col_values = (
        col_others[..., nested_function : 2 * nested_function]
        .astype(jnp.bfloat16)
        .reshape(col_shape)
    )
    col_gates = jax.nn.sigmoid(col_others[..., 2 * nested_function :])
    col_penalty = MASK_PENALTY_SCALE * (col_mask - 1.0)
    scores = jnp.einsum(
        "sihc,tihc->ihst", col_queries, col_keys, preferred_element_type=jnp.float32
    )
    scores = scores + jnp.transpose(col_penalty)[:, None, None, :]
    softmax_probabilities = jax.nn.softmax(scores, axis=-1).astype(jnp.bfloat16)
    col_mixed = jnp.einsum(
        "uovg,guox->vuox", softmax_probabilities, col_values, preferred_element_type=jnp.float32
    ).reshape(seq_total, row_count, nested_function)
    alignment_after_columns = column_view + jnp.dot(
        (col_mixed * col_gates).astype(jnp.bfloat16),
        vertical_final_matrix,
        preferred_element_type=jnp.float32,
    )
    standardized_source = standardize_features(
        alignment_after_columns, tensor_average_factor, -1
    ).astype(jnp.bfloat16)
    halves = jnp.dot(
        standardized_source, tensor_average_mapping, preferred_element_type=jnp.float32
    )
    left_proj = (halves[..., :TENSOR_HIDDEN] * col_mask[..., None]).astype(jnp.bfloat16)
    right_proj = (halves[..., TENSOR_HIDDEN:] * col_mask[..., None]).astype(jnp.bfloat16)
    block = jnp.concatenate(
        [right_proj, col_mask.astype(jnp.bfloat16)[..., None]], axis=-1
    )
    block = jnp.transpose(block, (1, 2, 0))
    whole = gather_blocks(block).reshape(amino_total, TENSOR_HIDDEN + 1, seq_total)
    right_whole = jnp.transpose(whole[:, :TENSOR_HIDDEN], (2, 0, 1))
    mask_whole = jnp.transpose(whole[:, TENSOR_HIDDEN])
    outer = jnp.einsum("sra,sjb->rjab", left_proj, right_whole, preferred_element_type=jnp.float32)
    outer = outer.astype(jnp.bfloat16).reshape(
        row_count, amino_total, TENSOR_HIDDEN * TENSOR_HIDDEN
    )
    counts = jnp.dot(
        jnp.transpose(col_mask), mask_whole.astype(jnp.float32), precision=lax.Precision.HIGHEST
    )
    product = (
        jnp.dot(outer, tensor_average_final, preferred_element_type=jnp.float32)
        / jnp.maximum(counts, 1.0)[..., None]
    )
    pair_one = couple_tensor + product
    pair_two = triangle(
        pair_one,
        trio_entry_factors[0],
        trio_flank_mappings[0],
        trio_final_switches[0],
        trio_multiplied_factors[0],
        trio_final_matrices[0],
        amino_presence,
        False,
    )
    pair_after_incoming = triangle(
        pair_two,
        trio_entry_factors[1],
        trio_flank_mappings[1],
        trio_final_switches[1],
        trio_multiplied_factors[1],
        trio_final_matrices[1],
        amino_presence,
        True,
    )
    return (alignment_after_columns, pair_after_incoming)


def normed_rows(x, gain):
    centred = x - jnp.mean(x, axis=-1, keepdims=True)
    spread = jnp.mean(centred * centred, axis=-1, keepdims=True)
    return centred * lax.rsqrt(spread + EPSILON) * gain


def dot_nn(a, b):
    return lax.dot_general(a, b, (((1,), (0,)), ((), ())), preferred_element_type=jnp.float32)


def dot_nt(a, b):
    return lax.dot_general(a, b, (((1,), (1,)), ((), ())), preferred_element_type=jnp.float32)


def dot_tn(a, b):
    return lax.dot_general(a, b, (((0,), (0,)), ((), ())), preferred_element_type=jnp.float32)


def lane_iota(shape):
    return lax.broadcasted_iota(jnp.int32, shape, len(shape) - 1)


def vmem_call(body, outs, scratch=(), count=0, later=0, away=(), grant=20 << 20):
    whole = pl.BlockSpec(memory_space=pltpu.VMEM)
    there = pl.BlockSpec(memory_space=pl.ANY)
    hbm = pl.BlockSpec(memory_space=pltpu.HBM)

    def reader(*refs):
        body(*refs[:count], *refs[count + later :])

    return pl.pallas_call(
        reader,
        out_shape=outs,
        in_specs=[hbm if k in away else whole for k in range(count)] + [there] * later,
        out_specs=jax.tree.map(lambda _: whole, outs),
        scratch_shapes=list(scratch),
        compiler_params=pltpu.CompilerParams(vmem_limit_bytes=grant),
    )


ROW_GAIN, COLUMN_GAIN, MEAN_GAIN, ENTRY_GAINS, MID_GAINS, PRESENCE = range(6)


def bias_body(pair_at, gain_at, weight_at, present_at, out_ref, near_ref, pair, gain, weight, present, sems):
    moves = [
        pltpu.make_async_copy(there, here, sems.at[k])
        for k, (there, here) in enumerate(
            ((pair_at, pair), (gain_at, gain), (weight_at, weight), (present_at, present))
        )
    ]
    for move in moves:
        move.start()
    for move in moves:
        move.wait()
    near_ref[0] = pair[...].astype(jnp.bfloat16)
    normed = normed_rows(pair[...], gain[...]).astype(jnp.bfloat16)
    bias = dot_nt(weight[...], normed)
    here = present[...].astype(jnp.float32)
    mask_row = jnp.concatenate([here[0:1], here[1:2]], axis=1)
    fill = jnp.zeros((out_ref.shape[1] - bias.shape[0] - 1, bias.shape[1]), jnp.float32)
    block = jnp.concatenate([bias, mask_row, fill], axis=0).astype(jnp.bfloat16)
    out_ref[...] = jnp.broadcast_to(block[None], out_ref.shape)


def put_parts(ref, value):
    lanes = ref.shape[2]
    for part in range(ref.shape[0]):
        ref[part] = value[:, part * lanes : (part + 1) * lanes]


def rows_of(ref, rows):
    return jnp.concatenate([ref[part, rows, :] for part in range(ref.shape[0])], axis=1)


def project_body(x_ref, small_ref, ask_ref, look_ref, q_ref, k_ref, v_ref, g_ref):
    width = ask_ref.shape[1]
    normed = normed_rows(x_ref[...], small_ref[ROW_GAIN : ROW_GAIN + 1]).astype(jnp.bfloat16)
    scaling = 1.0 / math.sqrt(PER_FOCUS_WIDTH)
    q = (dot_nn(normed, ask_ref[...]) * scaling).astype(jnp.bfloat16).astype(jnp.float32)
    put_parts(q_ref, q)
    others = dot_nn(normed, look_ref[...])
    k_ref[...] = others[:, :width].astype(jnp.bfloat16)
    v_ref[...] = others[:, width : 2 * width].astype(jnp.bfloat16)
    put_parts(g_ref, jax.nn.sigmoid(others[:, 2 * width :]))


def head_spread(q):
    head_of = lane_iota(q.shape) // PER_FOCUS_WIDTH
    return jnp.concatenate(
        [jnp.where(head_of == h, q, 0.0) for h in range(FOCUS_NUMBER)], axis=0
    ).astype(jnp.bfloat16)


def attend_heads(q, k, v, offset):
    scores = dot_nt(head_spread(q), k) + offset
    scores = scores - jnp.max(scores, axis=-1, keepdims=True)
    raised = jnp.exp(scores)
    shares = (raised / jnp.sum(raised, axis=-1, keepdims=True)).astype(jnp.bfloat16)
    mixed = dot_nn(shares, v)
    rows = q.shape[0]
    head_of = lane_iota(q.shape) // PER_FOCUS_WIDTH
    total = jnp.where(head_of == 0, mixed[:rows], 0.0)
    for h in range(1, FOCUS_NUMBER):
        total = jnp.where(head_of == h, mixed[h * rows : (h + 1) * rows], total)
    return total


def row_body(blk_ref, x_ref, q_ref, k_ref, v_ref, g_ref, final_ref, out_ref, wide, send, x_parts):
    devices = blk_ref.shape[0]
    put_parts(x_parts, x_ref[...])
    per_block = blk_ref.shape[1]
    half = wide.shape[1] // 2
    per_seq = 2 * devices
    wide[...] = blk_ref[...].astype(jnp.float32).reshape(wide.shape)
    mine = wide[pl.ds(lax.axis_index("dap") * per_block + FOCUS_NUMBER, 1), :]
    penalty = MASK_PENALTY_SCALE * (mine - 1.0)
    heads = [wide[pl.ds(h, devices, stride=per_block), :] for h in range(FOCUS_NUMBER)]
    for s in range(2):
        keys = k_ref[s * per_seq : (s + 1) * per_seq, :]
        values = v_ref[s * per_seq : (s + 1) * per_seq, :]
        for r in range(2):
            rows = pl.ds(s * per_seq + r, devices, stride=2)
            bias = jnp.concatenate([b[:, r * half : (r + 1) * half] for b in heads], axis=0)
            mixed = attend_heads(rows_of(q_ref, rows), keys, values, bias + penalty[:, s * half : (s + 1) * half])
            y = (mixed * rows_of(g_ref, rows)).astype(jnp.bfloat16)
            updated = rows_of(x_parts, rows) + dot_nn(y, final_ref[...])
            for part in range(updated.shape[1] // (2 * half)):
                to = pl.ds((s * 2 + r) * 2 + part, devices, stride=out_ref.shape[1])
                send[to, :] = updated[:, part * 2 * half : (part + 1) * 2 * half]
    out_ref[...] = send[...].reshape(out_ref.shape).astype(jnp.bfloat16)


def mask_block(blk_ref, wide):
    wide[...] = blk_ref[...].astype(jnp.float32).reshape(wide.shape)
    rows = pl.ds(FOCUS_NUMBER, blk_ref.shape[0], stride=blk_ref.shape[1])
    return wide[rows, :].astype(jnp.bfloat16)


def column_body(
    arrived_ref, blk_ref, small_ref, ask_ref, look_ref, final_ref, map_ref,
    msa_ref, opm_ref, wide, wide_blk, x_all, msa,
):
    devices = arrived_ref.shape[0]
    width = ask_ref.shape[1]
    lanes = wide.shape[1]
    half = lanes // 2
    seqs = 2 * devices
    me = lax.axis_index("dap")
    wide[...] = arrived_ref[...].astype(jnp.float32).reshape(wide.shape)
    for r in range(2):
        for s in range(2):
            base = (s * 2 + r) * 2
            at = (r * 2 + s) * devices
            for part in range(2):
                x_all[at : at + devices, part * lanes : (part + 1) * lanes] = wide[
                    pl.ds(base + part, devices, stride=8), :
                ]
    mask_lanes = mask_block(blk_ref, wide_blk)
    row = lax.broadcasted_iota(jnp.int32, (8, lanes), 0)
    wanted = (row % 2) * half + 2 * me + row // 2
    pick = jnp.where((lane_iota((8, lanes)) == wanted) & (row < 4), 1.0, 0.0).astype(jnp.bfloat16)
    picked = dot_nt(pick, mask_lanes)
    present = [
        jnp.concatenate([picked[2 * r : 2 * r + 1], picked[2 * r + 1 : 2 * r + 2]], axis=1)
        for r in range(2)
    ]
    x = x_all[...]
    normed = normed_rows(x, small_ref[COLUMN_GAIN : COLUMN_GAIN + 1]).astype(jnp.bfloat16)
    scaling = 1.0 / math.sqrt(PER_FOCUS_WIDTH)
    q = (dot_nn(normed, ask_ref[...]) * scaling).astype(jnp.bfloat16).astype(jnp.float32)
    others = dot_nn(normed, look_ref[...])
    keys = others[:, :width].astype(jnp.bfloat16)
    values = others[:, width : 2 * width].astype(jnp.bfloat16)
    gates = jax.nn.sigmoid(others[:, 2 * width :])
    mixed = jnp.concatenate(
        [
            attend_heads(
                q[r * seqs : (r + 1) * seqs],
                keys[r * seqs : (r + 1) * seqs],
                values[r * seqs : (r + 1) * seqs],
                MASK_PENALTY_SCALE * (present[r] - 1.0),
            )
            for r in range(2)
        ],
        axis=0,
    )
    updated = x + dot_nn((mixed * gates).astype(jnp.bfloat16), final_ref[...])
    for r in range(2):
        for s in range(2):
            at = (r * 2 + s) * devices
            for part in range(2):
                msa[r * 2 + part, pl.ds(s, devices, stride=2), :] = updated[
                    at : at + devices, part * lanes : (part + 1) * lanes
                ]
    for part in range(4):
        msa_ref[:, part * lanes : (part + 1) * lanes] = msa[part]
    normed = normed_rows(updated, small_ref[MEAN_GAIN : MEAN_GAIN + 1]).astype(jnp.bfloat16)
    sides = [
        dot_nt(map_ref[...], normed[r * seqs : (r + 1) * seqs]) * present[r] for r in range(2)
    ]
    block = jnp.concatenate(sides, axis=1).astype(jnp.bfloat16)
    opm_ref[...] = jnp.broadcast_to(block[None], opm_ref.shape)


def gated(projected, q_at, g_at, width):
    return jax.nn.sigmoid(projected[:, g_at : g_at + width]) * projected[:, q_at : q_at + width]


def presence_down(amino_row, half, lanes):
    square = lax.broadcasted_iota(jnp.int32, (half, half), 0) == lane_iota((half, half))
    diagonal = jnp.where(square, amino_row.astype(jnp.float32), 0.0).astype(jnp.bfloat16)
    return dot_nn(diagonal, jnp.ones((half, lanes), jnp.bfloat16))


def opm_body(steps, own_ref, oth_ref, *refs):
    couples, refs = refs[:steps], refs[steps:]
    (
        blk_ref, fin_ref, small_ref, flank_ref,
        pair_one_ref, normed_ref, right_ref,
        order, order16, outer, counts, mkeys, wide_blk,
    ) = refs
    chips, lanes, channels = pair_one_ref.shape
    hidden = outer.shape[1]
    half = lanes // 2
    me = lax.axis_index("dap")
    parity = lax.rem(me, 2)
    my_chip = me // 2
    for k in range(steps):
        for h in range(chips // steps):
            pair_one_ref[my_chip ^ (h * steps + k)] = couples[k][h].astype(jnp.float32)
    rows = (chips * hidden, lanes)
    order16[parity] = own_ref[:, hidden:, :].astype(jnp.float32).reshape(rows)
    order16[1 - parity] = oth_ref[:, hidden:, :].astype(jnp.float32).reshape(rows)
    early = lane_iota((chips, lanes)) < half
    for b in range(hidden):
        for p in range(2):
            rows = order16[p, pl.ds(b, chips, stride=hidden), :]
            turned = pltpu.roll(rows, half, 1)
            for r in range(2):
                for rj in range(2):
                    part = rows if r == rj else turned
                    part = jnp.where(early, 0.0, part) if r else jnp.where(early, part, 0.0)
                    order[pl.ds(b * lanes + r * half + 2 * p + rj, chips, stride=4), :] = part
    rights = order[...].astype(jnp.bfloat16)
    few = 4
    for q in range(chips // few):
        lhs = own_ref[q * few : (q + 1) * few, :hidden, :].reshape(few * hidden, lanes)
        outer[q * few : (q + 1) * few] = (
            dot_nt(lhs, rights).astype(jnp.bfloat16).reshape((few,) + outer.shape[1:])
        )
    mask_rows = mask_block(blk_ref, wide_blk)
    total = jnp.zeros((half, lanes), jnp.float32)
    for s in range(2):
        part = mask_rows[:, s * half : (s + 1) * half]
        total = total + dot_tn(part, jnp.concatenate([part, part], axis=1))
    counts[...] = 1.0 / jnp.maximum(total, 1.0)
    mkeys[...] = presence_down(small_ref[PRESENCE : PRESENCE + 1, :half], half, lanes)
    gain = small_ref[ENTRY_GAINS : ENTRY_GAINS + 1, :channels]
    low_row = lane_iota((1, lanes)) < half
    group = 16

    @pl.loop(0, chips // group)
    def _(block):
        pairs, keeps = [], []
        made = []
        for c in range(0, group, 2):
            sides = []
            for chip in (block * group + c, block * group + c + 1):
                strip = outer[chip]
                sides.append(
                    jnp.concatenate(
                        [strip[:, b * lanes : (b + 1) * lanes] for b in range(hidden)], axis=0
                    )
                )
            res = dot_nn(fin_ref[...], jnp.concatenate(sides, axis=1))
            made += [res[:, :lanes], res[:, lanes:]]
        for c in range(group):
            chip = block * group + c
            i0 = 4 * chip + 2 * parity
            share = jnp.where(low_row, counts[pl.ds(i0, 1), :], counts[pl.ds(i0 + 1, 1), :])
            pairs.append(jnp.transpose(made[c] * share) + pair_one_ref[chip])
            for r in range(2):
                keeps.append(mkeys[...] * mkeys[pl.ds(i0 + r, 1), :])
        pair = jnp.concatenate(pairs, axis=0)
        keep = jnp.concatenate(keeps, axis=0)
        normed = normed_rows(pair, gain).astype(jnp.bfloat16)
        projected = dot_nn(normed, flank_ref[0, :, 2 * channels :])
        right = gated(projected, 0, channels, channels) * keep
        for c in range(group):
            chip = block * group + c
            rows = slice(c * lanes, (c + 1) * lanes)
            pair_one_ref[chip] = pair[rows]
            normed_ref[chip] = normed[rows]
            right_ref[chip] = jnp.transpose(right[rows]).astype(jnp.bfloat16)


def left_body(normed_ref, small_ref, flank_ref, switch_ref, left_ref, gate_ref, mkeys):
    chips, lanes, channels = gate_ref.shape
    half = lanes // 2
    parity = lax.rem(lax.axis_index("dap"), 2)
    mkeys[...] = presence_down(small_ref[PRESENCE : PRESENCE + 1, :half], half, lanes)
    group = 8
    for block in range(chips // group):
        keeps = []
        for c in range(group):
            for r in range(2):
                keeps.append(mkeys[...] * mkeys[pl.ds(4 * (block * group + c) + 2 * parity + r, 1), :])
        normed = normed_ref[block * group : (block + 1) * group].reshape(group * lanes, channels)
        projected = dot_nn(normed, flank_ref[0, :, : 2 * channels])
        left = gated(projected, 0, channels, channels) * jnp.concatenate(keeps, axis=0)
        gate = jax.nn.sigmoid(dot_nn(normed, switch_ref[0]))
        for c in range(group):
            chip = block * group + c
            rows = slice(c * lanes, (c + 1) * lanes)
            gate_ref[chip] = gate[rows]
            left_ref[chip * channels : (chip + 1) * channels, :] = jnp.transpose(left[rows])


def outgoing_body(
    pair_one_ref, left_ref, gate_ref, own_ref, oth_ref, small_ref, final_ref, flank_ref,
    two_ref, send_ref,
    sides, prods, mkeys, pair_two, rows_out, cols,
):
    chips, channels, lanes = own_ref.shape
    half = lanes // 2
    me = lax.axis_index("dap")
    parity = lax.rem(me, 2)
    my_chip = me // 2
    flag = jnp.broadcast_to(parity, (1, 1)) == 0

    @pl.loop(0, chips)
    def _(chip):
        own = own_ref[chip].astype(jnp.float32)
        oth = oth_ref[chip].astype(jnp.float32)
        rows = pl.ds(pl.multiple_of(chip * channels, channels), channels)
        sides[0, rows, :] = jnp.where(flag, own, oth)
        sides[1, rows, :] = jnp.where(flag, oth, own)

    low = lane_iota((chips, lanes)) < half

    per_step = 64

    @pl.loop(0, channels // per_step)
    def _(step):
        for o in range(per_step // 8):
            base = step * per_step + o * 8
            left, even, odd = (
                jnp.swapaxes(
                    jnp.stack(
                        [
                            ref[pl.ds(pl.multiple_of(chip * channels + base, 8), 8), :]
                            for chip in range(chips)
                        ]
                    ),
                    0,
                    1,
                )
                for ref in (left_ref, sides.at[0], sides.at[1])
            )
            for c in range(8):
                lhs = jnp.concatenate(
                    [jnp.where(low, left[c], 0.0), jnp.where(low, 0.0, left[c])], axis=0
                )
                rhs = jnp.concatenate(
                    [even[c], pltpu.roll(even[c], half, 1), odd[c], pltpu.roll(odd[c], half, 1)],
                    axis=0,
                )
                out = dot_nt(lhs.astype(jnp.bfloat16), rhs.astype(jnp.bfloat16))
                out = jnp.concatenate([out[:chips], out[chips:]], axis=1)
                to = pl.ds(base + c, chips, stride=channels)
                prods[to, :] = out.astype(jnp.bfloat16).astype(jnp.float32)

    mkeys[...] = presence_down(small_ref[PRESENCE : PRESENCE + 1, :half], half, channels)
    gain_mid = small_ref[MID_GAINS : MID_GAINS + 1, :channels]
    gain_mid = jnp.transpose(jnp.broadcast_to(gain_mid, (channels, channels)))
    final_t = jnp.transpose(final_ref[0].astype(jnp.float32)).astype(jnp.bfloat16)
    gain = small_ref[ENTRY_GAINS : ENTRY_GAINS + 1, channels : 2 * channels]
    flank_right = flank_ref[1, :, 2 * channels :]
    flank_left = flank_ref[1, :, : 2 * channels]
    octet = pl.multiple_of(8 * (my_chip // 2), 8)
    group = 8
    for block in range(chips // group):
        changed = []
        for c in range(group):
            x = prods[(block * group + c) * channels : (block * group + c + 1) * channels, :]
            centred = x - jnp.mean(x, axis=0, keepdims=True)
            spread = jnp.mean(centred * centred, axis=0, keepdims=True)
            changed.append((centred * lax.rsqrt(spread + EPSILON) * gain_mid).astype(jnp.bfloat16))
        changed = dot_nn(final_t, jnp.concatenate(changed, axis=1))
        for c in range(group):
            part = jnp.transpose(changed[:, c * lanes : (c + 1) * lanes])
            for k in range(8):
                r, p = k // 4, (k // 2) % 2
                rj = k % 2 if r == 0 else 1 - k % 2
                rows_out[block * group + c, pl.ds(r * half + 2 * p + rj, chips, stride=4), :] = part[
                    k * chips : (k + 1) * chips
                ]
        twos, keeps = [], []
        for c in range(group):
            chip = block * group + c
            two = pair_one_ref[chip] + rows_out[chip] * gate_ref[chip]
            twos.append(two)
            for r in range(2):
                keeps.append(mkeys[pl.ds(4 * chip + 2 * parity + r, 1), :])
        two = jnp.concatenate(twos, axis=0)
        full = normed_rows(two, gain)
        normed = full.astype(jnp.bfloat16)
        keep = jnp.concatenate([mkeys[...] * m for m in keeps], axis=0)
        going = (gated(dot_nn(normed, flank_right), 0, channels, channels) * keep).astype(jnp.bfloat16)
        cols[block] = full
        few = jnp.concatenate(
            [cols[block, pl.ds(k * half + octet, 8), :] for k in range(2 * group)], axis=0
        ).astype(jnp.bfloat16)
        mine = mkeys[pl.ds(octet, 8), :]
        keep = jnp.concatenate([mine * m for m in keeps], axis=0)
        few = (gated(dot_nn(few, flank_left), 0, channels, channels) * keep).astype(jnp.bfloat16)
        for c in range(group):
            chip = block * group + c
            pair_two[chip] = twos[c]
            send_ref[chip, :lanes, :] = going[c * lanes : (c + 1) * lanes]
            send_ref[chip, lanes:, :] = few[c * 16 : (c + 1) * 16]
    two_ref[...] = pair_two[my_chip]


def add_products(side_ref, tails, totals):
    chips = side_ref.shape[0]
    half, _ = totals[0].shape
    lanes = 2 * half
    me = lax.axis_index("dap")
    first = 4 * lax.rem(me // 2, 2) + 2 * lax.rem(me, 2)
    tails[...] = side_ref[:, lanes:, :].astype(jnp.float32).reshape(tails.shape)
    ahead = 4

    def step(block, totals):
        totals = list(totals)
        for c in range(ahead):
            chip = block * ahead + c
            for k in range(2):
                there = side_ref[chip, k * half : (k + 1) * half, :].astype(jnp.float32)
                for i in range(2):
                    one = tails[pl.ds(chip * 16 + 8 * k + first + i, 1), :]
                    totals[i] = totals[i] + one * there
        return tuple(totals)

    return lax.fori_loop(0, chips // ahead, step, tuple(totals))


def incoming_own_body(own_ref, two_ref, couple_ref, small_ref, switch_ref, sums_ref, kept_ref, gate_ref, tails):
    lanes, channels = two_ref.shape
    half = lanes // 2
    zero = jnp.zeros((half, channels), jnp.float32)
    sums_ref[...] = jnp.concatenate(add_products(own_ref, tails, (zero, zero)), axis=0)
    two = two_ref[...]
    gain = small_ref[ENTRY_GAINS : ENTRY_GAINS + 1, channels : 2 * channels]
    normed = normed_rows(two, gain).astype(jnp.bfloat16)
    gate_ref[...] = jax.nn.sigmoid(dot_nn(normed, switch_ref[1]))
    couple = couple_ref[...]
    kept_ref[...] = two + (couple - couple.astype(jnp.bfloat16).astype(jnp.float32))


def incoming_body(oth_ref, sums_ref, kept_ref, gate_ref, small_ref, final_ref, out_ref, tails):
    lanes, channels = out_ref.shape
    half = lanes // 2
    prod = jnp.concatenate(
        add_products(oth_ref, tails, (sums_ref[:half, :], sums_ref[half:, :])), axis=0
    )
    prod = prod.astype(jnp.bfloat16).astype(jnp.float32)
    gain_mid = small_ref[MID_GAINS : MID_GAINS + 1, channels : 2 * channels]
    changed = dot_nn(normed_rows(prod, gain_mid).astype(jnp.bfloat16), final_ref[1])
    out_ref[...] = kept_ref[...] + changed * gate_ref[...]


def gather_by_steps(block, chips):
    bits = chips.bit_length() - 1
    steps = 1 << (bits // 2)
    devices = 2 * chips

    def fetch(value, apart):
        return lax.ppermute(value, "dap", [(d, d ^ (2 * apart)) for d in range(devices)])

    parts = [fetch(block, h * steps) for h in range(1, chips // steps)]
    near = jnp.concatenate([block] + parts, axis=0)
    return near, [fetch(near, k) for k in range(1, steps)]


def paired_shards(
    homolog_stack,
    couple_tensor,
    homolog_presence,
    amino_presence,
    horizontal_standard_factor,
    horizontal_asking_matrix,
    horizontal_lookup_triple,
    horizontal_final_matrix,
    couple_offset_factor,
    couple_offset_matrix,
    vertical_standard_factor,
    vertical_asking_matrix,
    vertical_lookup_triple,
    vertical_final_matrix,
    tensor_average_factor,
    tensor_average_mapping,
    tensor_average_final,
    trio_entry_factors,
    trio_flank_mappings,
    trio_final_switches,
    trio_multiplied_factors,
    trio_final_matrices,
):
    devices = lax.axis_size("dap")
    chips = devices // 2
    strands, aminos, features = homolog_stack.shape
    rows, _, channels = couple_tensor.shape
    lanes = rows * aminos
    heads = FOCUS_NUMBER
    hidden = TENSOR_HIDDEN
    f32, bf16 = jnp.float32, jnp.bfloat16
    shape = jax.ShapeDtypeStruct
    same_parity = [[2 * chip + p for chip in range(chips)] for p in range(2)]
    swap = [(d, d ^ 1) for d in range(devices)]

    def line(v):
        return v.reshape(1, -1)

    couple = couple_tensor.reshape(lanes, channels)
    x = homolog_stack.reshape(strands * aminos, features)
    block, near = vmem_call(
        bias_body,
        (shape((devices, 16, lanes), bf16), shape((1, lanes, channels), bf16)),
        scratch=[
            pltpu.VMEM((lanes, channels), f32),
            pltpu.VMEM((1, channels), f32),
            pltpu.VMEM((heads, channels), bf16),
            pltpu.VMEM((strands, aminos), jnp.int32),
            pltpu.SemaphoreType.DMA((4,)),
        ],
        count=4,
        away=range(4),
        grant=60 << 20,
    )(couple, line(couple_offset_factor), couple_offset_matrix.T, homolog_presence)
    blocks = lax.all_to_all(block, "dap", split_axis=0, concat_axis=0, tiled=True)
    small = jnp.concatenate(
        [
            line(horizontal_standard_factor),
            line(vertical_standard_factor),
            line(tensor_average_factor),
            line(trio_entry_factors),
            line(trio_multiplied_factors),
            jnp.pad(line(amino_presence.astype(f32)), ((0, 0), (0, features - aminos))),
            jnp.zeros((2, features), f32),
        ],
        axis=0,
    )
    final = jnp.transpose(
        tensor_average_final.reshape(hidden, hidden, channels), (2, 1, 0)
    ).reshape(channels, hidden * hidden)
    q, k, v, g = vmem_call(
        project_body,
        (
            shape((features // lanes, lanes, lanes), f32),
            shape((lanes, features), bf16),
            shape((lanes, features), bf16),
            shape((features // lanes, lanes, lanes), f32),
        ),
        count=4,
    )(x, small, horizontal_asking_matrix, horizontal_lookup_triple)
    near, fars = gather_by_steps(near, chips)
    couples = [near, *fars]
    sent = vmem_call(
        row_body,
        shape((devices, 8, lanes), bf16),
        scratch=[
            pltpu.VMEM((devices * 16, lanes), f32),
            pltpu.VMEM((devices * 8, lanes), f32),
            pltpu.VMEM((features // lanes, lanes, lanes), f32),
        ],
        count=7,
    )(blocks, x, q, k, v, g, horizontal_final_matrix)
    arrived = lax.all_to_all(sent, "dap", split_axis=0, concat_axis=0, tiled=True)
    msa, opm = vmem_call(
        column_body,
        (shape((devices * strands, rows * features), f32), shape((chips, 2 * hidden, lanes), bf16)),
        scratch=[
            pltpu.VMEM((devices * 8, lanes), f32),
            pltpu.VMEM((devices * 16, lanes), f32),
            pltpu.VMEM((lanes, features), f32),
            pltpu.VMEM((4, devices * strands, lanes), f32),
        ],
        count=7,
        later=1,
    )(
        arrived,
        blocks,
        small,
        vertical_asking_matrix,
        vertical_lookup_triple,
        vertical_final_matrix,
        tensor_average_mapping.T,
        final,
    )
    opm_own = lax.all_to_all(
        opm, "dap", split_axis=0, concat_axis=0, tiled=True, axis_index_groups=same_parity
    )
    opm_oth = lax.ppermute(opm_own, "dap", swap)
    msa = msa.reshape(devices * strands, rows, features)
    stack = (chips, lanes, channels)
    pair_one, normed, right_own = vmem_call(
        functools.partial(opm_body, len(couples)),
        (shape(stack, f32), shape(stack, bf16), shape(stack, bf16)),
        scratch=[
            pltpu.VMEM((hidden * lanes, lanes), f32),
            pltpu.VMEM((2, chips * hidden, lanes), f32),
            pltpu.VMEM((chips, hidden, hidden * lanes), bf16),
            pltpu.VMEM((aminos, lanes), f32),
            pltpu.VMEM((aminos, channels), f32),
            pltpu.VMEM((devices * 16, lanes), f32),
        ],
        count=len(couples) + 6,
        later=1,
    )(
        opm_own,
        opm_oth,
        *couples,
        blocks,
        final,
        small,
        trio_flank_mappings,
        msa,
    )
    right_oth = lax.ppermute(right_own, "dap", swap)
    left, gate = vmem_call(
        left_body,
        (shape((chips * channels, lanes), f32), shape(stack, f32)),
        scratch=[pltpu.VMEM((aminos, channels), f32)],
        count=4,
    )(normed, small, trio_flank_mappings, trio_final_switches)
    two, going = vmem_call(
        outgoing_body,
        (shape((lanes, channels), f32), shape((chips, lanes + 16, channels), bf16)),
        scratch=[
            pltpu.VMEM((2, chips * channels, lanes), f32),
            pltpu.VMEM((channels * chips, lanes), f32),
            pltpu.VMEM((aminos, channels), f32),
            pltpu.VMEM(stack, f32),
            pltpu.VMEM(stack, f32),
            pltpu.VMEM((chips // 8, 8 * lanes, channels), f32),
        ],
        count=8,
    )(
        pair_one,
        left,
        gate,
        right_own,
        right_oth,
        small,
        trio_final_matrices,
        trio_flank_mappings,
    )
    coming = lax.ppermute(going, "dap", swap)
    own_rows = shape((lanes, channels), f32)
    tails = [pltpu.VMEM((chips * 16, channels), f32)]
    sums, kept, gate = vmem_call(
        incoming_own_body, (own_rows,) * 3, scratch=tails, count=5
    )(going, two, couple, small, trio_final_switches)
    pair_out = vmem_call(incoming_body, own_rows, scratch=tails, count=6)(
        coming, sums, kept, gate, small, trio_final_matrices
    )
    return msa, pair_out.reshape(rows, aminos, channels)


def fits_pairs(homolog_stack, couple_tensor, devices):
    strands, aminos, features = homolog_stack.shape
    rows, _, channels = couple_tensor.shape
    lanes = 128
    return (
        strands == rows == 2
        and devices % 8 == 0
        and devices & (devices - 1) == 0
        and rows * aminos == lanes == channels
        and aminos == 2 * devices
        and features == 2 * lanes
    )


def either(*arrays):
    if fits_pairs(arrays[0], arrays[1], lax.axis_size("dap")):
        return paired_shards(*arrays)
    return shards(*arrays)


def solution(mesh):
    placed = (
        P("dap", None, None),
        P("dap", None, None),
        P("dap", None),
        P(),
        P(),
        P(),
        P(),
        P(),
        P(),
        P(),
        P(),
        P(),
        P(),
        P(),
        P(),
        P(),
        P(),
        P(),
        P(),
        P(),
        P(),
        P(),
    )
    return jax.shard_map(
        either,
        mesh=mesh,
        in_specs=placed,
        out_specs=(P(None, "dap", None), P("dap", None, None)),
        check_vma=False,
    )
```

```python
import functools
import math

import jax
import jax.numpy as jnp
from jax import lax
from jax.experimental import pallas as pl
from jax.experimental.pallas import tpu as pltpu
from jax.sharding import PartitionSpec as P

FOCUS_NUMBER = 8
PER_FOCUS_WIDTH = 32
TENSOR_HIDDEN = 32
TRI_HID = 128


EPSILON = 1e-05
MASK_PENALTY_SCALE = 1000000000.0


def standardize_features(content_vectors, gain, axis):
    centred = content_vectors - jnp.mean(content_vectors, axis=axis, keepdims=True)
    spread = jnp.mean(centred * centred, axis=axis, keepdims=True)
    return centred * lax.rsqrt(spread + EPSILON) * gain


def gather_blocks(block):
    device_count = lax.axis_size("dap")
    copies = jnp.broadcast_to(block[None], (device_count,) + block.shape)
    return lax.all_to_all(copies, "dap", split_axis=0, concat_axis=0, tiled=True)


def triangle(
    pair_now, gain_in, proj_weight, gate_weight, gain_mid, final_weight, amino_presence, incoming
):
    hidden = TRI_HID
    row_count = pair_now.shape[0]
    my_index = lax.axis_index("dap")
    standardized_source = standardize_features(pair_now, gain_in, -1).astype(jnp.bfloat16)
    projected = jnp.einsum(
        "rkd,de->erk", standardized_source, proj_weight, preferred_element_type=jnp.float32
    )
    res_float = amino_presence.astype(jnp.float32)
    own_rows = lax.dynamic_slice_in_dim(res_float, my_index * row_count, row_count)
    pair_mask = own_rows[:, None] * res_float[None, :]
    left_side = (
        jax.nn.sigmoid(projected[hidden : 2 * hidden]) * projected[:hidden] * pair_mask[None]
    ).astype(jnp.bfloat16)
    right_side = (
        jax.nn.sigmoid(projected[3 * hidden :])
        * projected[2 * hidden : 3 * hidden]
        * pair_mask[None]
    ).astype(jnp.bfloat16)
    gating = jax.nn.sigmoid(
        jnp.dot(standardized_source, gate_weight, preferred_element_type=jnp.float32)
    )
    device_count = lax.axis_size("dap")
    per_device = hidden // device_count
    both = jnp.stack(
        [
            left_side.reshape(device_count, per_device, row_count, -1),
            right_side.reshape(device_count, per_device, row_count, -1),
        ],
        axis=1,
    )
    both = lax.all_to_all(both, "dap", split_axis=0, concat_axis=0, tiled=True)
    both = jnp.moveaxis(both, 0, 2).reshape(2, per_device, device_count * row_count, -1)
    left_chan, right_chan = both[0], both[1]
    if incoming:
        product = jnp.einsum(
            "cki,ckj->cij", left_chan, right_chan, preferred_element_type=jnp.float32
        )
    else:
        product = jnp.einsum(
            "cik,cjk->cij", left_chan, right_chan, preferred_element_type=jnp.float32
        )
    product = product.astype(jnp.bfloat16)
    returned = lax.all_to_all(product, "dap", split_axis=1, concat_axis=0, tiled=True)
    product_normed = standardize_features(
        returned.astype(jnp.float32), gain_mid[:, None, None], 0
    ).astype(jnp.bfloat16)
    update = jnp.einsum(
        "crj,cd->rjd", product_normed, final_weight, preferred_element_type=jnp.float32
    )
    return pair_now + update * gating


def shards(
    homolog_stack,
    couple_tensor,
    homolog_presence,
    amino_presence,
    horizontal_standard_factor,
    horizontal_asking_matrix,
    horizontal_lookup_triple,
    horizontal_final_matrix,
    couple_offset_factor,
    couple_offset_matrix,
    vertical_standard_factor,
    vertical_asking_matrix,
    vertical_lookup_triple,
    vertical_final_matrix,
    tensor_average_factor,
    tensor_average_mapping,
    tensor_average_final,
    trio_entry_factors,
    trio_flank_mappings,
    trio_final_switches,
    trio_multiplied_factors,
    trio_final_matrices,
):
    nested_function = FOCUS_NUMBER * PER_FOCUS_WIDTH
    scaling = 1.0 / math.sqrt(PER_FOCUS_WIDTH)
    strand_portion = homolog_stack.shape[0]
    amino_total = homolog_stack.shape[1]
    row_count = couple_tensor.shape[0]
    pair_normed = standardize_features(couple_tensor, couple_offset_factor, -1).astype(jnp.bfloat16)
    bias_local = jnp.einsum(
        "rjc,ch->hrj", pair_normed, couple_offset_matrix, preferred_element_type=jnp.float32
    ).astype(jnp.bfloat16)
    standardized_source = standardize_features(
        homolog_stack, horizontal_standard_factor, -1
    ).astype(jnp.bfloat16)
    shaped = (strand_portion, amino_total, FOCUS_NUMBER, PER_FOCUS_WIDTH)
    queries = (
        (
            jnp.dot(
                standardized_source, horizontal_asking_matrix, preferred_element_type=jnp.float32
            )
            * scaling
        )
        .astype(jnp.bfloat16)
        .reshape(shaped)
    )
    others = jnp.dot(
        standardized_source, horizontal_lookup_triple, preferred_element_type=jnp.float32
    )
    keys_all = others[..., :nested_function].astype(jnp.bfloat16).reshape(shaped)
    content_entire = (
        others[..., nested_function : 2 * nested_function].astype(jnp.bfloat16).reshape(shaped)
    )
    sigmoid_switches = jax.nn.sigmoid(others[..., 2 * nested_function :])
    mask_penalty = MASK_PENALTY_SCALE * (homolog_presence.astype(jnp.float32) - 1.0)

    def attend(bias_piece):
        query_rows = bias_piece.shape[1]
        scores = jnp.einsum(
            "sihc,sjhc->shij", queries, keys_all, preferred_element_type=jnp.float32
        )
        scores = scores + bias_piece.astype(jnp.float32)[None] + mask_penalty[:, None, None, :]
        softmax_probabilities = jax.nn.softmax(scores, axis=-1).astype(jnp.bfloat16)
        mixed = jnp.einsum(
            "shij,sjhc->sihc",
            softmax_probabilities,
            content_entire,
            preferred_element_type=jnp.float32,
        )
        return mixed.reshape(strand_portion, query_rows, nested_function)

    bias_whole = jnp.moveaxis(gather_blocks(bias_local), 0, 1).reshape(
        FOCUS_NUMBER, amino_total, amino_total
    )
    block_rows = math.gcd(amino_total, 256)

    def one_block(block_index):
        return attend(bias_whole)

    blocks = lax.map(one_block, jnp.arange(amino_total // block_rows, dtype=jnp.int32))
    focused_content = jnp.moveaxis(blocks, 0, 1).reshape(
        strand_portion, amino_total, nested_function
    )
    homolog_stack_horizontal = homolog_stack + jnp.dot(
        (focused_content * sigmoid_switches).astype(jnp.bfloat16),
        horizontal_final_matrix,
        preferred_element_type=jnp.float32,
    )
    travelling = jnp.concatenate(
        [
            homolog_stack_horizontal.astype(jnp.bfloat16),
            jnp.broadcast_to(
                homolog_presence.astype(jnp.bfloat16)[..., None],
                (strand_portion, amino_total, 128),
            ),
        ],
        axis=-1,
    )
    arrived = lax.all_to_all(travelling, "dap", split_axis=1, concat_axis=0, tiled=True)
    column_view = arrived[..., :nested_function].astype(jnp.float32)
    col_mask = arrived[..., nested_function].astype(jnp.float32)
    seq_total = column_view.shape[0]
    col_shape = (seq_total, row_count, FOCUS_NUMBER, PER_FOCUS_WIDTH)
    standardized_source = standardize_features(column_view, vertical_standard_factor, -1).astype(
        jnp.bfloat16
    )
    col_queries = (
        (
            jnp.dot(standardized_source, vertical_asking_matrix, preferred_element_type=jnp.float32)
            * scaling
        )
        .astype(jnp.bfloat16)
        .reshape(col_shape)
    )
    col_others = jnp.dot(
        standardized_source, vertical_lookup_triple, preferred_element_type=jnp.float32
    )
    col_keys = col_others[..., :nested_function].astype(jnp.bfloat16).reshape(col_shape)
    col_values = (
        col_others[..., nested_function : 2 * nested_function]
        .astype(jnp.bfloat16)
        .reshape(col_shape)
    )
    col_gates = jax.nn.sigmoid(col_others[..., 2 * nested_function :])
    col_penalty = MASK_PENALTY_SCALE * (col_mask - 1.0)
    scores = jnp.einsum(
        "sihc,tihc->ihst", col_queries, col_keys, preferred_element_type=jnp.float32
    )
    scores = scores + jnp.transpose(col_penalty)[:, None, None, :]
    softmax_probabilities = jax.nn.softmax(scores, axis=-1).astype(jnp.bfloat16)
    col_mixed = jnp.einsum(
        "uovg,guox->vuox", softmax_probabilities, col_values, preferred_element_type=jnp.float32
    ).reshape(seq_total, row_count, nested_function)
    alignment_after_columns = column_view + jnp.dot(
        (col_mixed * col_gates).astype(jnp.bfloat16),
        vertical_final_matrix,
        preferred_element_type=jnp.float32,
    )
    standardized_source = standardize_features(
        alignment_after_columns, tensor_average_factor, -1
    ).astype(jnp.bfloat16)
    halves = jnp.dot(
        standardized_source, tensor_average_mapping, preferred_element_type=jnp.float32
    )
    left_proj = (halves[..., :TENSOR_HIDDEN] * col_mask[..., None]).astype(jnp.bfloat16)
    right_proj = (halves[..., TENSOR_HIDDEN:] * col_mask[..., None]).astype(jnp.bfloat16)
    block = jnp.concatenate(
        [right_proj, col_mask.astype(jnp.bfloat16)[..., None]], axis=-1
    )
    block = jnp.transpose(block, (1, 2, 0))
    whole = gather_blocks(block).reshape(amino_total, TENSOR_HIDDEN + 1, seq_total)
    right_whole = jnp.transpose(whole[:, :TENSOR_HIDDEN], (2, 0, 1))
    mask_whole = jnp.transpose(whole[:, TENSOR_HIDDEN])
    outer = jnp.einsum("sra,sjb->rjab", left_proj, right_whole, preferred_element_type=jnp.float32)
    outer = outer.astype(jnp.bfloat16).reshape(
        row_count, amino_total, TENSOR_HIDDEN * TENSOR_HIDDEN
    )
    counts = jnp.dot(
        jnp.transpose(col_mask), mask_whole.astype(jnp.float32), precision=lax.Precision.HIGHEST
    )
    product = (
        jnp.dot(outer, tensor_average_final, preferred_element_type=jnp.float32)
        / jnp.maximum(counts, 1.0)[..., None]
    )
    pair_one = couple_tensor + product
    pair_two = triangle(
        pair_one,
        trio_entry_factors[0],
        trio_flank_mappings[0],
        trio_final_switches[0],
        trio_multiplied_factors[0],
        trio_final_matrices[0],
        amino_presence,
        False,
    )
    pair_after_incoming = triangle(
        pair_two,
        trio_entry_factors[1],
        trio_flank_mappings[1],
        trio_final_switches[1],
        trio_multiplied_factors[1],
        trio_final_matrices[1],
        amino_presence,
        True,
    )
    return (alignment_after_columns, pair_after_incoming)


def normed_rows(x, gain):
    centred = x - jnp.mean(x, axis=-1, keepdims=True)
    spread = jnp.mean(centred * centred, axis=-1, keepdims=True)
    return centred * lax.rsqrt(spread + EPSILON) * gain


def dot_nn(a, b):
    return lax.dot_general(a, b, (((1,), (0,)), ((), ())), preferred_element_type=jnp.float32)


def dot_nt(a, b):
    return lax.dot_general(a, b, (((1,), (1,)), ((), ())), preferred_element_type=jnp.float32)


def dot_tn(a, b):
    return lax.dot_general(a, b, (((0,), (0,)), ((), ())), preferred_element_type=jnp.float32)


def lane_iota(shape):
    return lax.broadcasted_iota(jnp.int32, shape, len(shape) - 1)


def vmem_call(body, outs, scratch=(), count=0, later=0, away=(), grant=20 << 20):
    whole = pl.BlockSpec(memory_space=pltpu.VMEM)
    there = pl.BlockSpec(memory_space=pl.ANY)
    hbm = pl.BlockSpec(memory_space=pltpu.HBM)

    def reader(*refs):
        body(*refs[:count], *refs[count + later :])

    return pl.pallas_call(
        reader,
        out_shape=outs,
        in_specs=[hbm if k in away else whole for k in range(count)] + [there] * later,
        out_specs=jax.tree.map(lambda _: whole, outs),
        scratch_shapes=list(scratch),
        compiler_params=pltpu.CompilerParams(vmem_limit_bytes=grant),
    )


ROW_GAIN, COLUMN_GAIN, MEAN_GAIN, ENTRY_GAINS, MID_GAINS, PRESENCE = range(6)


def bias_body(pair_at, gain_at, weight_at, present_at, out_ref, near_ref, pair, gain, weight, present, sems):
    moves = [
        pltpu.make_async_copy(there, here, sems.at[k])
        for k, (there, here) in enumerate(
            ((pair_at, pair), (gain_at, gain), (weight_at, weight), (present_at, present))
        )
    ]
    for move in moves:
        move.start()
    for move in moves:
        move.wait()
    near_ref[0] = pair[...].astype(jnp.bfloat16)
    normed = normed_rows(pair[...], gain[...]).astype(jnp.bfloat16)
    bias = dot_nt(weight[...], normed)
    here = present[...].astype(jnp.float32)
    mask_row = jnp.concatenate([here[0:1], here[1:2]], axis=1)
    fill = jnp.zeros((out_ref.shape[1] - bias.shape[0] - 1, bias.shape[1]), jnp.float32)
    block = jnp.concatenate([bias, mask_row, fill], axis=0).astype(jnp.bfloat16)
    out_ref[...] = jnp.broadcast_to(block[None], out_ref.shape)


def put_parts(ref, value):
    lanes = ref.shape[2]
    for part in range(ref.shape[0]):
        ref[part] = value[:, part * lanes : (part + 1) * lanes]


def rows_of(ref, rows):
    return jnp.concatenate([ref[part, rows, :] for part in range(ref.shape[0])], axis=1)


def project_body(x_ref, small_ref, ask_ref, look_ref, q_ref, k_ref, v_ref, g_ref):
    width = ask_ref.shape[1]
    normed = normed_rows(x_ref[...], small_ref[ROW_GAIN : ROW_GAIN + 1]).astype(jnp.bfloat16)
    scaling = 1.0 / math.sqrt(PER_FOCUS_WIDTH)
    q = (dot_nn(normed, ask_ref[...]) * scaling).astype(jnp.bfloat16).astype(jnp.float32)
    put_parts(q_ref, q)
    others = dot_nn(normed, look_ref[...])
    k_ref[...] = others[:, :width].astype(jnp.bfloat16)
    v_ref[...] = others[:, width : 2 * width].astype(jnp.bfloat16)
    put_parts(g_ref, jax.nn.sigmoid(others[:, 2 * width :]))


def head_spread(q):
    head_of = lane_iota(q.shape) // PER_FOCUS_WIDTH
    return jnp.concatenate(
        [jnp.where(head_of == h, q, 0.0) for h in range(FOCUS_NUMBER)], axis=0
    ).astype(jnp.bfloat16)


def attend_heads(q, k, v, offset):
    scores = dot_nt(head_spread(q), k) + offset
    scores = scores - jnp.max(scores, axis=-1, keepdims=True)
    raised = jnp.exp(scores)
    shares = (raised / jnp.sum(raised, axis=-1, keepdims=True)).astype(jnp.bfloat16)
    mixed = dot_nn(shares, v)
    rows = q.shape[0]
    head_of = lane_iota(q.shape) // PER_FOCUS_WIDTH
    total = jnp.where(head_of == 0, mixed[:rows], 0.0)
    for h in range(1, FOCUS_NUMBER):
        total = jnp.where(head_of == h, mixed[h * rows : (h + 1) * rows], total)
    return total


def row_body(blk_ref, x_ref, q_ref, k_ref, v_ref, g_ref, final_ref, out_ref, wide, send, x_parts):
    devices = blk_ref.shape[0]
    put_parts(x_parts, x_ref[...])
    per_block = blk_ref.shape[1]
    half = wide.shape[1] // 2
    per_seq = 2 * devices
    wide[...] = blk_ref[...].astype(jnp.float32).reshape(wide.shape)
    mine = wide[pl.ds(lax.axis_index("dap") * per_block + FOCUS_NUMBER, 1), :]
    penalty = MASK_PENALTY_SCALE * (mine - 1.0)
    heads = [wide[pl.ds(h, devices, stride=per_block), :] for h in range(FOCUS_NUMBER)]
    for s in range(2):
        keys = k_ref[s * per_seq : (s + 1) * per_seq, :]
        values = v_ref[s * per_seq : (s + 1) * per_seq, :]
        for r in range(2):
            rows = pl.ds(s * per_seq + r, devices, stride=2)
            bias = jnp.concatenate([b[:, r * half : (r + 1) * half] for b in heads], axis=0)
            mixed = attend_heads(rows_of(q_ref, rows), keys, values, bias + penalty[:, s * half : (s + 1) * half])
            y = (mixed * rows_of(g_ref, rows)).astype(jnp.bfloat16)
            updated = rows_of(x_parts, rows) + dot_nn(y, final_ref[...])
            for part in range(updated.shape[1] // (2 * half)):
                to = pl.ds((s * 2 + r) * 2 + part, devices, stride=out_ref.shape[1])
                send[to, :] = updated[:, part * 2 * half : (part + 1) * 2 * half]
    out_ref[...] = send[...].reshape(out_ref.shape).astype(jnp.bfloat16)


def mask_block(blk_ref, wide):
    wide[...] = blk_ref[...].astype(jnp.float32).reshape(wide.shape)
    rows = pl.ds(FOCUS_NUMBER, blk_ref.shape[0], stride=blk_ref.shape[1])
    return wide[rows, :].astype(jnp.bfloat16)


def column_body(
    arrived_ref, blk_ref, small_ref, ask_ref, look_ref, final_ref, map_ref,
    msa_ref, opm_ref, wide, wide_blk, x_all, msa,
):
    devices = arrived_ref.shape[0]
    width = ask_ref.shape[1]
    lanes = wide.shape[1]
    half = lanes // 2
    seqs = 2 * devices
    me = lax.axis_index("dap")
    wide[...] = arrived_ref[...].astype(jnp.float32).reshape(wide.shape)
    for r in range(2):
        for s in range(2):
            base = (s * 2 + r) * 2
            at = (r * 2 + s) * devices
            for part in range(2):
                x_all[at : at + devices, part * lanes : (part + 1) * lanes] = wide[
                    pl.ds(base + part, devices, stride=8), :
                ]
    mask_lanes = mask_block(blk_ref, wide_blk)
    row = lax.broadcasted_iota(jnp.int32, (8, lanes), 0)
    wanted = (row % 2) * half + 2 * me + row // 2
    pick = jnp.where((lane_iota((8, lanes)) == wanted) & (row < 4), 1.0, 0.0).astype(jnp.bfloat16)
    picked = dot_nt(pick, mask_lanes)
    present = [
        jnp.concatenate([picked[2 * r : 2 * r + 1], picked[2 * r + 1 : 2 * r + 2]], axis=1)
        for r in range(2)
    ]
    x = x_all[...]
    normed = normed_rows(x, small_ref[COLUMN_GAIN : COLUMN_GAIN + 1]).astype(jnp.bfloat16)
    scaling = 1.0 / math.sqrt(PER_FOCUS_WIDTH)
    q = (dot_nn(normed, ask_ref[...]) * scaling).astype(jnp.bfloat16).astype(jnp.float32)
    others = dot_nn(normed, look_ref[...])
    keys = others[:, :width].astype(jnp.bfloat16)
    values = others[:, width : 2 * width].astype(jnp.bfloat16)
    gates = jax.nn.sigmoid(others[:, 2 * width :])
    mixed = jnp.concatenate(
        [
            attend_heads(
                q[r * seqs : (r + 1) * seqs],
                keys[r * seqs : (r + 1) * seqs],
                values[r * seqs : (r + 1) * seqs],
                MASK_PENALTY_SCALE * (present[r] - 1.0),
            )
            for r in range(2)
        ],
        axis=0,
    )
    updated = x + dot_nn((mixed * gates).astype(jnp.bfloat16), final_ref[...])
    for r in range(2):
        for s in range(2):
            at = (r * 2 + s) * devices
            for part in range(2):
                msa[r * 2 + part, pl.ds(s, devices, stride=2), :] = updated[
                    at : at + devices, part * lanes : (part + 1) * lanes
                ]
    for part in range(4):
        msa_ref[:, part * lanes : (part + 1) * lanes] = msa[part]
    normed = normed_rows(updated, small_ref[MEAN_GAIN : MEAN_GAIN + 1]).astype(jnp.bfloat16)
    sides = [
        dot_nt(map_ref[...], normed[r * seqs : (r + 1) * seqs]) * present[r] for r in range(2)
    ]
    block = jnp.concatenate(sides, axis=1).astype(jnp.bfloat16)
    opm_ref[...] = jnp.broadcast_to(block[None], opm_ref.shape)


def gated(projected, q_at, g_at, width):
    return jax.nn.sigmoid(projected[:, g_at : g_at + width]) * projected[:, q_at : q_at + width]


def presence_down(amino_row, half, lanes):
    square = lax.broadcasted_iota(jnp.int32, (half, half), 0) == lane_iota((half, half))
    diagonal = jnp.where(square, amino_row.astype(jnp.float32), 0.0).astype(jnp.bfloat16)
    return dot_nn(diagonal, jnp.ones((half, lanes), jnp.bfloat16))


def opm_body(steps, own_ref, oth_ref, *refs):
    couples, refs = refs[:steps], refs[steps:]
    (
        blk_ref, fin_ref, small_ref, flank_ref,
        pair_one_ref, normed_ref, right_ref,
        order, order16, outer, counts, mkeys, wide_blk,
    ) = refs
    chips, lanes, channels = pair_one_ref.shape
    hidden = outer.shape[1]
    half = lanes // 2
    me = lax.axis_index("dap")
    parity = lax.rem(me, 2)
    my_chip = me // 2
    for k in range(steps):
        for h in range(chips // steps):
            pair_one_ref[my_chip ^ (h * steps + k)] = couples[k][h].astype(jnp.float32)
    rows = (chips * hidden, lanes)
    order16[parity] = own_ref[:, hidden:, :].astype(jnp.float32).reshape(rows)
    order16[1 - parity] = oth_ref[:, hidden:, :].astype(jnp.float32).reshape(rows)
    early = lane_iota((chips, lanes)) < half
    for b in range(hidden):
        for p in range(2):
            rows = order16[p, pl.ds(b, chips, stride=hidden), :]
            turned = pltpu.roll(rows, half, 1)
            for r in range(2):
                for rj in range(2):
                    part = rows if r == rj else turned
                    part = jnp.where(early, 0.0, part) if r else jnp.where(early, part, 0.0)
                    order[pl.ds(b * lanes + r * half + 2 * p + rj, chips, stride=4), :] = part
    rights = order[...].astype(jnp.bfloat16)
    few = 4
    for q in range(chips // few):
        lhs = own_ref[q * few : (q + 1) * few, :hidden, :].reshape(few * hidden, lanes)
        outer[q * few : (q + 1) * few] = (
            dot_nt(lhs, rights).astype(jnp.bfloat16).reshape((few,) + outer.shape[1:])
        )
    mask_rows = mask_block(blk_ref, wide_blk)
    total = jnp.zeros((half, lanes), jnp.float32)
    for s in range(2):
        part = mask_rows[:, s * half : (s + 1) * half]
        total = total + dot_tn(part, jnp.concatenate([part, part], axis=1))
    counts[...] = 1.0 / jnp.maximum(total, 1.0)
    mkeys[...] = presence_down(small_ref[PRESENCE : PRESENCE + 1, :half], half, lanes)
    gain = small_ref[ENTRY_GAINS : ENTRY_GAINS + 1, :channels]
    low_row = lane_iota((1, lanes)) < half
    group = 16

    @pl.loop(0, chips // group)
    def _(block):
        pairs, keeps = [], []
        made = []
        for c in range(0, group, 2):
            sides = []
            for chip in (block * group + c, block * group + c + 1):
                strip = outer[chip]
                sides.append(
                    jnp.concatenate(
                        [strip[:, b * lanes : (b + 1) * lanes] for b in range(hidden)], axis=0
                    )
                )
            res = dot_nn(fin_ref[...], jnp.concatenate(sides, axis=1))
            made += [res[:, :lanes], res[:, lanes:]]
        for c in range(group):
            chip = block * group + c
            i0 = 4 * chip + 2 * parity
            share = jnp.where(low_row, counts[pl.ds(i0, 1), :], counts[pl.ds(i0 + 1, 1), :])
            pairs.append(jnp.transpose(made[c] * share) + pair_one_ref[chip])
            for r in range(2):
                keeps.append(mkeys[...] * mkeys[pl.ds(i0 + r, 1), :])
        pair = jnp.concatenate(pairs, axis=0)
        keep = jnp.concatenate(keeps, axis=0)
        normed = normed_rows(pair, gain).astype(jnp.bfloat16)
        projected = dot_nn(normed, flank_ref[0, :, 2 * channels :])
        right = gated(projected, 0, channels, channels) * keep
        for c in range(group):
            chip = block * group + c
            rows = slice(c * lanes, (c + 1) * lanes)
            pair_one_ref[chip] = pair[rows]
            normed_ref[chip] = normed[rows]
            right_ref[chip] = jnp.transpose(right[rows]).astype(jnp.bfloat16)


def by_channel(ref, base, chips, channels):
    rows = [
        ref[pl.ds(pl.multiple_of(chip * channels + base, 8), 8), :] for chip in range(chips)
    ]
    return jnp.swapaxes(jnp.stack(rows), 0, 1)


def both_turns(rows):
    return jnp.concatenate([rows, pltpu.roll(rows, rows.shape[1] // 2, 1)], axis=0)


def left_body(
    normed_ref, own_ref, small_ref, flank_ref, switch_ref,
    lhs_ref, rhs_ref, gate_ref,
    left_ref, side, mkeys,
):
    chips, lanes, channels = gate_ref.shape
    half = lanes // 2
    parity = lax.rem(lax.axis_index("dap"), 2)
    mkeys[...] = presence_down(small_ref[PRESENCE : PRESENCE + 1, :half], half, lanes)
    group = 8
    for block in range(chips // group):
        keeps = []
        for c in range(group):
            for r in range(2):
                keeps.append(mkeys[...] * mkeys[pl.ds(4 * (block * group + c) + 2 * parity + r, 1), :])
        normed = normed_ref[block * group : (block + 1) * group].reshape(group * lanes, channels)
        projected = dot_nn(normed, flank_ref[0, :, : 2 * channels])
        left = gated(projected, 0, channels, channels) * jnp.concatenate(keeps, axis=0)
        gate = jax.nn.sigmoid(dot_nn(normed, switch_ref[0]))
        for c in range(group):
            chip = block * group + c
            rows = slice(c * lanes, (c + 1) * lanes)
            gate_ref[chip] = gate[rows]
            left_ref[chip * channels : (chip + 1) * channels, :] = jnp.transpose(left[rows])
            side[chip * channels : (chip + 1) * channels, :] = own_ref[chip].astype(jnp.float32)
    low = lane_iota((chips, lanes)) < half
    per_step = 64

    @pl.loop(0, channels // per_step)
    def _(step):
        for o in range(per_step // 8):
            base = step * per_step + o * 8
            left = by_channel(left_ref, base, chips, channels)
            own = by_channel(side, base, chips, channels)
            for c in range(8):
                lhs = jnp.concatenate(
                    [jnp.where(low, left[c], 0.0), jnp.where(low, 0.0, left[c])], axis=0
                )
                to = pl.ds(pl.multiple_of((base + c) * 2 * chips, 2 * chips), 2 * chips)
                lhs_ref[to, :] = lhs.astype(jnp.bfloat16)
                rhs_ref[to, :] = both_turns(own[c]).astype(jnp.bfloat16)


def outgoing_body(
    pair_one_ref, lhs_ref, rhs_ref, gate_ref, oth_ref, small_ref, final_ref, flank_ref,
    two_ref, send_ref,
    side, prods, mkeys, pair_two, rows_out, cols,
):
    chips, channels, lanes = oth_ref.shape
    half = lanes // 2
    me = lax.axis_index("dap")
    parity = lax.rem(me, 2)
    my_chip = me // 2

    side[...] = oth_ref[...].astype(jnp.float32).reshape(side.shape)
    per_step = 64

    @pl.loop(0, channels // per_step)
    def _(step):
        for o in range(per_step // 8):
            base = step * per_step + o * 8
            oth = by_channel(side, base, chips, channels)
            for c in range(8):
                at = pl.ds(pl.multiple_of((base + c) * 2 * chips, 2 * chips), 2 * chips)
                rhs = jnp.concatenate(
                    [rhs_ref[at, :], both_turns(oth[c]).astype(jnp.bfloat16)], axis=0
                )
                out = dot_nt(lhs_ref[at, :], rhs)
                out = jnp.concatenate([out[:chips], out[chips:]], axis=1)
                to = pl.ds(base + c, chips, stride=channels)
                prods[to, :] = out.astype(jnp.bfloat16).astype(jnp.float32)

    mkeys[...] = presence_down(small_ref[PRESENCE : PRESENCE + 1, :half], half, channels)
    gain_mid = small_ref[MID_GAINS : MID_GAINS + 1, :channels]
    gain_mid = jnp.transpose(jnp.broadcast_to(gain_mid, (channels, channels)))
    final_t = jnp.transpose(final_ref[0].astype(jnp.float32)).astype(jnp.bfloat16)
    gain = small_ref[ENTRY_GAINS : ENTRY_GAINS + 1, channels : 2 * channels]
    flank_right = flank_ref[1, :, 2 * channels :]
    flank_left = flank_ref[1, :, : 2 * channels]
    octet = pl.multiple_of(8 * (my_chip // 2), 8)
    group = 16
    for block in range(chips // group):
        changed = []
        for c in range(group):
            x = prods[(block * group + c) * channels : (block * group + c + 1) * channels, :]
            centred = x - jnp.mean(x, axis=0, keepdims=True)
            spread = jnp.mean(centred * centred, axis=0, keepdims=True)
            changed.append((centred * lax.rsqrt(spread + EPSILON) * gain_mid).astype(jnp.bfloat16))
        changed = dot_nn(final_t, jnp.concatenate(changed, axis=1))
        for c in range(group):
            part = jnp.transpose(changed[:, c * lanes : (c + 1) * lanes])
            for k in range(8):
                r = k // 4
                p = 1 - parity if (k // 2) % 2 else parity
                rj = k % 2 if r == 0 else 1 - k % 2
                rows_out[block * group + c, pl.ds(r * half + 2 * p + rj, chips, stride=4), :] = part[
                    k * chips : (k + 1) * chips
                ]
        twos, keeps = [], []
        for c in range(group):
            chip = block * group + c
            two = pair_one_ref[chip] + rows_out[chip] * gate_ref[chip]
            twos.append(two)
            for r in range(2):
                keeps.append(mkeys[pl.ds(4 * chip + 2 * parity + r, 1), :])
        two = jnp.concatenate(twos, axis=0)
        full = normed_rows(two, gain)
        normed = full.astype(jnp.bfloat16)
        keep = jnp.concatenate([mkeys[...] * m for m in keeps], axis=0)
        going = (gated(dot_nn(normed, flank_right), 0, channels, channels) * keep).astype(jnp.bfloat16)
        cols[block] = full
        few = jnp.concatenate(
            [cols[block, pl.ds(k * half + octet, 8), :] for k in range(2 * group)], axis=0
        ).astype(jnp.bfloat16)
        mine = mkeys[pl.ds(octet, 8), :]
        keep = jnp.concatenate([mine * m for m in keeps], axis=0)
        few = (gated(dot_nn(few, flank_left), 0, channels, channels) * keep).astype(jnp.bfloat16)
        for c in range(group):
            chip = block * group + c
            pair_two[chip] = twos[c]
            send_ref[chip, :lanes, :] = going[c * lanes : (c + 1) * lanes]
            send_ref[chip, lanes:, :] = few[c * 16 : (c + 1) * 16]
    two_ref[...] = pair_two[my_chip]


def add_products(side_ref, tails, totals):
    chips = side_ref.shape[0]
    half, _ = totals[0].shape
    lanes = 2 * half
    me = lax.axis_index("dap")
    first = 4 * lax.rem(me // 2, 2) + 2 * lax.rem(me, 2)
    tails[...] = side_ref[:, lanes:, :].astype(jnp.float32).reshape(tails.shape)
    ahead = 4

    def step(block, totals):
        totals = list(totals)
        for c in range(ahead):
            chip = block * ahead + c
            for k in range(2):
                there = side_ref[chip, k * half : (k + 1) * half, :].astype(jnp.float32)
                for i in range(2):
                    one = tails[pl.ds(chip * 16 + 8 * k + first + i, 1), :]
                    totals[i] = totals[i] + one * there
        return tuple(totals)

    return lax.fori_loop(0, chips // ahead, step, tuple(totals))


def incoming_own_body(own_ref, two_ref, couple_ref, small_ref, switch_ref, sums_ref, kept_ref, gate_ref, tails):
    lanes, channels = two_ref.shape
    half = lanes // 2
    zero = jnp.zeros((half, channels), jnp.float32)
    sums_ref[...] = jnp.concatenate(add_products(own_ref, tails, (zero, zero)), axis=0)
    two = two_ref[...]
    gain = small_ref[ENTRY_GAINS : ENTRY_GAINS + 1, channels : 2 * channels]
    normed = normed_rows(two, gain).astype(jnp.bfloat16)
    gate_ref[...] = jax.nn.sigmoid(dot_nn(normed, switch_ref[1]))
    couple = couple_ref[...]
    kept_ref[...] = two + (couple - couple.astype(jnp.bfloat16).astype(jnp.float32))


def incoming_body(oth_ref, sums_ref, kept_ref, gate_ref, small_ref, final_ref, out_ref, tails):
    lanes, channels = out_ref.shape
    half = lanes // 2
    prod = jnp.concatenate(
        add_products(oth_ref, tails, (sums_ref[:half, :], sums_ref[half:, :])), axis=0
    )
    prod = prod.astype(jnp.bfloat16).astype(jnp.float32)
    gain_mid = small_ref[MID_GAINS : MID_GAINS + 1, channels : 2 * channels]
    changed = dot_nn(normed_rows(prod, gain_mid).astype(jnp.bfloat16), final_ref[1])
    out_ref[...] = kept_ref[...] + changed * gate_ref[...]


def gather_by_steps(block, chips):
    bits = chips.bit_length() - 1
    steps = 1 << (bits // 2)
    devices = 2 * chips

    def fetch(value, apart):
        return lax.ppermute(value, "dap", [(d, d ^ (2 * apart)) for d in range(devices)])

    near = block
    while near.shape[0] < chips // steps:
        near = jnp.concatenate([near, fetch(near, near.shape[0] * steps)], axis=0)
    return near, [fetch(near, k) for k in range(1, steps)]


def paired_shards(
    homolog_stack,
    couple_tensor,
    homolog_presence,
    amino_presence,
    horizontal_standard_factor,
    horizontal_asking_matrix,
    horizontal_lookup_triple,
    horizontal_final_matrix,
    couple_offset_factor,
    couple_offset_matrix,
    vertical_standard_factor,
    vertical_asking_matrix,
    vertical_lookup_triple,
    vertical_final_matrix,
    tensor_average_factor,
    tensor_average_mapping,
    tensor_average_final,
    trio_entry_factors,
    trio_flank_mappings,
    trio_final_switches,
    trio_multiplied_factors,
    trio_final_matrices,
):
    devices = lax.axis_size("dap")
    chips = devices // 2
    strands, aminos, features = homolog_stack.shape
    rows, _, channels = couple_tensor.shape
    lanes = rows * aminos
    heads = FOCUS_NUMBER
    hidden = TENSOR_HIDDEN
    f32, bf16 = jnp.float32, jnp.bfloat16
    shape = jax.ShapeDtypeStruct
    same_parity = [[2 * chip + p for chip in range(chips)] for p in range(2)]
    swap = [(d, d ^ 1) for d in range(devices)]

    def line(v):
        return v.reshape(1, -1)

    couple = couple_tensor.reshape(lanes, channels)
    x = homolog_stack.reshape(strands * aminos, features)
    block, near = vmem_call(
        bias_body,
        (shape((devices, 16, lanes), bf16), shape((1, lanes, channels), bf16)),
        scratch=[
            pltpu.VMEM((lanes, channels), f32),
            pltpu.VMEM((1, channels), f32),
            pltpu.VMEM((heads, channels), bf16),
            pltpu.VMEM((strands, aminos), jnp.int32),
            pltpu.SemaphoreType.DMA((4,)),
        ],
        count=4,
        away=range(4),
        grant=60 << 20,
    )(couple, line(couple_offset_factor), couple_offset_matrix.T, homolog_presence)
    blocks = lax.all_to_all(block, "dap", split_axis=0, concat_axis=0, tiled=True)
    small = jnp.concatenate(
        [
            line(horizontal_standard_factor),
            line(vertical_standard_factor),
            line(tensor_average_factor),
            line(trio_entry_factors),
            line(trio_multiplied_factors),
            jnp.pad(line(amino_presence.astype(f32)), ((0, 0), (0, features - aminos))),
            jnp.zeros((2, features), f32),
        ],
        axis=0,
    )
    final = jnp.transpose(
        tensor_average_final.reshape(hidden, hidden, channels), (2, 1, 0)
    ).reshape(channels, hidden * hidden)
    q, k, v, g = vmem_call(
        project_body,
        (
            shape((features // lanes, lanes, lanes), f32),
            shape((lanes, features), bf16),
            shape((lanes, features), bf16),
            shape((features // lanes, lanes, lanes), f32),
        ),
        count=4,
    )(x, small, horizontal_asking_matrix, horizontal_lookup_triple)
    near, fars = gather_by_steps(near, chips)
    couples = [near, *fars]
    sent = vmem_call(
        row_body,
        shape((devices, 8, lanes), bf16),
        scratch=[
            pltpu.VMEM((devices * 16, lanes), f32),
            pltpu.VMEM((devices * 8, lanes), f32),
            pltpu.VMEM((features // lanes, lanes, lanes), f32),
        ],
        count=7,
    )(blocks, x, q, k, v, g, horizontal_final_matrix)
    arrived = lax.all_to_all(sent, "dap", split_axis=0, concat_axis=0, tiled=True)
    msa, opm = vmem_call(
        column_body,
        (shape((devices * strands, rows * features), f32), shape((chips, 2 * hidden, lanes), bf16)),
        scratch=[
            pltpu.VMEM((devices * 8, lanes), f32),
            pltpu.VMEM((devices * 16, lanes), f32),
            pltpu.VMEM((lanes, features), f32),
            pltpu.VMEM((4, devices * strands, lanes), f32),
        ],
        count=7,
        later=1,
    )(
        arrived,
        blocks,
        small,
        vertical_asking_matrix,
        vertical_lookup_triple,
        vertical_final_matrix,
        tensor_average_mapping.T,
        final,
    )
    opm_own = lax.all_to_all(
        opm, "dap", split_axis=0, concat_axis=0, tiled=True, axis_index_groups=same_parity
    )
    opm_oth = lax.ppermute(opm_own, "dap", swap)
    msa = msa.reshape(devices * strands, rows, features)
    stack = (chips, lanes, channels)
    pair_one, normed, right_own = vmem_call(
        functools.partial(opm_body, len(couples)),
        (shape(stack, f32), shape(stack, bf16), shape(stack, bf16)),
        scratch=[
            pltpu.VMEM((hidden * lanes, lanes), f32),
            pltpu.VMEM((2, chips * hidden, lanes), f32),
            pltpu.VMEM((chips, hidden, hidden * lanes), bf16),
            pltpu.VMEM((aminos, lanes), f32),
            pltpu.VMEM((aminos, channels), f32),
            pltpu.VMEM((devices * 16, lanes), f32),
        ],
        count=len(couples) + 6,
        later=1,
    )(
        opm_own,
        opm_oth,
        *couples,
        blocks,
        final,
        small,
        trio_flank_mappings,
        msa,
    )
    right_oth = lax.ppermute(right_own, "dap", swap)
    by_channels = shape((channels * 2 * chips, lanes), bf16)
    lhs, rhs, gate = vmem_call(
        left_body,
        (by_channels, by_channels, shape(stack, f32)),
        scratch=[
            pltpu.VMEM((chips * channels, lanes), f32),
            pltpu.VMEM((chips * channels, lanes), f32),
            pltpu.VMEM((aminos, channels), f32),
        ],
        count=5,
    )(normed, right_own, small, trio_flank_mappings, trio_final_switches)
    two, going = vmem_call(
        outgoing_body,
        (shape((lanes, channels), f32), shape((chips, lanes + 16, channels), bf16)),
        scratch=[
            pltpu.VMEM((chips * channels, lanes), f32),
            pltpu.VMEM((channels * chips, lanes), f32),
            pltpu.VMEM((aminos, channels), f32),
            pltpu.VMEM(stack, f32),
            pltpu.VMEM(stack, f32),
            pltpu.VMEM((chips // 16, 16 * lanes, channels), f32),
        ],
        count=8,
    )(
        pair_one,
        lhs,
        rhs,
        gate,
        right_oth,
        small,
        trio_final_matrices,
        trio_flank_mappings,
    )
    coming = lax.ppermute(going, "dap", swap)
    own_rows = shape((lanes, channels), f32)
    tails = [pltpu.VMEM((chips * 16, channels), f32)]
    sums, kept, gate = vmem_call(
        incoming_own_body, (own_rows,) * 3, scratch=tails, count=5
    )(going, two, couple, small, trio_final_switches)
    pair_out = vmem_call(incoming_body, own_rows, scratch=tails, count=6)(
        coming, sums, kept, gate, small, trio_final_matrices
    )
    return msa, pair_out.reshape(rows, aminos, channels)


def fits_pairs(homolog_stack, couple_tensor, devices):
    strands, aminos, features = homolog_stack.shape
    rows, _, channels = couple_tensor.shape
    lanes = 128
    return (
        strands == rows == 2
        and devices % 8 == 0
        and devices & (devices - 1) == 0
        and rows * aminos == lanes == channels
        and aminos == 2 * devices
        and features == 2 * lanes
    )


def either(*arrays):
    if fits_pairs(arrays[0], arrays[1], lax.axis_size("dap")):
        return paired_shards(*arrays)
    return shards(*arrays)


def solution(mesh):
    placed = (
        P("dap", None, None),
        P("dap", None, None),
        P("dap", None),
        P(),
        P(),
        P(),
        P(),
        P(),
        P(),
        P(),
        P(),
        P(),
        P(),
        P(),
        P(),
        P(),
        P(),
        P(),
        P(),
        P(),
        P(),
        P(),
    )
    return jax.shard_map(
        either,
        mesh=mesh,
        in_specs=placed,
        out_specs=(P(None, "dap", None), P("dap", None, None)),
        check_vma=False,
    )
```

```python
import functools
import math

import jax
import jax.numpy as jnp
from jax import lax
from jax.experimental import pallas as pl
from jax.experimental.pallas import tpu as pltpu
from jax.sharding import PartitionSpec as P

FOCUS_NUMBER = 8
PER_FOCUS_WIDTH = 32
TENSOR_HIDDEN = 32
TRI_HID = 128


EPSILON = 1e-05
MASK_PENALTY_SCALE = 1000000000.0


def standardize_features(content_vectors, gain, axis):
    centred = content_vectors - jnp.mean(content_vectors, axis=axis, keepdims=True)
    spread = jnp.mean(centred * centred, axis=axis, keepdims=True)
    return centred * lax.rsqrt(spread + EPSILON) * gain


def gather_blocks(block):
    device_count = lax.axis_size("dap")
    copies = jnp.broadcast_to(block[None], (device_count,) + block.shape)
    return lax.all_to_all(copies, "dap", split_axis=0, concat_axis=0, tiled=True)


def triangle(
    pair_now, gain_in, proj_weight, gate_weight, gain_mid, final_weight, amino_presence, incoming
):
    hidden = TRI_HID
    row_count = pair_now.shape[0]
    my_index = lax.axis_index("dap")
    standardized_source = standardize_features(pair_now, gain_in, -1).astype(jnp.bfloat16)
    projected = jnp.einsum(
        "rkd,de->erk", standardized_source, proj_weight, preferred_element_type=jnp.float32
    )
    res_float = amino_presence.astype(jnp.float32)
    own_rows = lax.dynamic_slice_in_dim(res_float, my_index * row_count, row_count)
    pair_mask = own_rows[:, None] * res_float[None, :]
    left_side = (
        jax.nn.sigmoid(projected[hidden : 2 * hidden]) * projected[:hidden] * pair_mask[None]
    ).astype(jnp.bfloat16)
    right_side = (
        jax.nn.sigmoid(projected[3 * hidden :])
        * projected[2 * hidden : 3 * hidden]
        * pair_mask[None]
    ).astype(jnp.bfloat16)
    gating = jax.nn.sigmoid(
        jnp.dot(standardized_source, gate_weight, preferred_element_type=jnp.float32)
    )
    device_count = lax.axis_size("dap")
    per_device = hidden // device_count
    both = jnp.stack(
        [
            left_side.reshape(device_count, per_device, row_count, -1),
            right_side.reshape(device_count, per_device, row_count, -1),
        ],
        axis=1,
    )
    both = lax.all_to_all(both, "dap", split_axis=0, concat_axis=0, tiled=True)
    both = jnp.moveaxis(both, 0, 2).reshape(2, per_device, device_count * row_count, -1)
    left_chan, right_chan = both[0], both[1]
    if incoming:
        product = jnp.einsum(
            "cki,ckj->cij", left_chan, right_chan, preferred_element_type=jnp.float32
        )
    else:
        product = jnp.einsum(
            "cik,cjk->cij", left_chan, right_chan, preferred_element_type=jnp.float32
        )
    product = product.astype(jnp.bfloat16)
    returned = lax.all_to_all(product, "dap", split_axis=1, concat_axis=0, tiled=True)
    product_normed = standardize_features(
        returned.astype(jnp.float32), gain_mid[:, None, None], 0
    ).astype(jnp.bfloat16)
    update = jnp.einsum(
        "crj,cd->rjd", product_normed, final_weight, preferred_element_type=jnp.float32
    )
    return pair_now + update * gating


def shards(
    homolog_stack,
    couple_tensor,
    homolog_presence,
    amino_presence,
    horizontal_standard_factor,
    horizontal_asking_matrix,
    horizontal_lookup_triple,
    horizontal_final_matrix,
    couple_offset_factor,
    couple_offset_matrix,
    vertical_standard_factor,
    vertical_asking_matrix,
    vertical_lookup_triple,
    vertical_final_matrix,
    tensor_average_factor,
    tensor_average_mapping,
    tensor_average_final,
    trio_entry_factors,
    trio_flank_mappings,
    trio_final_switches,
    trio_multiplied_factors,
    trio_final_matrices,
):
    nested_function = FOCUS_NUMBER * PER_FOCUS_WIDTH
    scaling = 1.0 / math.sqrt(PER_FOCUS_WIDTH)
    strand_portion = homolog_stack.shape[0]
    amino_total = homolog_stack.shape[1]
    row_count = couple_tensor.shape[0]
    pair_normed = standardize_features(couple_tensor, couple_offset_factor, -1).astype(jnp.bfloat16)
    bias_local = jnp.einsum(
        "rjc,ch->hrj", pair_normed, couple_offset_matrix, preferred_element_type=jnp.float32
    ).astype(jnp.bfloat16)
    standardized_source = standardize_features(
        homolog_stack, horizontal_standard_factor, -1
    ).astype(jnp.bfloat16)
    shaped = (strand_portion, amino_total, FOCUS_NUMBER, PER_FOCUS_WIDTH)
    queries = (
        (
            jnp.dot(
                standardized_source, horizontal_asking_matrix, preferred_element_type=jnp.float32
            )
            * scaling
        )
        .astype(jnp.bfloat16)
        .reshape(shaped)
    )
    others = jnp.dot(
        standardized_source, horizontal_lookup_triple, preferred_element_type=jnp.float32
    )
    keys_all = others[..., :nested_function].astype(jnp.bfloat16).reshape(shaped)
    content_entire = (
        others[..., nested_function : 2 * nested_function].astype(jnp.bfloat16).reshape(shaped)
    )
    sigmoid_switches = jax.nn.sigmoid(others[..., 2 * nested_function :])
    mask_penalty = MASK_PENALTY_SCALE * (homolog_presence.astype(jnp.float32) - 1.0)

    def attend(bias_piece):
        query_rows = bias_piece.shape[1]
        scores = jnp.einsum(
            "sihc,sjhc->shij", queries, keys_all, preferred_element_type=jnp.float32
        )
        scores = scores + bias_piece.astype(jnp.float32)[None] + mask_penalty[:, None, None, :]
        softmax_probabilities = jax.nn.softmax(scores, axis=-1).astype(jnp.bfloat16)
        mixed = jnp.einsum(
            "shij,sjhc->sihc",
            softmax_probabilities,
            content_entire,
            preferred_element_type=jnp.float32,
        )
        return mixed.reshape(strand_portion, query_rows, nested_function)

    bias_whole = jnp.moveaxis(gather_blocks(bias_local), 0, 1).reshape(
        FOCUS_NUMBER, amino_total, amino_total
    )
    block_rows = math.gcd(amino_total, 256)

    def one_block(block_index):
        return attend(bias_whole)

    blocks = lax.map(one_block, jnp.arange(amino_total // block_rows, dtype=jnp.int32))
    focused_content = jnp.moveaxis(blocks, 0, 1).reshape(
        strand_portion, amino_total, nested_function
    )
    homolog_stack_horizontal = homolog_stack + jnp.dot(
        (focused_content * sigmoid_switches).astype(jnp.bfloat16),
        horizontal_final_matrix,
        preferred_element_type=jnp.float32,
    )
    travelling = jnp.concatenate(
        [
            homolog_stack_horizontal.astype(jnp.bfloat16),
            jnp.broadcast_to(
                homolog_presence.astype(jnp.bfloat16)[..., None],
                (strand_portion, amino_total, 128),
            ),
        ],
        axis=-1,
    )
    arrived = lax.all_to_all(travelling, "dap", split_axis=1, concat_axis=0, tiled=True)
    column_view = arrived[..., :nested_function].astype(jnp.float32)
    col_mask = arrived[..., nested_function].astype(jnp.float32)
    seq_total = column_view.shape[0]
    col_shape = (seq_total, row_count, FOCUS_NUMBER, PER_FOCUS_WIDTH)
    standardized_source = standardize_features(column_view, vertical_standard_factor, -1).astype(
        jnp.bfloat16
    )
    col_queries = (
        (
            jnp.dot(standardized_source, vertical_asking_matrix, preferred_element_type=jnp.float32)
            * scaling
        )
        .astype(jnp.bfloat16)
        .reshape(col_shape)
    )
    col_others = jnp.dot(
        standardized_source, vertical_lookup_triple, preferred_element_type=jnp.float32
    )
    col_keys = col_others[..., :nested_function].astype(jnp.bfloat16).reshape(col_shape)
    col_values = (
        col_others[..., nested_function : 2 * nested_function]
        .astype(jnp.bfloat16)
        .reshape(col_shape)
    )
    col_gates = jax.nn.sigmoid(col_others[..., 2 * nested_function :])
    col_penalty = MASK_PENALTY_SCALE * (col_mask - 1.0)
    scores = jnp.einsum(
        "sihc,tihc->ihst", col_queries, col_keys, preferred_element_type=jnp.float32
    )
    scores = scores + jnp.transpose(col_penalty)[:, None, None, :]
    softmax_probabilities = jax.nn.softmax(scores, axis=-1).astype(jnp.bfloat16)
    col_mixed = jnp.einsum(
        "uovg,guox->vuox", softmax_probabilities, col_values, preferred_element_type=jnp.float32
    ).reshape(seq_total, row_count, nested_function)
    alignment_after_columns = column_view + jnp.dot(
        (col_mixed * col_gates).astype(jnp.bfloat16),
        vertical_final_matrix,
        preferred_element_type=jnp.float32,
    )
    standardized_source = standardize_features(
        alignment_after_columns, tensor_average_factor, -1
    ).astype(jnp.bfloat16)
    halves = jnp.dot(
        standardized_source, tensor_average_mapping, preferred_element_type=jnp.float32
    )
    left_proj = (halves[..., :TENSOR_HIDDEN] * col_mask[..., None]).astype(jnp.bfloat16)
    right_proj = (halves[..., TENSOR_HIDDEN:] * col_mask[..., None]).astype(jnp.bfloat16)
    block = jnp.concatenate(
        [right_proj, col_mask.astype(jnp.bfloat16)[..., None]], axis=-1
    )
    block = jnp.transpose(block, (1, 2, 0))
    whole = gather_blocks(block).reshape(amino_total, TENSOR_HIDDEN + 1, seq_total)
    right_whole = jnp.transpose(whole[:, :TENSOR_HIDDEN], (2, 0, 1))
    mask_whole = jnp.transpose(whole[:, TENSOR_HIDDEN])
    outer = jnp.einsum("sra,sjb->rjab", left_proj, right_whole, preferred_element_type=jnp.float32)
    outer = outer.astype(jnp.bfloat16).reshape(
        row_count, amino_total, TENSOR_HIDDEN * TENSOR_HIDDEN
    )
    counts = jnp.dot(
        jnp.transpose(col_mask), mask_whole.astype(jnp.float32), precision=lax.Precision.HIGHEST
    )
    product = (
        jnp.dot(outer, tensor_average_final, preferred_element_type=jnp.float32)
        / jnp.maximum(counts, 1.0)[..., None]
    )
    pair_one = couple_tensor + product
    pair_two = triangle(
        pair_one,
        trio_entry_factors[0],
        trio_flank_mappings[0],
        trio_final_switches[0],
        trio_multiplied_factors[0],
        trio_final_matrices[0],
        amino_presence,
        False,
    )
    pair_after_incoming = triangle(
        pair_two,
        trio_entry_factors[1],
        trio_flank_mappings[1],
        trio_final_switches[1],
        trio_multiplied_factors[1],
        trio_final_matrices[1],
        amino_presence,
        True,
    )
    return (alignment_after_columns, pair_after_incoming)


def normed_rows(x, gain):
    centred = x - jnp.mean(x, axis=-1, keepdims=True)
    spread = jnp.mean(centred * centred, axis=-1, keepdims=True)
    return centred * lax.rsqrt(spread + EPSILON) * gain


def dot_nn(a, b):
    return lax.dot_general(a, b, (((1,), (0,)), ((), ())), preferred_element_type=jnp.float32)


def dot_nt(a, b):
    return lax.dot_general(a, b, (((1,), (1,)), ((), ())), preferred_element_type=jnp.float32)


def dot_tn(a, b):
    return lax.dot_general(a, b, (((0,), (0,)), ((), ())), preferred_element_type=jnp.float32)


def lane_iota(shape):
    return lax.broadcasted_iota(jnp.int32, shape, len(shape) - 1)


def vmem_call(body, outs, scratch=(), count=0, later=0, away=(), grant=20 << 20):
    whole = pl.BlockSpec(memory_space=pltpu.VMEM)
    there = pl.BlockSpec(memory_space=pl.ANY)
    hbm = pl.BlockSpec(memory_space=pltpu.HBM)

    def reader(*refs):
        body(*refs[:count], *refs[count + later :])

    return pl.pallas_call(
        reader,
        out_shape=outs,
        in_specs=[hbm if k in away else whole for k in range(count)] + [there] * later,
        out_specs=jax.tree.map(lambda _: whole, outs),
        scratch_shapes=list(scratch),
        compiler_params=pltpu.CompilerParams(vmem_limit_bytes=grant),
    )


ROW_GAIN, COLUMN_GAIN, MEAN_GAIN, ENTRY_GAINS, MID_GAINS, PRESENCE = range(6)


def bias_body(pair_at, gain_at, weight_at, present_at, out_ref, near_ref, pair, gain, weight, present, sems):
    moves = [
        pltpu.make_async_copy(there, here, sems.at[k])
        for k, (there, here) in enumerate(
            ((pair_at, pair), (gain_at, gain), (weight_at, weight), (present_at, present))
        )
    ]
    for move in moves:
        move.start()
    for move in moves:
        move.wait()
    near_ref[0] = pair[...].astype(jnp.bfloat16)
    normed = normed_rows(pair[...], gain[...]).astype(jnp.bfloat16)
    bias = dot_nt(weight[...], normed)
    here = present[...].astype(jnp.float32)
    mask_row = jnp.concatenate([here[0:1], here[1:2]], axis=1)
    fill = jnp.zeros((out_ref.shape[1] - bias.shape[0] - 1, bias.shape[1]), jnp.float32)
    block = jnp.concatenate([bias, mask_row, fill], axis=0).astype(jnp.bfloat16)
    out_ref[...] = jnp.broadcast_to(block[None], out_ref.shape)


def put_parts(ref, value):
    lanes = ref.shape[2]
    for part in range(ref.shape[0]):
        ref[part] = value[:, part * lanes : (part + 1) * lanes]


def rows_of(ref, rows):
    return jnp.concatenate([ref[part, rows, :] for part in range(ref.shape[0])], axis=1)


def project_body(x_ref, small_ref, ask_ref, look_ref, q_ref, k_ref, v_ref, g_ref):
    width = ask_ref.shape[1]
    normed = normed_rows(x_ref[...], small_ref[ROW_GAIN : ROW_GAIN + 1]).astype(jnp.bfloat16)
    scaling = 1.0 / math.sqrt(PER_FOCUS_WIDTH)
    q = (dot_nn(normed, ask_ref[...]) * scaling).astype(jnp.bfloat16).astype(jnp.float32)
    put_parts(q_ref, q)
    others = dot_nn(normed, look_ref[...])
    k_ref[...] = others[:, :width].astype(jnp.bfloat16)
    v_ref[...] = others[:, width : 2 * width].astype(jnp.bfloat16)
    put_parts(g_ref, jax.nn.sigmoid(others[:, 2 * width :]))


def head_spread(q):
    head_of = lane_iota(q.shape) // PER_FOCUS_WIDTH
    return jnp.concatenate(
        [jnp.where(head_of == h, q, 0.0) for h in range(FOCUS_NUMBER)], axis=0
    ).astype(jnp.bfloat16)


def attend_heads(q, k, v, *offsets):
    scores = dot_nt(head_spread(q), k)
    for offset in offsets:
        scores = scores + offset
    scores = scores - jnp.max(scores, axis=-1, keepdims=True)
    raised = jnp.exp(scores)
    shares = (raised / jnp.sum(raised, axis=-1, keepdims=True)).astype(jnp.bfloat16)
    mixed = dot_nn(shares, v)
    rows = q.shape[0]
    head_of = lane_iota(q.shape) // PER_FOCUS_WIDTH
    total = jnp.where(head_of == 0, mixed[:rows], 0.0)
    for h in range(1, FOCUS_NUMBER):
        total = jnp.where(head_of == h, mixed[h * rows : (h + 1) * rows], total)
    return total


def row_body(blk_ref, x_ref, q_ref, k_ref, v_ref, g_ref, final_ref, out_ref, wide, send, x_parts):
    devices = blk_ref.shape[0]
    put_parts(x_parts, x_ref[...])
    per_block = blk_ref.shape[1]
    half = wide.shape[1] // 2
    per_seq = 2 * devices
    wide[...] = blk_ref[...].astype(jnp.float32).reshape(wide.shape)
    mine = wide[pl.ds(lax.axis_index("dap") * per_block + FOCUS_NUMBER, 1), :]
    penalty = MASK_PENALTY_SCALE * (mine - 1.0)
    heads = [wide[pl.ds(h, devices, stride=per_block), :] for h in range(FOCUS_NUMBER)]
    for s in range(2):
        keys = k_ref[s * per_seq : (s + 1) * per_seq, :]
        values = v_ref[s * per_seq : (s + 1) * per_seq, :]
        for r in range(2):
            rows = pl.ds(s * per_seq + r, devices, stride=2)
            bias = jnp.concatenate([b[:, r * half : (r + 1) * half] for b in heads], axis=0)
            mixed = attend_heads(
                rows_of(q_ref, rows), keys, values, bias, penalty[:, s * half : (s + 1) * half]
            )
            y = (mixed * rows_of(g_ref, rows)).astype(jnp.bfloat16)
            updated = rows_of(x_parts, rows) + dot_nn(y, final_ref[...])
            for part in range(updated.shape[1] // (2 * half)):
                to = pl.ds((s * 2 + r) * 2 + part, devices, stride=out_ref.shape[1])
                send[to, :] = updated[:, part * 2 * half : (part + 1) * 2 * half]
    out_ref[...] = send[...].reshape(out_ref.shape).astype(jnp.bfloat16)


def mask_block(blk_ref, wide):
    wide[...] = blk_ref[...].astype(jnp.float32).reshape(wide.shape)
    rows = pl.ds(FOCUS_NUMBER, blk_ref.shape[0], stride=blk_ref.shape[1])
    return wide[rows, :].astype(jnp.bfloat16)


def column_body(
    arrived_ref, blk_ref, small_ref, ask_ref, look_ref, final_ref, map_ref,
    msa_ref, opm_ref, wide, wide_blk, x_all, msa,
):
    devices = arrived_ref.shape[0]
    width = ask_ref.shape[1]
    lanes = wide.shape[1]
    half = lanes // 2
    seqs = 2 * devices
    me = lax.axis_index("dap")
    wide[...] = arrived_ref[...].astype(jnp.float32).reshape(wide.shape)
    for r in range(2):
        for s in range(2):
            base = (s * 2 + r) * 2
            at = (r * 2 + s) * devices
            for part in range(2):
                x_all[at : at + devices, part * lanes : (part + 1) * lanes] = wide[
                    pl.ds(base + part, devices, stride=8), :
                ]
    mask_lanes = mask_block(blk_ref, wide_blk)
    row = lax.broadcasted_iota(jnp.int32, (8, lanes), 0)
    wanted = (row % 2) * half + 2 * me + row // 2
    pick = jnp.where((lane_iota((8, lanes)) == wanted) & (row < 4), 1.0, 0.0).astype(jnp.bfloat16)
    picked = dot_nt(pick, mask_lanes)
    present = [
        jnp.concatenate([picked[2 * r : 2 * r + 1], picked[2 * r + 1 : 2 * r + 2]], axis=1)
        for r in range(2)
    ]
    x = x_all[...]
    normed = normed_rows(x, small_ref[COLUMN_GAIN : COLUMN_GAIN + 1]).astype(jnp.bfloat16)
    scaling = 1.0 / math.sqrt(PER_FOCUS_WIDTH)
    q = (dot_nn(normed, ask_ref[...]) * scaling).astype(jnp.bfloat16).astype(jnp.float32)
    others = dot_nn(normed, look_ref[...])
    keys = others[:, :width].astype(jnp.bfloat16)
    values = others[:, width : 2 * width].astype(jnp.bfloat16)
    gates = jax.nn.sigmoid(others[:, 2 * width :])
    mixed = jnp.concatenate(
        [
            attend_heads(
                q[r * seqs : (r + 1) * seqs],
                keys[r * seqs : (r + 1) * seqs],
                values[r * seqs : (r + 1) * seqs],
                MASK_PENALTY_SCALE * (present[r] - 1.0),
            )
            for r in range(2)
        ],
        axis=0,
    )
    updated = x + dot_nn((mixed * gates).astype(jnp.bfloat16), final_ref[...])
    for r in range(2):
        for s in range(2):
            at = (r * 2 + s) * devices
            for part in range(2):
                msa[r * 2 + part, pl.ds(s, devices, stride=2), :] = updated[
                    at : at + devices, part * lanes : (part + 1) * lanes
                ]
    for part in range(4):
        msa_ref[:, part * lanes : (part + 1) * lanes] = msa[part]
    normed = normed_rows(updated, small_ref[MEAN_GAIN : MEAN_GAIN + 1]).astype(jnp.bfloat16)
    sides = [
        dot_nt(map_ref[...], normed[r * seqs : (r + 1) * seqs]) * present[r] for r in range(2)
    ]
    block = jnp.concatenate(sides, axis=1).astype(jnp.bfloat16)
    opm_ref[...] = jnp.broadcast_to(block[None], opm_ref.shape)


def gated(projected, q_at, g_at, width):
    return jax.nn.sigmoid(projected[:, g_at : g_at + width]) * projected[:, q_at : q_at + width]


def presence_down(amino_row, half, lanes):
    square = lax.broadcasted_iota(jnp.int32, (half, half), 0) == lane_iota((half, half))
    diagonal = jnp.where(square, amino_row.astype(jnp.float32), 0.0).astype(jnp.bfloat16)
    return dot_nn(diagonal, jnp.ones((half, lanes), jnp.bfloat16))


def opm_body(steps, own_ref, oth_ref, *refs):
    couples, refs = refs[:steps], refs[steps:]
    (
        blk_ref, fin_ref, small_ref, flank_ref,
        pair_one_ref, normed_ref, right_ref,
        order, order16, outer, counts, mkeys, wide_blk,
    ) = refs
    chips, lanes, channels = pair_one_ref.shape
    hidden = outer.shape[1]
    half = lanes // 2
    me = lax.axis_index("dap")
    parity = lax.rem(me, 2)
    my_chip = me // 2
    for k in range(steps):
        for h in range(chips // steps):
            pair_one_ref[my_chip ^ (h * steps + k)] = couples[k][h].astype(jnp.float32)
    rows = (chips * hidden, lanes)
    order16[parity] = own_ref[:, hidden:, :].astype(jnp.float32).reshape(rows)
    order16[1 - parity] = oth_ref[:, hidden:, :].astype(jnp.float32).reshape(rows)
    early = lane_iota((chips, lanes)) < half
    for b in range(hidden):
        for p in range(2):
            rows = order16[p, pl.ds(b, chips, stride=hidden), :]
            turned = pltpu.roll(rows, half, 1)
            for r in range(2):
                for rj in range(2):
                    part = rows if r == rj else turned
                    part = jnp.where(early, 0.0, part) if r else jnp.where(early, part, 0.0)
                    order[pl.ds(b * lanes + r * half + 2 * p + rj, chips, stride=4), :] = part
    rights = order[...].astype(jnp.bfloat16)
    few = 4
    for q in range(chips // few):
        lhs = own_ref[q * few : (q + 1) * few, :hidden, :].reshape(few * hidden, lanes)
        outer[q * few : (q + 1) * few] = (
            dot_nt(lhs, rights).astype(jnp.bfloat16).reshape((few,) + outer.shape[1:])
        )
    mask_rows = mask_block(blk_ref, wide_blk)
    total = jnp.zeros((half, lanes), jnp.float32)
    for s in range(2):
        part = mask_rows[:, s * half : (s + 1) * half]
        total = total + dot_tn(part, jnp.concatenate([part, part], axis=1))
    counts[...] = 1.0 / jnp.maximum(total, 1.0)
    mkeys[...] = presence_down(small_ref[PRESENCE : PRESENCE + 1, :half], half, lanes)
    gain = small_ref[ENTRY_GAINS : ENTRY_GAINS + 1, :channels]
    low_row = lane_iota((1, lanes)) < half
    group = 16

    @pl.loop(0, chips // group)
    def _(block):
        pairs, keeps = [], []
        made = []
        for c in range(0, group, 2):
            sides = []
            for chip in (block * group + c, block * group + c + 1):
                strip = outer[chip]
                sides.append(
                    jnp.concatenate(
                        [strip[:, b * lanes : (b + 1) * lanes] for b in range(hidden)], axis=0
                    )
                )
            res = dot_nn(fin_ref[...], jnp.concatenate(sides, axis=1))
            made += [res[:, :lanes], res[:, lanes:]]
        for c in range(group):
            chip = block * group + c
            i0 = 4 * chip + 2 * parity
            share = jnp.where(low_row, counts[pl.ds(i0, 1), :], counts[pl.ds(i0 + 1, 1), :])
            pairs.append(jnp.transpose(made[c] * share) + pair_one_ref[chip])
            for r in range(2):
                keeps.append(mkeys[...] * mkeys[pl.ds(i0 + r, 1), :])
        pair = jnp.concatenate(pairs, axis=0)
        keep = jnp.concatenate(keeps, axis=0)
        normed = normed_rows(pair, gain).astype(jnp.bfloat16)
        projected = dot_nn(normed, flank_ref[0, :, 2 * channels :])
        right = gated(projected, 0, channels, channels) * keep
        for c in range(group):
            chip = block * group + c
            rows = slice(c * lanes, (c + 1) * lanes)
            pair_one_ref[chip] = pair[rows]
            normed_ref[chip] = normed[rows]
            right_ref[chip] = jnp.transpose(right[rows]).astype(jnp.bfloat16)


def by_channel(ref, base, chips, channels):
    rows = [
        ref[pl.ds(pl.multiple_of(chip * channels + base, 8), 8), :] for chip in range(chips)
    ]
    return jnp.swapaxes(jnp.stack(rows), 0, 1)


def both_turns(rows):
    return jnp.concatenate([rows, pltpu.roll(rows, rows.shape[1] // 2, 1)], axis=0)


def left_body(
    normed_ref, own_ref, small_ref, flank_ref, switch_ref,
    lhs_ref, rhs_ref, gate_ref,
    left_ref, side, mkeys,
):
    chips, lanes, channels = gate_ref.shape
    half = lanes // 2
    parity = lax.rem(lax.axis_index("dap"), 2)
    mkeys[...] = presence_down(small_ref[PRESENCE : PRESENCE + 1, :half], half, lanes)
    group = 8
    for block in range(chips // group):
        keeps = []
        for c in range(group):
            for r in range(2):
                keeps.append(mkeys[...] * mkeys[pl.ds(4 * (block * group + c) + 2 * parity + r, 1), :])
        normed = normed_ref[block * group : (block + 1) * group].reshape(group * lanes, channels)
        projected = dot_nn(normed, flank_ref[0, :, : 2 * channels])
        left = gated(projected, 0, channels, channels) * jnp.concatenate(keeps, axis=0)
        gate = jax.nn.sigmoid(dot_nn(normed, switch_ref[0]))
        for c in range(group):
            chip = block * group + c
            rows = slice(c * lanes, (c + 1) * lanes)
            gate_ref[chip] = gate[rows]
            left_ref[chip * channels : (chip + 1) * channels, :] = jnp.transpose(left[rows])
            side[chip * channels : (chip + 1) * channels, :] = own_ref[chip].astype(jnp.float32)
    low = lane_iota((chips, lanes)) < half
    per_step = channels

    @pl.loop(0, channels // per_step)
    def _(step):
        for o in range(per_step // 8):
            base = step * per_step + o * 8
            left = by_channel(left_ref, base, chips, channels)
            own = by_channel(side, base, chips, channels)
            for c in range(8):
                lhs = jnp.concatenate(
                    [jnp.where(low, left[c], 0.0), jnp.where(low, 0.0, left[c])], axis=0
                )
                to = pl.ds(pl.multiple_of((base + c) * 2 * chips, 2 * chips), 2 * chips)
                lhs_ref[to, :] = lhs.astype(jnp.bfloat16)
                rhs_ref[to, :] = both_turns(own[c]).astype(jnp.bfloat16)


def outgoing_body(
    pair_one_ref, lhs_ref, rhs_ref, gate_ref, oth_ref, small_ref, final_ref, flank_ref,
    two_ref, send_ref,
    side, prods, mkeys, pair_two, rows_out, cols,
):
    chips, channels, lanes = oth_ref.shape
    half = lanes // 2
    me = lax.axis_index("dap")
    parity = lax.rem(me, 2)
    my_chip = me // 2

    side[...] = oth_ref[...].astype(jnp.float32).reshape(side.shape)
    per_step = channels

    @pl.loop(0, channels // per_step)
    def _(step):
        for o in range(per_step // 8):
            base = step * per_step + o * 8
            oth = by_channel(side, base, chips, channels)
            for c in range(8):
                at = pl.ds(pl.multiple_of((base + c) * 2 * chips, 2 * chips), 2 * chips)
                rhs = jnp.concatenate(
                    [rhs_ref[at, :], both_turns(oth[c]).astype(jnp.bfloat16)], axis=0
                )
                out = dot_nt(lhs_ref[at, :], rhs)
                out = jnp.concatenate([out[:chips], out[chips:]], axis=1)
                to = pl.ds(base + c, chips, stride=channels)
                prods[to, :] = out.astype(jnp.bfloat16).astype(jnp.float32)

    mkeys[...] = presence_down(small_ref[PRESENCE : PRESENCE + 1, :half], half, channels)
    gain_mid = small_ref[MID_GAINS : MID_GAINS + 1, :channels]
    gain_mid = jnp.transpose(jnp.broadcast_to(gain_mid, (channels, channels)))
    final_t = jnp.transpose(final_ref[0].astype(jnp.float32)).astype(jnp.bfloat16)
    gain = small_ref[ENTRY_GAINS : ENTRY_GAINS + 1, channels : 2 * channels]
    flank_right = flank_ref[1, :, 2 * channels :]
    flank_left = flank_ref[1, :, : 2 * channels]
    octet = pl.multiple_of(8 * (my_chip // 2), 8)
    group = 16
    for block in range(chips // group):
        changed = []
        for c in range(group):
            x = prods[(block * group + c) * channels : (block * group + c + 1) * channels, :]
            centred = x - jnp.mean(x, axis=0, keepdims=True)
            spread = jnp.mean(centred * centred, axis=0, keepdims=True)
            changed.append((centred * lax.rsqrt(spread + EPSILON) * gain_mid).astype(jnp.bfloat16))
        changed = dot_nn(final_t, jnp.concatenate(changed, axis=1))
        for c in range(group):
            part = jnp.transpose(changed[:, c * lanes : (c + 1) * lanes])
            for k in range(8):
                r = k // 4
                p = 1 - parity if (k // 2) % 2 else parity
                rj = k % 2 if r == 0 else 1 - k % 2
                rows_out[block * group + c, pl.ds(r * half + 2 * p + rj, chips, stride=4), :] = part[
                    k * chips : (k + 1) * chips
                ]
        twos, keeps = [], []
        for c in range(group):
            chip = block * group + c
            two = pair_one_ref[chip] + rows_out[chip] * gate_ref[chip]
            twos.append(two)
            for r in range(2):
                keeps.append(mkeys[pl.ds(4 * chip + 2 * parity + r, 1), :])
        two = jnp.concatenate(twos, axis=0)
        full = normed_rows(two, gain)
        normed = full.astype(jnp.bfloat16)
        keep = jnp.concatenate([mkeys[...] * m for m in keeps], axis=0)
        going = (gated(dot_nn(normed, flank_right), 0, channels, channels) * keep).astype(jnp.bfloat16)
        cols[block] = full
        few = jnp.concatenate(
            [cols[block, pl.ds(k * half + octet, 8), :] for k in range(2 * group)], axis=0
        ).astype(jnp.bfloat16)
        mine = mkeys[pl.ds(octet, 8), :]
        keep = jnp.concatenate([mine * m for m in keeps], axis=0)
        few = (gated(dot_nn(few, flank_left), 0, channels, channels) * keep).astype(jnp.bfloat16)
        for c in range(group):
            chip = block * group + c
            pair_two[chip] = twos[c]
            send_ref[chip, :lanes, :] = going[c * lanes : (c + 1) * lanes]
            send_ref[chip, lanes:, :] = few[c * 16 : (c + 1) * 16]
    two_ref[...] = pair_two[my_chip]


def add_products(side_ref, tails, totals):
    chips = side_ref.shape[0]
    half, _ = totals[0].shape
    lanes = 2 * half
    me = lax.axis_index("dap")
    first = 4 * lax.rem(me // 2, 2) + 2 * lax.rem(me, 2)
    tails[...] = side_ref[:, lanes:, :].astype(jnp.float32).reshape(tails.shape)
    ahead = 4

    def step(block, totals):
        totals = list(totals)
        for c in range(ahead):
            chip = block * ahead + c
            for k in range(2):
                there = side_ref[chip, k * half : (k + 1) * half, :].astype(jnp.float32)
                for i in range(2):
                    one = tails[pl.ds(chip * 16 + 8 * k + first + i, 1), :]
                    totals[i] = totals[i] + one * there
        return tuple(totals)

    return lax.fori_loop(0, chips // ahead, step, tuple(totals))


def incoming_own_body(own_ref, two_ref, couple_ref, small_ref, switch_ref, sums_ref, kept_ref, gate_ref, tails):
    lanes, channels = two_ref.shape
    half = lanes // 2
    zero = jnp.zeros((half, channels), jnp.float32)
    sums_ref[...] = jnp.concatenate(add_products(own_ref, tails, (zero, zero)), axis=0)
    two = two_ref[...]
    gain = small_ref[ENTRY_GAINS : ENTRY_GAINS + 1, channels : 2 * channels]
    normed = normed_rows(two, gain).astype(jnp.bfloat16)
    gate_ref[...] = jax.nn.sigmoid(dot_nn(normed, switch_ref[1]))
    couple = couple_ref[...]
    kept_ref[...] = two + (couple - couple.astype(jnp.bfloat16).astype(jnp.float32))


def incoming_body(oth_ref, sums_ref, kept_ref, gate_ref, small_ref, final_ref, out_ref, tails):
    lanes, channels = out_ref.shape
    half = lanes // 2
    prod = jnp.concatenate(
        add_products(oth_ref, tails, (sums_ref[:half, :], sums_ref[half:, :])), axis=0
    )
    prod = prod.astype(jnp.bfloat16).astype(jnp.float32)
    gain_mid = small_ref[MID_GAINS : MID_GAINS + 1, channels : 2 * channels]
    changed = dot_nn(normed_rows(prod, gain_mid).astype(jnp.bfloat16), final_ref[1])
    out_ref[...] = kept_ref[...] + changed * gate_ref[...]


def gather_by_steps(block, chips):
    bits = chips.bit_length() - 1
    steps = 1 << (bits // 2)
    devices = 2 * chips

    def fetch(value, apart):
        return lax.ppermute(value, "dap", [(d, d ^ (2 * apart)) for d in range(devices)])

    near = block
    while near.shape[0] < chips // steps:
        near = jnp.concatenate([near, fetch(near, near.shape[0] * steps)], axis=0)
    return near, [fetch(near, k) for k in range(1, steps)]


def paired_shards(
    homolog_stack,
    couple_tensor,
    homolog_presence,
    amino_presence,
    horizontal_standard_factor,
    horizontal_asking_matrix,
    horizontal_lookup_triple,
    horizontal_final_matrix,
    couple_offset_factor,
    couple_offset_matrix,
    vertical_standard_factor,
    vertical_asking_matrix,
    vertical_lookup_triple,
    vertical_final_matrix,
    tensor_average_factor,
    tensor_average_mapping,
    tensor_average_final,
    trio_entry_factors,
    trio_flank_mappings,
    trio_final_switches,
    trio_multiplied_factors,
    trio_final_matrices,
):
    devices = lax.axis_size("dap")
    chips = devices // 2
    strands, aminos, features = homolog_stack.shape
    rows, _, channels = couple_tensor.shape
    lanes = rows * aminos
    heads = FOCUS_NUMBER
    hidden = TENSOR_HIDDEN
    f32, bf16 = jnp.float32, jnp.bfloat16
    shape = jax.ShapeDtypeStruct
    same_parity = [[2 * chip + p for chip in range(chips)] for p in range(2)]
    swap = [(d, d ^ 1) for d in range(devices)]

    def line(v):
        return v.reshape(1, -1)

    couple = couple_tensor.reshape(lanes, channels)
    x = homolog_stack.reshape(strands * aminos, features)
    block, near = vmem_call(
        bias_body,
        (shape((devices, 16, lanes), bf16), shape((1, lanes, channels), bf16)),
        scratch=[
            pltpu.VMEM((lanes, channels), f32),
            pltpu.VMEM((1, channels), f32),
            pltpu.VMEM((heads, channels), bf16),
            pltpu.VMEM((strands, aminos), jnp.int32),
            pltpu.SemaphoreType.DMA((4,)),
        ],
        count=4,
        away=range(4),
        grant=60 << 20,
    )(couple, line(couple_offset_factor), couple_offset_matrix.T, homolog_presence)
    blocks = lax.all_to_all(block, "dap", split_axis=0, concat_axis=0, tiled=True)
    small = jnp.concatenate(
        [
            line(horizontal_standard_factor),
            line(vertical_standard_factor),
            line(tensor_average_factor),
            line(trio_entry_factors),
            line(trio_multiplied_factors),
            jnp.pad(line(amino_presence.astype(f32)), ((0, 0), (0, features - aminos))),
            jnp.zeros((2, features), f32),
        ],
        axis=0,
    )
    final = jnp.transpose(
        tensor_average_final.reshape(hidden, hidden, channels), (2, 1, 0)
    ).reshape(channels, hidden * hidden)
    q, k, v, g = vmem_call(
        project_body,
        (
            shape((features // lanes, lanes, lanes), f32),
            shape((lanes, features), bf16),
            shape((lanes, features), bf16),
            shape((features // lanes, lanes, lanes), f32),
        ),
        count=4,
    )(x, small, horizontal_asking_matrix, horizontal_lookup_triple)
    near, fars = gather_by_steps(near, chips)
    couples = [near, *fars]
    sent = vmem_call(
        row_body,
        shape((devices, 8, lanes), bf16),
        scratch=[
            pltpu.VMEM((devices * 16, lanes), f32),
            pltpu.VMEM((devices * 8, lanes), f32),
            pltpu.VMEM((features // lanes, lanes, lanes), f32),
        ],
        count=7,
    )(blocks, x, q, k, v, g, horizontal_final_matrix)
    arrived = lax.all_to_all(sent, "dap", split_axis=0, concat_axis=0, tiled=True)
    msa, opm = vmem_call(
        column_body,
        (shape((devices * strands, rows * features), f32), shape((chips, 2 * hidden, lanes), bf16)),
        scratch=[
            pltpu.VMEM((devices * 8, lanes), f32),
            pltpu.VMEM((devices * 16, lanes), f32),
            pltpu.VMEM((lanes, features), f32),
            pltpu.VMEM((4, devices * strands, lanes), f32),
        ],
        count=7,
        later=1,
    )(
        arrived,
        blocks,
        small,
        vertical_asking_matrix,
        vertical_lookup_triple,
        vertical_final_matrix,
        tensor_average_mapping.T,
        final,
    )
    opm_own = lax.all_to_all(
        opm, "dap", split_axis=0, concat_axis=0, tiled=True, axis_index_groups=same_parity
    )
    opm_oth = lax.ppermute(opm_own, "dap", swap)
    msa = msa.reshape(devices * strands, rows, features)
    stack = (chips, lanes, channels)
    pair_one, normed, right_own = vmem_call(
        functools.partial(opm_body, len(couples)),
        (shape(stack, f32), shape(stack, bf16), shape(stack, bf16)),
        scratch=[
            pltpu.VMEM((hidden * lanes, lanes), f32),
            pltpu.VMEM((2, chips * hidden, lanes), f32),
            pltpu.VMEM((chips, hidden, hidden * lanes), bf16),
            pltpu.VMEM((aminos, lanes), f32),
            pltpu.VMEM((aminos, channels), f32),
            pltpu.VMEM((devices * 16, lanes), f32),
        ],
        count=len(couples) + 6,
        later=1,
    )(
        opm_own,
        opm_oth,
        *couples,
        blocks,
        final,
        small,
        trio_flank_mappings,
        msa,
    )
    right_oth = lax.ppermute(right_own, "dap", swap)
    by_channels = shape((channels * 2 * chips, lanes), bf16)
    lhs, rhs, gate = vmem_call(
        left_body,
        (by_channels, by_channels, shape(stack, f32)),
        scratch=[
            pltpu.VMEM((chips * channels, lanes), f32),
            pltpu.VMEM((chips * channels, lanes), f32),
            pltpu.VMEM((aminos, channels), f32),
        ],
        count=5,
    )(normed, right_own, small, trio_flank_mappings, trio_final_switches)
    two, going = vmem_call(
        outgoing_body,
        (shape((lanes, channels), f32), shape((chips, lanes + 16, channels), bf16)),
        scratch=[
            pltpu.VMEM((chips * channels, lanes), f32),
            pltpu.VMEM((channels * chips, lanes), f32),
            pltpu.VMEM((aminos, channels), f32),
            pltpu.VMEM(stack, f32),
            pltpu.VMEM(stack, f32),
            pltpu.VMEM((chips // 16, 16 * lanes, channels), f32),
        ],
        count=8,
    )(
        pair_one,
        lhs,
        rhs,
        gate,
        right_oth,
        small,
        trio_final_matrices,
        trio_flank_mappings,
    )
    coming = lax.ppermute(going, "dap", swap)
    own_rows = shape((lanes, channels), f32)
    tails = [pltpu.VMEM((chips * 16, channels), f32)]
    sums, kept, gate = vmem_call(
        incoming_own_body, (own_rows,) * 3, scratch=tails, count=5
    )(going, two, couple, small, trio_final_switches)
    pair_out = vmem_call(incoming_body, own_rows, scratch=tails, count=6)(
        coming, sums, kept, gate, small, trio_final_matrices
    )
    return msa, pair_out.reshape(rows, aminos, channels)


def fits_pairs(homolog_stack, couple_tensor, devices):
    strands, aminos, features = homolog_stack.shape
    rows, _, channels = couple_tensor.shape
    lanes = 128
    return (
        strands == rows == 2
        and devices % 8 == 0
        and devices & (devices - 1) == 0
        and rows * aminos == lanes == channels
        and aminos == 2 * devices
        and features == 2 * lanes
    )


def either(*arrays):
    if fits_pairs(arrays[0], arrays[1], lax.axis_size("dap")):
        return paired_shards(*arrays)
    return shards(*arrays)


def solution(mesh):
    placed = (
        P("dap", None, None),
        P("dap", None, None),
        P("dap", None),
        P(),
        P(),
        P(),
        P(),
        P(),
        P(),
        P(),
        P(),
        P(),
        P(),
        P(),
        P(),
        P(),
        P(),
        P(),
        P(),
        P(),
        P(),
        P(),
    )
    return jax.shard_map(
        either,
        mesh=mesh,
        in_specs=placed,
        out_specs=(P(None, "dap", None), P("dap", None, None)),
        check_vma=False,
    )
```
